32 devices in a mesh: grp: 4 (over z), blk: 4 (over x, core), sub: 2 (over y).
Axes of the slice: x: 2, y: 2, z: 4, core: 2. Of those that a mesh axis runs over, the one named last changes fastest.
Arguments:
- mass_per_volume: float32 [16, 64, 512], P('blk', 'sub', 'grp'), may hold values from 0.8 to 1.2
- flow_speed_vector: float32 [3, 16, 64, 512], P(None, 'blk', 'sub', 'grp'), may hold values from -1 to 1
- normal_stress: float32 [16, 64, 512], P('blk', 'sub', 'grp'), may hold values from 0.8 to 1.2
- facing_strip_index: int32 [4, 4, 64], P('grp', 'blk', 'sub'), may hold values from 0 to 63, as said below
- solid_kelvin: float32 [32, 16, 512], P('blk', 'sub', 'grp'), may hold values from 0.5 to 1.5
- face_coupling: float32 [6, 32, 16, 512], P(None, 'blk', 'sub', 'grp'), may hold values from 0 to 2, as said below
- substance_index: int32 [32, 16, 512], P('blk', 'sub', 'grp'), may hold values from 0 to 7
- substance_storage: float32 [8], replicated, may hold values from 0.5 to 4
Outputs:
- fluid_next: float32 [5, 16, 64, 512], P(None, 'blk', 'sub', 'grp')
- metal_next: float32 [32, 16, 512], P('blk', 'sub', 'grp')
The draws below stay inside these ranges and needn't reach their ends.
Inputs may be any that keep to these rules, and one draw needn't show every extreme that they name: `facing_strip_index`: A value v names metal device v // 8 of the blade (devices numbered over blk then sub) and strip v % 8 on it. The strips of each fluid device name exactly 4 distinct metal devices, each exactly 8 times; strips within a metal device are named with any multiplicity. `face_coupling`: channels 0 to 2 are the conductances across the lower x, y and z face of each cell, channels 3 to 5 across the upper ones; a cell's upper conductance equals the lower one of the next cell along that dimension. Conductances across the grid's ends in x and y and across multiples of 128 along z are zero, all others lie in 0.2 to 2.
All inputs are finite; a program needn't handle non-finite values.
Results may differ from the reference program's by a relative error of at most 0.0001.
Values sent between devices are 32-bit elements; how exact they have to be, the bound alone decides.
No kernel may reach another device: no remote copies, remote signals or barrier semaphores. Data moves between devices by JAX's collectives and lax.ppermute only.
A program may use at most 64 MiB of HBM per device.

```python
import math
import jax
import jax.numpy as jnp
from jax import lax

FX = 4
FY = 32
UNIT_SPAN_NODES = 128
UNIT_SOLID_ALONG = 8
UNIT_SOLID_ACROSS = 8
MATS = 8
ITERS = 4
NX = 16
NY = 64
SPAN_NODE_COUNT = 512
SOLID_ALONG_NUM = 32
SOLID_ACROSS_NUM = 16
UNITS_PER_VANE = 8
CAP = 8


def draw_facing_strip_index(key, part):
    vane_sequence = SPAN_NODE_COUNT // UNIT_SPAN_NODES
    partition_sequence = NX // FX
    devices = vane_sequence * partition_sequence * (NY // FY)

    def one_device(device_key):
        key_first, key_second, key_third = jax.random.split(device_key, 3)
        chosen = jax.random.permutation(key_first, UNITS_PER_VANE)[:UNITS_PER_VANE // 2]
        targets = jnp.repeat(chosen, CAP, total_repeat_length=FY)
        targets = jax.random.permutation(key_second, targets)
        slot_ids = jax.random.randint(key_third, (FY,), 0, UNIT_SOLID_ACROSS)
        return (targets * UNIT_SOLID_ACROSS + slot_ids).astype(jnp.int32)
    rows = jax.vmap(one_device)(jax.random.split(key, devices))
    return rows.reshape(vane_sequence, partition_sequence, NY)


def draw_face_coupling(key, part):
    face_keys = jax.random.split(jax.random.fold_in(key, 17), 3)

    def faces(face_key):
        values = jnp.exp(jax.random.uniform(face_key, (SOLID_ALONG_NUM, SOLID_ACROSS_NUM, SPAN_NODE_COUNT), jnp.float32, jnp.log(0.2), jnp.log(2.0)))
        return values
    lower_x = faces(face_keys[0]).at[0].set(0.0)
    lower_y = faces(face_keys[1]).at[:, 0].set(0.0)
    lower_z = faces(face_keys[2])
    lower_z = jnp.where((jnp.arange(SPAN_NODE_COUNT) % UNIT_SPAN_NODES == 0)[None, None, :], 0.0, lower_z)
    upper_x = jnp.concatenate([lower_x[1:], jnp.zeros_like(lower_x[:1])], axis=0)
    upper_y = jnp.concatenate([lower_y[:, 1:], jnp.zeros_like(lower_y[:, :1])], axis=1)
    upper_z = jnp.concatenate([lower_z[:, :, 1:], jnp.zeros_like(lower_z[:, :, :1])], axis=2)
    return jnp.stack([lower_x, lower_y, lower_z, upper_x, upper_y, upper_z]).astype(jnp.float32)


def place_ends(values, own_key, low, high):
    extent = values.shape
    spot = [jax.random.randint(jax.random.fold_in(own_key, axis), (), 0, extent[axis]) for axis in range(len(extent))]
    values = values.at[tuple(spot)].set(low)
    longest = extent.index(max(extent))
    spot[longest] = (spot[longest] + 1) % extent[longest]
    return values.at[tuple(spot)].set(high)


def block_levels(stream_key, shape, pieces, least, top_value):
    def one(axis_at, shards_of):
        heights = jax.random.uniform(jax.random.fold_in(jax.random.fold_in(stream_key, 6), axis_at), (shards_of,), jnp.float32, least / len(pieces), top_value / len(pieces))
        return jnp.repeat(jnp.exp(heights), shape[axis_at] // shards_of).reshape((-1,) + (1,) * (len(shape) - axis_at - 1))

    gain = one(*pieces[0])
    for cut in pieces[1:]:
        gain = gain * one(*cut)
    return gain


def centred(stream_key, extent, deviation, most, shards=(), kind=jnp.bfloat16):
    values = jax.random.normal(stream_key, extent, jnp.float32) * deviation
    if len(shards) > 0:
        values = block_levels(stream_key, extent, shards, -0.22, 0.18) * values
    return jnp.clip(values, min=-most, max=most).astype(kind)


def setup_inputs(seed: int = 0) -> dict:
    keys = jax.random.split(jax.random.key(seed), 9)
    return {
        "mass_per_volume": jnp.clip(0.8 + 0.40000004 * jax.random.uniform(keys[0], (NX, NY, SPAN_NODE_COUNT), jnp.float32) ** block_levels(keys[0], (NX, NY, SPAN_NODE_COUNT), ((0, 4), (1, 2), (2, 4)), -0.2, 0.2), 0.8, 1.2),
        "flow_speed_vector": centred(keys[1], (3, NX, NY, SPAN_NODE_COUNT), 0.3, 1.0, ((1, 4), (2, 2), (3, 4)), jnp.float32),
        "normal_stress": jnp.clip(0.8 + 0.40000004 * jax.random.uniform(keys[2], (NX, NY, SPAN_NODE_COUNT), jnp.float32) ** block_levels(keys[2], (NX, NY, SPAN_NODE_COUNT), ((0, 4), (1, 2), (2, 4)), -0.2, 0.2), 0.8, 1.2),
        "facing_strip_index": draw_facing_strip_index(jax.random.fold_in(keys[8], 71), 0),
        "solid_kelvin": jnp.clip(0.5 + 1.0 * jax.random.uniform(keys[4], (SOLID_ALONG_NUM, SOLID_ACROSS_NUM, SPAN_NODE_COUNT), jnp.float32) ** block_levels(keys[4], (SOLID_ALONG_NUM, SOLID_ACROSS_NUM, SPAN_NODE_COUNT), ((0, 4), (1, 2), (2, 4)), -0.2, 0.2), 0.5, 1.5),
        "face_coupling": draw_face_coupling(jax.random.fold_in(keys[8], 71), 0),
        "substance_index": place_ends(jax.random.randint(keys[6], (SOLID_ALONG_NUM, SOLID_ACROSS_NUM, SPAN_NODE_COUNT), 0, MATS), jax.random.fold_in(keys[6], 1), 0, MATS - 1).astype(jnp.int32),
        "substance_storage": jnp.clip(jnp.exp(jax.random.uniform(keys[7], (MATS,), jnp.float32, math.log(0.5), math.log(4.0))), 0.5, 4.0),
    }


gamma_gas = 1.4
time_step = 0.1
viscosity = 0.05
film_coeff = 1.0
third_part = 1.0 / 3.0
two_thirds = 2.0 / 3.0

def cut_faces(values, axis_id, start_at, stop_at):
    first_space = values.ndim - 3
    indexer = [slice(None)] * values.ndim
    for member in range(3):
        if member == axis_id:
            indexer[first_space + member] = slice(start_at, stop_at)
        else:
            indexer[first_space + member] = slice(1, -1)
    return values[tuple(indexer)]

def cut_along(values, axis_id, start_at, stop_at):
    indexer = [slice(None)] * values.ndim
    indexer[values.ndim - 3 + axis_id] = slice(start_at, stop_at)
    return values[tuple(indexer)]

def crop_cells(values, margin):
    return values[..., margin:-margin, margin:-margin, margin:-margin]

def advance_rate(padded, source):
    mass_per_volume = padded[0]
    flow_speed_vector = padded[1:4] / mass_per_volume
    kinetic = 0.5 * lax.optimization_barrier(jnp.sum(padded[1:4] * flow_speed_vector, axis=0))
    normal_stress = (gamma_gas - 1.0) * (padded[4] - kinetic)
    sound_speed = jnp.sqrt(gamma_gas * normal_stress / mass_per_volume)
    interior = crop_cells(padded, 1)
    rate_sum = jnp.zeros_like(interior)
    smooth_sum = jnp.zeros_like(interior)
    for axis_id in range(3):
        along_vel = flow_speed_vector[axis_id]
        flux_dir = padded * along_vel
        flux_dir = flux_dir.at[1 + axis_id].add(normal_stress)
        flux_dir = flux_dir.at[4].add(normal_stress * along_vel)
        wave_speed = jnp.abs(along_vel) + sound_speed
        left_flux = cut_faces(flux_dir, axis_id, 0, -1)
        right_flux = cut_faces(flux_dir, axis_id, 1, None)
        left_state = cut_faces(padded, axis_id, 0, -1)
        right_state = cut_faces(padded, axis_id, 1, None)
        face_speed = jnp.maximum(cut_faces(wave_speed, axis_id, 0, -1), cut_faces(wave_speed, axis_id, 1, None))
        face_flux = 0.5 * (left_flux + right_flux) - 0.5 * face_speed * (right_state - left_state)
        rate_sum = rate_sum - (cut_along(face_flux, axis_id, 1, None) - cut_along(face_flux, axis_id, 0, -1))
        line_cut = cut_faces(padded, axis_id, None, None)
        smooth_sum = smooth_sum + (cut_along(line_cut, axis_id, 2, None) - 2.0 * cut_along(line_cut, axis_id, 1, -1) + cut_along(line_cut, axis_id, 0, -2))
    weights = jnp.array([0.0, 1.0, 1.0, 1.0, 1.0], jnp.float32).reshape(5, 1, 1, 1)
    rate_sum = rate_sum + viscosity * weights * smooth_sum
    return rate_sum.at[4].add(-source)

def fluid_state(mass_per_volume, flow_speed_vector, normal_stress):
    momentum = mass_per_volume[None] * flow_speed_vector
    energy = normal_stress / (gamma_gas - 1.0) + 0.5 * lax.optimization_barrier(jnp.sum(momentum * flow_speed_vector, axis=0))
    return jnp.concatenate([mass_per_volume[None], momentum, energy[None]], axis=0)

def metal_apply(padded, face_coupling, storage_coefficient):
    center = padded[1:-1, 1:-1, 1:-1]
    result = storage_coefficient * center
    result = result + face_coupling[0] * (center - padded[:-2, 1:-1, 1:-1]) + face_coupling[3] * (center - padded[2:, 1:-1, 1:-1])
    result = result + face_coupling[1] * (center - padded[1:-1, :-2, 1:-1]) + face_coupling[4] * (center - padded[1:-1, 2:, 1:-1])
    result = result + face_coupling[2] * (center - padded[1:-1, 1:-1, :-2]) + face_coupling[5] * (center - padded[1:-1, 1:-1, 2:])
    return result

def rate_global(conserved, source):
    padded = jnp.pad(conserved, ((0, 0), (1, 1), (1, 1), (1, 1)), mode='wrap')

    def slab_rate(slab_no):
        slab_cut = lax.dynamic_slice_in_dim(padded, slab_no * UNIT_SPAN_NODES, UNIT_SPAN_NODES + 2, axis=3)
        slab_source = lax.dynamic_slice_in_dim(source, slab_no * UNIT_SPAN_NODES, UNIT_SPAN_NODES, axis=2)
        return advance_rate(slab_cut, slab_source)
    rates = lax.map(slab_rate, jnp.arange(SPAN_NODE_COUNT // UNIT_SPAN_NODES, dtype=jnp.int32))
    return jnp.moveaxis(rates, 0, 3).reshape(5, NX, NY, SPAN_NODE_COUNT)

def invert_solid_conduction(solid_kelvin, face_coupling, storage_coefficient, kelvin_distribution):

    def apply_operator(field_in):
        return metal_apply(jnp.pad(field_in, 1), face_coupling, storage_coefficient)
    forcing_vector = storage_coefficient * solid_kelvin + kelvin_distribution
    converged_kelvin = solid_kelvin
    equation_misfit = forcing_vector - apply_operator(converged_kelvin)
    search_vector = equation_misfit
    norm_now = jnp.sum(equation_misfit * equation_misfit)
    for step_no in range(ITERS):
        image_dir = apply_operator(search_vector)
        search_factor = norm_now / jnp.sum(search_vector * image_dir)
        converged_kelvin = converged_kelvin + search_factor * search_vector
        equation_misfit = equation_misfit - search_factor * image_dir
        norm_next = jnp.sum(equation_misfit * equation_misfit)
        search_vector = equation_misfit + norm_next / norm_now * search_vector
        norm_now = norm_next
    return converged_kelvin

def pick_rows(table_rows, row_ids):
    return jnp.take(table_rows, row_ids, axis=0)

def sum_rows(flux_rows, row_ids):
    return jax.ops.segment_sum(flux_rows, row_ids, num_segments=UNITS_PER_VANE * UNIT_SOLID_ACROSS)

def bundled_iterative_method(pack):
    return invert_solid_conduction(pack[0], pack[1], pack[2], pack[3])

def reference(mass_per_volume, flow_speed_vector, normal_stress, facing_strip_index, solid_kelvin, face_coupling, substance_index, substance_storage):
    vane_sequence = SPAN_NODE_COUNT // UNIT_SPAN_NODES
    partition_sequence = NX // FX
    conserved = fluid_state(mass_per_volume, flow_speed_vector, normal_stress)
    face_temp = normal_stress.reshape(partition_sequence, FX, NY, SPAN_NODE_COUNT)[:, 0] / mass_per_volume.reshape(partition_sequence, FX, NY, SPAN_NODE_COUNT)[:, 0]
    face_temp = jnp.moveaxis(face_temp.reshape(partition_sequence * NY, vane_sequence, UNIT_SPAN_NODES), 1, 0)
    collected_surfaces = solid_kelvin.reshape(partition_sequence, UNIT_SOLID_ALONG, SOLID_ACROSS_NUM, SPAN_NODE_COUNT)[:, 0].reshape(UNITS_PER_VANE * UNIT_SOLID_ACROSS, vane_sequence, UNIT_SPAN_NODES)
    collected_surfaces = jnp.moveaxis(collected_surfaces, 1, 0)
    route_rows = facing_strip_index.reshape(vane_sequence, partition_sequence * NY)
    wall_seen = jax.vmap(pick_rows)(collected_surfaces, route_rows)
    heat_flux = film_coeff * (face_temp - wall_seen)
    arriving_energy = jax.vmap(sum_rows)(heat_flux, route_rows)
    sink = jnp.moveaxis(heat_flux, 0, 1).reshape(partition_sequence, NY, SPAN_NODE_COUNT)
    sink = jnp.zeros((partition_sequence, FX, NY, SPAN_NODE_COUNT), jnp.float32).at[:, 0].set(sink).reshape(NX, NY, SPAN_NODE_COUNT)
    present_iterate = conserved
    for section_no in range(3):
        fresh = present_iterate + time_step * rate_global(present_iterate, sink)
        if section_no == 0:
            present_iterate = fresh
        elif section_no == 1:
            present_iterate = 0.75 * conserved + 0.25 * fresh
        else:
            present_iterate = third_part * conserved + two_thirds * fresh
    storage_coefficient = substance_storage[substance_index]

    def vane_portion(values):
        return jnp.moveaxis(values.reshape(values.shape[:-1] + (vane_sequence, UNIT_SPAN_NODES)), -2, 0)
    kelvin_distribution = jnp.zeros((vane_sequence, partition_sequence, UNIT_SOLID_ALONG, SOLID_ACROSS_NUM, UNIT_SPAN_NODES), jnp.float32)
    kelvin_distribution = kelvin_distribution.at[:, :, 0].set(arriving_energy.reshape(vane_sequence, partition_sequence, SOLID_ACROSS_NUM, UNIT_SPAN_NODES)).reshape(vane_sequence, SOLID_ALONG_NUM, SOLID_ACROSS_NUM, UNIT_SPAN_NODES)
    solid_outcome = lax.map(bundled_iterative_method, (vane_portion(solid_kelvin), vane_portion(face_coupling), vane_portion(storage_coefficient), kelvin_distribution))
    metal_next = jnp.moveaxis(solid_outcome, 0, 2).reshape(SOLID_ALONG_NUM, SOLID_ACROSS_NUM, SPAN_NODE_COUNT)
    return (present_iterate, metal_next)
```

```python
import functools

import jax
import jax.numpy as jnp
from jax import lax
from jax.experimental import pallas as pl
from jax.experimental.pallas import tpu as pltpu
from jax.sharding import PartitionSpec as P

ITERS = 4
HALO = 3
TILE = 8
FIELDS = 5

gamma_gas = 1.4
time_step = 0.1
viscosity = 0.05
film_coeff = 1.0
third_part = 1.0 / 3.0
two_thirds = 2.0 / 3.0

HIGHEST = lax.Precision.HIGHEST
VMEM_BYTES = 56 * 1024 * 1024


def call(body, out, inputs, smem=(), cost=100_000, scratch=(), name=None):
    in_specs = [
        pl.BlockSpec(memory_space=pltpu.SMEM if i in smem else pltpu.VMEM)
        for i in range(len(inputs))
    ]
    return pl.pallas_call(
        body,
        out_shape=out,
        in_specs=in_specs,
        out_specs=jax.tree.map(lambda _: pl.BlockSpec(memory_space=pltpu.VMEM), out),
        scratch_shapes=list(scratch),
        name=name,
        cost_estimate=pl.CostEstimate(flops=cost, bytes_accessed=cost, transcendentals=0),
        compiler_params=pltpu.CompilerParams(vmem_limit_bytes=VMEM_BYTES),
    )(*inputs)


def f32(*shape):
    return jax.ShapeDtypeStruct(shape, jnp.float32)


def up_to_tile(count):
    return -(-count // TILE) * TILE


def iota(shape, dim):
    return lax.broadcasted_iota(jnp.int32, shape, dim)


def dot(a, b, a_dim, b_dim):
    return lax.dot_general(
        a, b, (((a_dim,), (b_dim,)), ((), ())), precision=HIGHEST,
        preferred_element_type=jnp.float32,
    )


def below(ref, r, count, *at):
    start = pl.multiple_of(r - TILE, TILE)
    return ref[(*at, pl.ds(start, count + TILE))][TILE - 1:TILE - 1 + count]


def above(ref, r, count, *at):
    start = pl.multiple_of(r, TILE)
    return ref[(*at, pl.ds(start, count + TILE))][1:1 + count]


def parity():
    return lax.rem(lax.axis_index("blk"), 2)


def pack_kernel(
    rho_ref, vel_ref, pre_ref, route_ref, kelvin_ref, couple_ref, kind_ref, store_ref,
    state_ref, yedge_ref, aface_ref, bface_ref, metal_ref, wall_ref,
):
    planes, rows, lanes = rho_ref.shape
    along, across, _ = kelvin_ref.shape
    cells = along * across
    wall_ref[0:across] = kelvin_ref[0]
    wall_ref[across:across + TILE] = jnp.zeros((TILE, lanes), jnp.float32)
    wall_ref[across:across + 1, 0:rows] = route_ref[...].astype(jnp.float32)
    for x in range(planes):
        rho = rho_ref[x]
        vel = [vel_ref[d, x] for d in range(3)]
        mom = [rho * v for v in vel]
        kinetic = mom[0] * vel[0] + mom[1] * vel[1] + mom[2] * vel[2]
        energy = pre_ref[x] / (gamma_gas - 1.0) + 0.5 * kinetic
        for f, value in enumerate([rho, *mom, energy]):
            state_ref[f, x] = value
    used = FIELDS * planes * HALO
    for f in range(FIELDS):
        for x in range(planes):
            at = (f * planes + x) * HALO
            yedge_ref[0, at:at + HALO] = state_ref[f, x, 0:HALO]
            yedge_ref[1, at:at + HALO] = state_ref[f, x, rows - HALO:rows]
    if yedge_ref.shape[1] > used:
        for side in range(2):
            yedge_ref[side, used:] = jnp.zeros(
                (yedge_ref.shape[1] - used, lanes), jnp.float32
            )
    for odd in range(2):

        @pl.when(parity() == odd)
        def _():
            for f in range(FIELDS):
                for j in range(HALO):
                    aface_ref[f, j] = state_ref[f, j + (planes - HALO) * (1 - odd)]
                    bface_ref[f, j] = state_ref[f, j + (planes - HALO) * odd]

    for x in range(along):
        at = x * across
        metal_ref[at:at + across] = kelvin_ref[x]
        kind = kind_ref[x]
        capacity = jnp.zeros((across, lanes), jnp.float32)
        for m in range(store_ref.shape[0]):
            capacity = jnp.where(kind == m, store_ref[m], capacity)
        metal_ref[cells + at:cells + at + across] = capacity
        for d in range(3):
            base = (2 + d) * cells + at
            metal_ref[base:base + across] = couple_ref[d, x]
    metal_ref[5 * cells:5 * cells + rows] = pre_ref[0] / rho_ref[0]
    metal_ref[5 * cells + rows:5 * cells + rows + TILE] = wall_ref[across:across + TILE]


def edge_kernel(planes, lo_at, hi_at, starts, *refs):
    ylo_ref, yhi_ref = refs[0], refs[1]
    parts, (aedge_ref, bedge_ref) = refs[2:-2], refs[-2:]
    used = FIELDS * HALO * HALO
    span = up_to_tile(used)
    for odd in range(2):

        @pl.when(parity() == odd)
        def _():
            for out, first in (
                (aedge_ref, (planes - HALO) * (1 - odd)),
                (bedge_ref, (planes - HALO) * odd),
            ):
                for f in range(FIELDS):
                    for side, (ref, base) in enumerate(((ylo_ref, lo_at), (yhi_ref, hi_at))):
                        at = side * span + f * HALO * HALO
                        src = base + (f * planes + first) * HALO
                        out[at:at + HALO * HALO] = ref[src:src + HALO * HALO]

    for out in (aedge_ref, bedge_ref):
        for side in range(2):
            if span > used:
                out[side * span + used:(side + 1) * span] = jnp.zeros(
                    (span - used, ylo_ref.shape[1]), jnp.float32
                )
    at = 2 * span
    for ref, (start, count) in zip(parts, starts):
        bedge_ref[at:at + count] = ref[start:start + count]
        at += count


def assemble_kernel(dims, lo_at, hi_at, wall_at, *refs):
    axes, across = dims
    count_blk, count_sub = axes
    state_ref, aface_ref, bface_ref, ylo_ref, yhi_ref, aedge_ref, bedge_ref = refs[:7]
    wall_refs = refs[7:-5]
    block_ref, zlo_ref, zhi_ref, table, seen = refs[-5:]
    _, planes, rows, lanes = state_ref.shape
    stride = rows + TILE
    span = up_to_tile(FIELDS * HALO * HALO)
    each = across + TILE
    blk, sub = lax.axis_index("blk"), lax.axis_index("sub")

    def place(f, x, own, lo, hi):
        base = (x + HALO) * stride + TILE
        block_ref[f, base:base + rows] = own
        block_ref[f, base - HALO:base] = lo
        block_ref[f, base + rows:base + rows + HALO] = hi

    for f in range(FIELDS):
        for x in range(planes):
            at = (f * planes + x) * HALO
            place(
                f, x, state_ref[f, x],
                ylo_ref[lo_at + at:lo_at + at + HALO], yhi_ref[hi_at + at:hi_at + at + HALO],
            )
    for odd in range(2):

        @pl.when(parity() == odd)
        def _():
            for face_ref, edge_ref, above in (
                (aface_ref, aedge_ref, odd == 0), (bface_ref, bedge_ref, odd == 1),
            ):
                for f in range(FIELDS):
                    for j in range(HALO):
                        at = (f * HALO + j) * HALO
                        place(
                            f, planes + j if above else j - HALO, face_ref[f, j],
                            edge_ref[at:at + HALO], edge_ref[span + at:span + at + HALO],
                        )

    if wall_at is None:
        table = wall_refs[0]
    else:
        for ref, (start, flip_blk, flip_sub) in zip(wall_refs, wall_at):
            device = jnp.bitwise_xor(blk, flip_blk) * count_sub + jnp.bitwise_xor(sub, flip_sub)
            table[pl.ds(pl.multiple_of(device * each, TILE), each)] = ref[start:start + each]
    devices = count_blk * count_sub
    walls = jnp.concatenate(
        [table[d * each:d * each + across] for d in range(devices)], axis=0
    )

    def facing(blk_at, sub_at):
        device = lax.rem(blk_at, count_blk) * count_sub + lax.rem(sub_at, count_sub)
        at = pl.multiple_of(device * each + across, TILE)
        routes = table[pl.ds(at, TILE)][0:1, 0:rows].astype(jnp.int32)
        chosen = (iota((devices * across, rows), 0) == routes).astype(jnp.float32)
        return dot(chosen, walls, 0, 0)

    block_ref[FIELDS] = jnp.zeros(block_ref.shape[1:], jnp.float32)
    for x, blk_at in ((0, blk), (planes, blk + 1)):
        own = facing(blk_at, sub)
        below = facing(blk_at, sub + count_sub - 1)
        above = below if count_sub == 2 else facing(blk_at, sub + 1)
        seen[0:TILE] = jnp.zeros((TILE, lanes), jnp.float32)
        seen[TILE:TILE + rows] = own
        seen[TILE - HALO:TILE] = below[rows - HALO:rows]
        seen[TILE + rows:] = jnp.zeros((TILE, lanes), jnp.float32)
        seen[TILE + rows:TILE + rows + HALO] = above[0:HALO]
        base = (x + HALO) * stride
        rho, mx, my, mz, energy = [
            block_ref[f, base:base + stride + TILE] for f in range(FIELDS)
        ]
        pressure = (gamma_gas - 1.0) * (energy - 0.5 * (mx * mx + my * my + mz * mz) / rho)
        flux = film_coeff * (pressure / rho - seen[...])
        block_ref[FIELDS, base + TILE - HALO:base + TILE + rows + HALO] = flux[
            TILE - HALO:TILE + rows + HALO
        ]
    pick = iota((TILE, lanes), 0)
    cell = iota((TILE, lanes), 1)
    low = ((pick == cell) & (pick < HALO)).astype(jnp.float32)
    high = ((pick + lanes - HALO == cell) & (pick < HALO)).astype(jnp.float32)
    for f in range(FIELDS + 1):
        zlo_ref[f * HALO:(f + 1) * HALO] = dot(low, block_ref[f], 1, 1)[0:HALO]
        zhi_ref[f * HALO:(f + 1) * HALO] = dot(high, block_ref[f], 1, 1)[0:HALO]
    left = zlo_ref.shape[0] - (FIELDS + 1) * HALO
    if left:
        for ref in (zlo_ref, zhi_ref):
            ref[(FIELDS + 1) * HALO:] = jnp.zeros((left, ref.shape[1]), jnp.float32)


def fluid_kernel(planes, rows, block_ref, zlo_ref, zhi_ref, out_ref, base, now, prim, xface, yface, part, comb):
    total, lanes = block_ref.shape[1:]
    wide = 2 * lanes
    stride = rows + TILE
    pick = iota((TILE, lanes), 0)
    cell = iota((TILE, lanes), 1)
    spread = (
        ((pick == cell) & (pick < HALO))
        | ((pick - HALO + lanes - HALO == cell) & (pick >= HALO) & (pick < 2 * HALO))
    ).astype(jnp.float32)
    comb[2 * HALO:] = jnp.zeros((TILE - 2 * HALO, total), jnp.float32)
    for f in range(FIELDS + 1):
        comb[0:HALO] = zhi_ref[f * HALO:(f + 1) * HALO]
        comb[HALO:2 * HALO] = zlo_ref[f * HALO:(f + 1) * HALO]
        base[f, :, 0:lanes] = block_ref[f]
        base[f, :, lanes:wide] = dot(comb[...], spread, 0, 0)

    def flux(d, u, speed, pressure):
        f = [u[1 + d]] + [u[1 + i] * speed for i in range(3)] + [(u[4] + pressure) * speed]
        f[1 + d] = f[1 + d] + pressure
        return f

    def faces(d, lo_u, lo_p, hi_u, hi_p):
        lo_f = flux(d, lo_u, lo_p[d], lo_p[3])
        hi_f = flux(d, hi_u, hi_p[d], hi_p[3])
        fast = jnp.maximum(jnp.abs(lo_p[d]) + lo_p[4], jnp.abs(hi_p[d]) + hi_p[4])
        slow = fast + 2.0 * viscosity
        return [
            (lo_f[i] + hi_f[i]) - (fast if i == 0 else slow) * (hi_u[i] - lo_u[i])
            for i in range(5)
        ]

    def tiles(first, last, body, unroll=1):
        @pl.loop(first // TILE, last // TILE, unroll=unroll)
        def _(i):
            body(pl.multiple_of(i * TILE, TILE))

    for stage in range(3):
        src = base if stage == 0 else now
        margin = 2 - stage
        first = (HALO - margin) * stride
        last = (HALO + planes + margin - 1) * stride + 2 * TILE + rows
        if stage == 2:
            first, last = first + TILE, last - TILE

        def primitives(r, src=src):
            rho, mx, my, mz, energy = [src[f, pl.ds(r, TILE)] for f in range(5)]
            inverse = 1.0 / rho
            ux, uy, uz = mx * inverse, my * inverse, mz * inverse
            pressure = (gamma_gas - 1.0) * (energy - 0.5 * (mx * ux + my * uy + mz * uz))
            sound = jnp.sqrt(gamma_gas * pressure * inverse)
            for k, value in enumerate([ux, uy, uz, pressure, sound]):
                prim[k, pl.ds(r, TILE)] = value

        def load(r, src=src):
            return (
                [src[f, pl.ds(r, TILE)] for f in range(5)],
                [prim[k, pl.ds(r, TILE)] for k in range(5)],
            )

        def along_x(r):
            hi, lo = load(r), load(r - stride)
            for k, value in enumerate(faces(0, *lo, *hi)):
                xface[k, pl.ds(r, TILE)] = value

        def along_y(r, src=src):
            hi = load(r)
            lo = (
                [below(src, r, TILE, f) for f in range(5)],
                [below(prim, r, TILE, k) for k in range(5)],
            )
            for k, value in enumerate(faces(1, *lo, *hi)):
                yface[k, pl.ds(r, TILE)] = value

        def along_z(r):
            hi = load(r)
            lo = [[pltpu.roll(v, 1, axis=1) for v in vs] for vs in hi]
            for k, value in enumerate(faces(2, *lo, *hi)):
                part[k, pl.ds(r, TILE)] = pltpu.roll(value, wide - 1, axis=1) - value

        def finish(r, stage=stage, src=src):
            for k in range(5):
                here = pl.ds(r, TILE)
                rate = part[k, here]
                rate += xface[k, pl.ds(r + stride, TILE)] - xface[k, here]
                rate += above(yface, r, TILE, k) - yface[k, here]
                fresh = src[k, here] - (0.5 * time_step) * rate
                if k == 4:
                    fresh -= time_step * base[5, here]
                if stage == 1:
                    fresh = 0.75 * base[k, here] + 0.25 * fresh
                if stage == 2:
                    fresh = third_part * base[k, here] + two_thirds * fresh
                now[k, here] = fresh

        tiles(max(first - stride, 0), min(last + stride, total), primitives)
        tiles(first, last + stride, along_x)
        tiles(first, last + TILE, along_y)
        tiles(first, last, along_z)
        tiles(first, last, finish)
    for k in range(5):
        for x in range(planes):
            at = (x + HALO) * stride + TILE
            out_ref[k, x] = now[k, at:at + rows, 0:lanes]


def metal_kernel(dims, rows, order, held_ref, other_ref, out_ref, sol, res, dirn, image, diag, cx, cy, cz, czu, caps, heat):
    count_blk, count_sub, along, across = dims
    devices = count_blk * count_sub
    lanes = out_ref.shape[-1]
    cells = along * across
    wide = count_sub * across
    total = count_blk * along * wide
    pad = wide
    blk, sub = lax.axis_index("blk"), lax.axis_index("sub")
    pieces = [(held_ref, k) for k in range(held_ref.shape[0])]
    pieces += [(other_ref, k) for k in range(other_ref.shape[0])]

    zero = jnp.zeros((pad, lanes), jnp.float32)
    for ref in (dirn, cx, cy):
        ref[0:pad] = zero
        ref[pad + total:pad + total + pad] = zero

    walls = []
    for (ref, k), (flip_blk, flip_sub) in zip(pieces, order):
        b, s = jnp.bitwise_xor(blk, flip_blk), jnp.bitwise_xor(sub, flip_sub)
        for x in range(along):
            at = (b * along + x) * wide + s * across
            src = x * across
            for field, (dest, shift) in enumerate(
                ((dirn, pad), (caps, 0), (cx, pad), (cy, pad), (cz, 0))
            ):
                start = field * cells + src
                dest[pl.ds(pl.multiple_of(at + shift, TILE), across)] = ref[
                    k, start:start + across
                ]
    walls = jnp.concatenate(
        [dirn[pad + b * along * wide:pad + b * along * wide + wide] for b in range(count_blk)],
        axis=0,
    )
    heat[...] = jnp.zeros_like(heat)
    for ref, k in pieces:
        at = 5 * cells
        routes = ref[k, at + rows:at + rows + TILE][0:1, 0:rows].astype(jnp.int32)
        chosen = (iota((devices * across, rows), 0) == routes).astype(jnp.float32)
        flux = film_coeff * (ref[k, at:at + rows] - dot(chosen, walls, 0, 0))
        heat[...] += dot(chosen, flux, 1, 0)

    chunk = 32 if total % 32 == 0 else TILE
    none = jnp.zeros((chunk, lanes), jnp.float32)

    def sweep(body, init):
        return lax.fori_loop(
            0, total // chunk, lambda i, c: body(pl.multiple_of(i * chunk, TILE), c), init
        )

    def prepare(r, carry):
        here = pl.ds(r, chunk)
        own = pl.ds(r + pad, chunk)
        upper = pltpu.roll(cz[here], lanes - 1, axis=1)
        czu[here] = upper
        ups = cx[pl.ds(r + pad + wide, chunk)], above(cy, r + pad, chunk)
        links = (cx[own] + ups[0]) + (cy[own] + ups[1]) + (cz[here] + upper)
        diag[here] = caps[here] + links
        v = dirn[own]
        res[here] = -(
            cx[own] * (v - dirn[pl.ds(r + pad - wide, chunk)])
            + ups[0] * (v - dirn[pl.ds(r + pad + wide, chunk)])
            + cy[own] * (v - below(dirn, r + pad, chunk))
            + ups[1] * (v - above(dirn, r + pad, chunk))
            + cz[here] * (v - pltpu.roll(v, 1, axis=1))
            + upper * (v - pltpu.roll(v, lanes - 1, axis=1))
        )
        return carry

    sweep(prepare, 0)
    for x in range(along):
        at = pl.multiple_of((blk * along + x) * wide + sub * across + pad, TILE)
        sol[x * across:(x + 1) * across] = dirn[pl.ds(at, across)]
    for b in range(count_blk):
        at = b * along * wide
        res[at:at + wide] = res[at:at + wide] + heat[b * wide:(b + 1) * wide]

    def start(r, acc):
        here = pl.ds(r, chunk)
        dirn[pl.ds(r + pad, chunk)] = res[here]
        return acc + res[here] * res[here]

    def apply(r, acc):
        here = pl.ds(r, chunk)
        own = pl.ds(r + pad, chunk)
        v = dirn[own]
        value = (
            diag[here] * v
            - cx[own] * dirn[pl.ds(r + pad - wide, chunk)]
            - cx[pl.ds(r + pad + wide, chunk)] * dirn[pl.ds(r + pad + wide, chunk)]
            - cy[own] * below(dirn, r + pad, chunk)
            - above(cy, r + pad, chunk) * above(dirn, r + pad, chunk)
            - cz[here] * pltpu.roll(v, 1, axis=1)
            - czu[here] * pltpu.roll(v, lanes - 1, axis=1)
        )
        image[here] = value
        return acc + v * value

    norm = jnp.sum(sweep(start, none))
    for step in range(ITERS):
        alpha = norm / jnp.sum(sweep(apply, none))
        for x in range(along):
            at = pl.multiple_of((blk * along + x) * wide + sub * across + pad, TILE)
            own = slice(x * across, (x + 1) * across)
            sol[own] = sol[own] + alpha * dirn[pl.ds(at, across)]
        if step + 1 == ITERS:
            break

        def reduce(r, acc, alpha=alpha):
            here = pl.ds(r, chunk)
            value = res[here] - alpha * image[here]
            res[here] = value
            return acc + value * value

        fresh = jnp.sum(sweep(reduce, none))
        beta = fresh / norm

        def turn(r, carry, beta=beta):
            own = pl.ds(r + pad, chunk)
            dirn[own] = res[pl.ds(r, chunk)] + beta * dirn[own]
            return carry

        sweep(turn, 0)
        norm = fresh
    for x in range(along):
        out_ref[x] = sol[x * across:(x + 1) * across]


def swap(value, axis, flip):
    count = lax.axis_size(axis)
    return lax.ppermute(value, axis, [(i, i ^ flip) for i in range(count)])


def outer(value):
    count = lax.axis_size("blk")
    pairs = [(i, (i + 1 if i % 2 else i - 1) % count) for i in range(count)]
    return lax.ppermute(value, "blk", pairs)


def ring(value, axis, step):
    count = lax.axis_size(axis)
    return lax.ppermute(value, axis, [(i, (i + step) % count) for i in range(count)])


def flips(count):
    return [1 << k for k in reversed(range((count - 1).bit_length()))]


def shards(
    mass_per_volume,
    flow_speed_vector,
    normal_stress,
    facing_strip_index,
    solid_kelvin,
    face_coupling,
    substance_index,
    substance_storage,
):
    planes, rows, lanes = mass_per_volume.shape
    along, across, _ = solid_kelvin.shape
    count_blk, count_sub = lax.axis_size("blk"), lax.axis_size("sub")
    devices = count_blk * count_sub
    cells = along * across
    edge = up_to_tile(FIELDS * planes * HALO)
    each = across + TILE
    record = 5 * cells + rows + TILE

    state, yedge, aface, bface, metal, wall = call(
        pack_kernel,
        [
            f32(FIELDS, planes, rows, lanes), f32(2, edge, lanes),
            f32(FIELDS, HALO, rows, lanes), f32(FIELDS, HALO, rows, lanes),
            f32(record, lanes), f32(each, lanes),
        ],
        [
            mass_per_volume, flow_speed_vector, normal_stress,
            facing_strip_index.reshape(1, rows), solid_kelvin, face_coupling[:3],
            substance_index, substance_storage,
        ],
        smem=(7,),
        name="pack",
    )
    paired = count_blk == 4 and count_sub == 2
    span = up_to_tile(FIELDS * HALO * HALO)
    if paired:
        wall_a = swap(wall, "blk", 1)
    bface = outer(bface)
    if paired:
        ypay = jnp.concatenate([yedge.reshape(2 * edge, lanes), wall, wall_a], axis=0)
        yrecv = swap(ypay, "sub", 1)
        ylo, yhi, lo_at, hi_at = yrecv, yrecv, edge, 0
        parts = [wall, wall_a, yrecv]
        starts = [(0, each), (0, each), (2 * edge, 2 * each)]
    else:
        ylo, yhi, lo_at, hi_at = ring(yedge[1], "sub", 1), ring(yedge[0], "sub", -1), 0, 0
        parts, starts = [], []
    aface = swap(aface, "blk", 1)
    metal_b = swap(metal, "blk", flips(count_blk)[0])
    aedge, bedge = call(
        functools.partial(edge_kernel, planes, lo_at, hi_at, starts),
        [f32(2 * span, lanes), f32(2 * span + sum(c for _, c in starts), lanes)],
        [ylo, yhi, *parts],
        name="edges",
    )
    bedge = outer(bedge)
    aedge = swap(aedge, "blk", 1)
    if paired:
        walls = [wall, wall_a, yrecv, yrecv] + 4 * [bedge]
        wall_at = [(0, 0, 0), (0, 1, 0), (2 * edge, 0, 1), (2 * edge + each, 1, 1)]
        wall_at += [(2 * span + k * each, 3 ^ (k & 1), k >> 1) for k in range(4)]
    else:
        walls = [lax.all_gather(wall, ("blk", "sub"), axis=0, tiled=True)]
        wall_at = None
    total = (planes + 2 * HALO) * (rows + TILE) + 2 * TILE
    block, zlo, zhi = call(
        functools.partial(
            assemble_kernel, ((count_blk, count_sub), across), lo_at, hi_at, wall_at
        ),
        [
            f32(FIELDS + 1, total, lanes),
            f32(up_to_tile((FIELDS + 1) * HALO), total),
            f32(up_to_tile((FIELDS + 1) * HALO), total),
        ],
        [state, aface, bface, ylo, yhi, aedge, bedge, *walls],
        scratch=[
            pltpu.VMEM((devices * each, lanes), jnp.float32),
            pltpu.VMEM((rows + 2 * TILE, lanes), jnp.float32),
        ],
        name="assemble",
    )
    zlo, zhi = ring(zhi, "grp", 1), ring(zlo, "grp", -1)

    held, order = metal[None], [(0, 0)]
    steps = [("blk", flip) for flip in flips(count_blk)[:-1]]
    steps += [("sub", flip) for flip in flips(count_sub)]
    for k, (axis, flip) in enumerate(steps):
        other = metal_b[None] if k == 0 else swap(held, axis, flip)
        held = jnp.concatenate([held, other], axis=0)
        order = order + [
            (b ^ flip, s) if axis == "blk" else (b, s ^ flip) for b, s in order
        ]
    other = swap(held, "blk", 1)
    order = order + [(b ^ 1, s) for b, s in order]
    wide = count_sub * across
    cells_all = devices * cells
    metal_next = call(
        functools.partial(metal_kernel, (count_blk, count_sub, along, across), rows, order),
        f32(along, across, lanes),
        [held, other],
        scratch=[
            pltpu.VMEM((cells, lanes), jnp.float32),
            pltpu.VMEM((cells_all, lanes), jnp.float32),
            pltpu.VMEM((cells_all + 2 * wide, lanes), jnp.float32),
            pltpu.VMEM((cells_all, lanes), jnp.float32),
            pltpu.VMEM((cells_all, lanes), jnp.float32),
            pltpu.VMEM((cells_all + 2 * wide, lanes), jnp.float32),
            pltpu.VMEM((cells_all + 2 * wide, lanes), jnp.float32),
            pltpu.VMEM((cells_all, lanes), jnp.float32),
            pltpu.VMEM((cells_all, lanes), jnp.float32),
            pltpu.VMEM((cells_all, lanes), jnp.float32),
            pltpu.VMEM((devices * across, lanes), jnp.float32),
        ],
        name="metal",
    )
    big = pltpu.VMEM((FIELDS, total, 2 * lanes), jnp.float32)
    fluid_next = call(
        functools.partial(fluid_kernel, planes, rows),
        f32(FIELDS, planes, rows, lanes),
        [block, zlo, zhi],
        scratch=[
            pltpu.VMEM((FIELDS + 1, total, 2 * lanes), jnp.float32),
            big, big, big, big, big,
            pltpu.VMEM((TILE, total), jnp.float32),
        ],
        name="fluid",
    )
    return (fluid_next, metal_next)


def solution(mesh):
    in_specs = (
        P("blk", "sub", "grp"),
        P(None, "blk", "sub", "grp"),
        P("blk", "sub", "grp"),
        P("grp", "blk", "sub"),
        P("blk", "sub", "grp"),
        P(None, "blk", "sub", "grp"),
        P("blk", "sub", "grp"),
        P(),
    )
    out_specs = (P(None, "blk", "sub", "grp"), P("blk", "sub", "grp"))
    return jax.shard_map(shards, mesh=mesh, in_specs=in_specs, out_specs=out_specs, check_vma=False)
```

```python
import functools
import math

import jax
import jax.numpy as jnp
from jax import lax
from jax.experimental import pallas as pl
from jax.experimental.pallas import tpu as pltpu
from jax.sharding import PartitionSpec as P


ITERS = 4
HALO = 3
TILE = 8
FIELDS = 5

gamma_gas = 1.4
time_step = 0.1
viscosity = 0.05
film_coeff = 1.0
third_part = 1.0 / 3.0
two_thirds = 2.0 / 3.0

HIGHEST = lax.Precision.HIGHEST
SPARE_BYTES = 6 * 1024 * 1024


def bytes_of(shapes):
    total = 0
    for shape in shapes:
        *lead, rows, lanes = (1, 1, *shape)
        total += 4 * math.prod(lead) * up_to_tile(rows) * (-(-lanes // 128) * 128)
    return total


def call(body, out, inputs, hbm=(), cost=100_000, scratch=()):
    inputs = [
        pltpu.with_memory_space_constraint(x, pltpu.HBM) if i in hbm else x
        for i, x in enumerate(inputs)
    ]
    limit = SPARE_BYTES + bytes_of(
        [x.shape for i, x in enumerate(inputs) if i not in hbm]
        + [x.shape for x in jax.tree.leaves(out)]
        + [x for x in scratch if isinstance(x, tuple)]
    )
    return pl.pallas_call(
        body,
        out_shape=out,
        in_specs=[
            pl.BlockSpec(memory_space=pltpu.HBM if i in hbm else pltpu.VMEM)
            for i in range(len(inputs))
        ],
        out_specs=jax.tree.map(lambda _: pl.BlockSpec(memory_space=pltpu.VMEM), out),
        scratch_shapes=[
            pltpu.VMEM(x, jnp.float32) if isinstance(x, tuple) else x for x in scratch
        ],
        cost_estimate=pl.CostEstimate(flops=cost, bytes_accessed=cost, transcendentals=0),
        compiler_params=pltpu.CompilerParams(vmem_limit_bytes=limit),
    )(*inputs)


def f32(*shape):
    return jax.ShapeDtypeStruct(shape, jnp.float32)


def up_to_tile(count):
    return -(-count // TILE) * TILE


def iota(shape, dim):
    return lax.broadcasted_iota(jnp.int32, shape, dim)


def dot(a, b, a_dim, b_dim):
    return lax.dot_general(
        a, b, (((a_dim,), (b_dim,)), ((), ())), precision=HIGHEST,
        preferred_element_type=jnp.float32,
    )


def parity():
    return lax.rem(lax.axis_index("blk"), 2)


def pack_kernel(
    rho_hbm, vel_hbm, pre_hbm, route_hbm, kelvin_hbm, couple_hbm, kind_hbm, store_hbm,
    state_ref, yedge_ref, apay_ref, bpay_ref, metal_ref, wall_ref,
    rho_ref, vel_ref, pre_ref, route_ref, kind_ref, store_ref, arrived,
):
    planes, rows, lanes = rho_ref.shape
    cells = kind_ref.shape[0]
    across = wall_ref.shape[0] - TILE
    face = FIELDS * HALO * rows
    copies = [
        pltpu.make_async_copy(src, dst, arrived.at[k])
        for k, (src, dst) in enumerate((
            (rho_hbm, rho_ref), (vel_hbm, vel_ref), (pre_hbm, pre_ref),
            (kelvin_hbm, metal_ref.at[0:cells]),
            (couple_hbm.at[0:3 * cells], metal_ref.at[2 * cells:5 * cells]),
            (kind_hbm, kind_ref), (store_hbm, store_ref), (route_hbm, route_ref),
        ))
    ]
    for copy in copies:
        copy.start()
    for copy in copies[:3]:
        copy.wait()
    for x in range(planes):
        rho = rho_ref[x]
        vel = [vel_ref[d, x] for d in range(3)]
        mom = [rho * v for v in vel]
        kinetic = mom[0] * vel[0] + mom[1] * vel[1] + mom[2] * vel[2]
        energy = pre_ref[x] / (gamma_gas - 1.0) + 0.5 * kinetic
        for f, value in enumerate([rho, *mom, energy]):
            state_ref[f, x] = value
    used = FIELDS * planes * HALO
    for f in range(FIELDS):
        for x in range(planes):
            at = (f * planes + x) * HALO
            yedge_ref[0, at:at + HALO] = state_ref[f, x, 0:HALO]
            yedge_ref[1, at:at + HALO] = state_ref[f, x, rows - HALO:rows]
    if yedge_ref.shape[1] > used:
        for side in range(2):
            yedge_ref[side, used:] = jnp.zeros(
                (yedge_ref.shape[1] - used, lanes), jnp.float32
            )
    for odd in range(2):

        @pl.when(parity() == odd)
        def _():
            for f in range(FIELDS):
                for j in range(HALO):
                    at = (f * HALO + j) * rows
                    apay_ref[at:at + rows] = state_ref[f, j + (planes - HALO) * (1 - odd)]
                    bpay_ref[at:at + rows] = state_ref[f, j + (planes - HALO) * odd]

    for copy in copies[3:]:
        copy.wait()
    wall_ref[0:across] = metal_ref[0:across]
    wall_ref[across:across + TILE] = jnp.zeros((TILE, lanes), jnp.float32)
    wall_ref[across:across + 1, 0:rows] = route_ref[...].astype(jnp.float32)
    kind = kind_ref[...]
    capacity = jnp.zeros((cells, lanes), jnp.float32)
    for m in range(store_ref.shape[0]):
        capacity = jnp.where(kind == m, store_ref[m], capacity)
    metal_ref[cells:2 * cells] = capacity
    metal_ref[5 * cells:5 * cells + rows] = pre_ref[0] / rho_ref[0]
    metal_ref[5 * cells + rows:5 * cells + rows + TILE] = wall_ref[across:across + TILE]
    record = 5 * cells + rows + TILE
    apay_ref[face:face + record] = metal_ref[...]
    bpay_ref[face:face + record] = metal_ref[...]


def edge_kernel(planes, lo_at, hi_at, starts, *refs):
    ylo_ref, yhi_ref = refs[0], refs[1]
    parts, (aedge_ref, bedge_ref) = refs[2:-2], refs[-2:]
    used = FIELDS * HALO * HALO
    span = up_to_tile(used)
    for odd in range(2):

        @pl.when(parity() == odd)
        def _():
            for out, first in (
                (aedge_ref, (planes - HALO) * (1 - odd)),
                (bedge_ref, (planes - HALO) * odd),
            ):
                for f in range(FIELDS):
                    for side, (ref, base) in enumerate(((ylo_ref, lo_at), (yhi_ref, hi_at))):
                        at = side * span + f * HALO * HALO
                        src = base + (f * planes + first) * HALO
                        out[at:at + HALO * HALO] = ref[src:src + HALO * HALO]

    for out in (aedge_ref, bedge_ref):
        for side in range(2):
            if span > used:
                out[side * span + used:(side + 1) * span] = jnp.zeros(
                    (span - used, ylo_ref.shape[1]), jnp.float32
                )
    at = 2 * span
    for ref, (start, count) in zip(parts, starts):
        bedge_ref[at:at + count] = ref[start:start + count]
        at += count


def assemble_kernel(dims, lo_at, hi_at, wall_at, *refs):
    axes, across = dims
    count_blk, count_sub = axes
    state_ref, aface_ref, bface_ref, ylo_ref, yhi_ref, aedge_ref, bedge_ref = refs[:7]
    wall_refs = refs[7:-5]
    block_ref, zlo_ref, zhi_ref, table, seen = refs[-5:]
    _, planes, rows, lanes = state_ref.shape
    deep, stride = block_ref.shape[1:3]
    span = up_to_tile(FIELDS * HALO * HALO)
    each = across + TILE
    blk, sub = lax.axis_index("blk"), lax.axis_index("sub")

    def place(f, x, own, lo, hi):
        block_ref[f, x + HALO, 0:rows] = own
        block_ref[f, x + HALO, rows:rows + HALO] = hi
        block_ref[f, x + HALO, stride - HALO:stride] = lo

    for f in range(FIELDS):
        for x in range(planes):
            at = (f * planes + x) * HALO
            place(
                f, x, state_ref[f, x],
                ylo_ref[lo_at + at:lo_at + at + HALO], yhi_ref[hi_at + at:hi_at + at + HALO],
            )
    for odd in range(2):

        @pl.when(parity() == odd)
        def _():
            for face_ref, edge_ref, above in (
                (aface_ref, aedge_ref, odd == 0), (bface_ref, bedge_ref, odd == 1),
            ):
                for f in range(FIELDS):
                    for j in range(HALO):
                        at = (f * HALO + j) * HALO
                        place(
                            f, planes + j if above else j - HALO,
                            face_ref[(f * HALO + j) * rows:(f * HALO + j + 1) * rows],
                            edge_ref[at:at + HALO], edge_ref[span + at:span + at + HALO],
                        )

    if wall_at is None:
        table = wall_refs[0]
    else:
        for ref, (start, flip_blk, flip_sub) in zip(wall_refs, wall_at):
            device = jnp.bitwise_xor(blk, flip_blk) * count_sub + jnp.bitwise_xor(sub, flip_sub)
            table[pl.ds(pl.multiple_of(device * each, TILE), each)] = ref[start:start + each]
    devices = count_blk * count_sub
    walls = jnp.concatenate(
        [table[d * each:d * each + across] for d in range(devices)], axis=0
    )

    def facing(blk_at, sub_at):
        device = lax.rem(blk_at, count_blk) * count_sub + lax.rem(sub_at, count_sub)
        at = pl.multiple_of(device * each + across, TILE)
        routes = table[pl.ds(at, TILE)][0:1, 0:rows].astype(jnp.int32)
        chosen = (iota((devices * across, rows), 0) == routes).astype(jnp.float32)
        return dot(chosen, walls, 0, 0)

    block_ref[FIELDS] = jnp.zeros(block_ref.shape[1:], jnp.float32)
    for x, blk_at in ((0, blk), (planes, blk + 1)):
        below = facing(blk_at, sub + count_sub - 1)
        above = below if count_sub == 2 else facing(blk_at, sub + 1)
        seen[0:rows] = facing(blk_at, sub)
        seen[rows:] = jnp.zeros((stride - rows, lanes), jnp.float32)
        seen[rows:rows + HALO] = above[0:HALO]
        seen[stride - HALO:stride] = below[rows - HALO:rows]
        rho, mx, my, mz, energy = [block_ref[f, x + HALO] for f in range(FIELDS)]
        pressure = (gamma_gas - 1.0) * (energy - 0.5 * (mx * mx + my * my + mz * mz) / rho)
        block_ref[FIELDS, x + HALO] = film_coeff * (pressure / rho - seen[...])
    pick = iota((TILE, lanes), 0)
    cell = iota((TILE, lanes), 1)
    chosen = (
        ((pick == cell) & (pick < HALO))
        | ((pick - HALO + lanes - HALO == cell) & (pick >= HALO) & (pick < 2 * HALO))
    ).astype(jnp.float32)
    size = deep * stride
    for f in range(FIELDS + 1):
        ends = dot(chosen, block_ref[f].reshape(size, lanes), 1, 1)
        zlo_ref[f * HALO:(f + 1) * HALO, 0:size] = ends[0:HALO]
        zhi_ref[f * HALO:(f + 1) * HALO, 0:size] = ends[HALO:2 * HALO]
    used = (FIELDS + 1) * HALO
    for ref in (zlo_ref, zhi_ref):
        if ref.shape[1] > size:
            ref[:, size:] = jnp.zeros((ref.shape[0], ref.shape[1] - size), jnp.float32)
        if ref.shape[0] > used:
            ref[used:] = jnp.zeros((ref.shape[0] - used, ref.shape[1]), jnp.float32)


def primitives(u):
    rho, mx, my, mz, energy = u
    inverse = 1.0 / rho
    ux, uy, uz = mx * inverse, my * inverse, mz * inverse
    pressure = (gamma_gas - 1.0) * (energy - 0.5 * (mx * ux + my * uy + mz * uz))
    sound = jnp.sqrt(gamma_gas * pressure * inverse)
    return [
        ux, uy, uz, jnp.abs(ux) + sound, jnp.abs(uy) + sound, jnp.abs(uz) + sound,
        pressure, energy + pressure,
    ]


def faces(d, lo, hi):
    def flux(v):
        speed, pressure, enthalpy = v[5], v[7], v[8]
        f = [v[1 + d]] + [v[1 + i] * speed for i in range(3)] + [enthalpy * speed]
        f[1 + d] = f[1 + d] + pressure
        return f

    below, here = flux(lo), flux(hi)
    fast = jnp.maximum(lo[6], hi[6])
    slow = fast + 2.0 * viscosity
    return [
        (below[i] + here[i]) - (fast if i == 0 else slow) * (hi[i] - lo[i]) for i in range(5)
    ]


def fluid_kernel(
    block_ref, above_ref, below_ref, low_ref, high_ref, out_ref,
    now, prim, xface, ends, slab_base, slab, comb,
):
    _, planes, rows, lanes = out_ref.shape
    deep, stride = block_ref.shape[1:3]
    size = deep * stride
    wide = slab.shape[2]
    group = TILE
    part = FIELDS * TILE
    source = iota((lanes, FIELDS * lanes), 0)
    target = iota((lanes, FIELDS * lanes), 1)
    field = lax.rem(source, part) // TILE
    end = lax.rem(source, TILE)
    spread = (
        ((end == 0) & (target == field * lanes))
        | ((end == 1) & (target == field * lanes + lanes - 1))
    ) & (source < 3 * part)
    spread = spread.astype(jnp.float32).astype(jnp.bfloat16)
    comb[...] = jnp.zeros(comb.shape, jnp.float32)
    slab_base[...] = jnp.zeros(slab_base.shape, jnp.float32)
    for f in range(FIELDS + 1):
        at = slice(f * HALO, (f + 1) * HALO)
        slab_base[f, 0:HALO] = below_ref[at]
        slab_base[f, HALO:2 * HALO] = low_ref[at]
        slab_base[f, group:group + HALO] = high_ref[at]
        slab_base[f, group + HALO:group + 2 * HALO] = above_ref[at]
    for f in range(FIELDS):
        slab[f] = slab_base[f]

    @pl.loop(0, deep)
    def _(x):
        for f in range(FIELDS):
            now[f, x] = block_ref[f, x]

    first_row = lax.rem(iota((2 * TILE, wide), 1), stride) == 0
    last_row = lax.rem(iota((2 * TILE, wide), 1), stride) == stride - 1

    def lane_roll(v, shift):
        return pltpu.roll(v, shift % wide, axis=1)

    def advance(old, change, start, sink, a, b):
        fresh = old - (0.5 * time_step) * change
        if sink is not None:
            fresh = fresh - time_step * sink
        return a * start + b * fresh

    lane = iota((stride, lanes), 1)

    @pl.loop(0, 3)
    def _(stage):
        a = jnp.where(stage == 0, 0.0, jnp.where(stage == 1, 0.75, third_part))
        b = jnp.where(stage == 0, 1.0, jnp.where(stage == 1, 0.25, two_thirds))

        u = [slab[f] for f in range(FIELDS)]
        q = primitives(u)
        hi = u + [q[2], q[5], q[6], q[7]]
        lo = [pltpu.roll(v, 1, axis=0) for v in hi]
        zface = faces(2, lo, hi)
        for f in range(FIELDS):
            comb[f * TILE:f * TILE + 1] = zface[f][HALO:HALO + 1]
            comb[f * TILE + 1:f * TILE + 2] = zface[f][group + HALO:group + HALO + 1]
        change = [pltpu.roll(v, 2 * TILE - 1, axis=0) - v for v in zface]
        hi = u + [q[0], q[3], q[6], q[7]]
        face = faces(0, [lane_roll(v, stride) for v in hi], hi)
        change = [c + (lane_roll(v, -stride) - v) for c, v in zip(change, face)]
        hi = u + [q[1], q[4], q[6], q[7]]
        lo = [
            jnp.where(first_row, lane_roll(v, 1 - stride), lane_roll(v, 1)) for v in hi
        ]
        face = faces(1, lo, hi)
        change = [
            c + (jnp.where(last_row, lane_roll(v, stride - 1), lane_roll(v, -1)) - v)
            for c, v in zip(change, face)
        ]
        for f in range(FIELDS):
            sink = slab_base[FIELDS] if f == FIELDS - 1 else None
            slab[f] = advance(u[f], change[f], slab_base[f], sink, a, b)
        whole = comb[0:part]
        for k in range(2):
            piece = whole.astype(jnp.bfloat16).astype(jnp.float32)
            comb[k * part:(k + 1) * part] = piece
            whole = whole - piece
        comb[2 * part:3 * part] = whole
        turned = jnp.transpose(comb[...]).astype(jnp.bfloat16)
        moved = lax.dot_general(
            turned, spread, (((1,), (0,)), ((), ())), preferred_element_type=jnp.float32
        )
        for f in range(FIELDS):
            ends[f] = moved[0:size, f * lanes:(f + 1) * lanes].reshape(deep, stride, lanes)

        low = stage + 1
        high = deep - 1 - stage

        @pl.loop(low - 1, high + 1)
        def _(x):
            for k, value in enumerate(primitives([now[f, x] for f in range(FIELDS)])):
                prim[k, x] = value

        def cells(x, d):
            return [now[f, x] for f in range(FIELDS)] + [
                prim[d, x], prim[3 + d, x], prim[6, x], prim[7, x]
            ]

        @pl.loop(low, high + 1)
        def _(x):
            new = faces(0, cells(x - 1, 0), cells(x, 0))
            old = lax.rem(x, 2)
            for f in range(FIELDS):
                xface[old, f] = new[f]

            @pl.when(x > low)
            def _():
                p = x - 1
                change = [new[f] - xface[1 - old, f] for f in range(FIELDS)]
                hi = cells(p, 1)
                lo = [pltpu.roll(v, 1, axis=0) for v in hi]
                face = faces(1, lo, hi)
                change = [
                    c + (pltpu.roll(v, stride - 1, axis=0) - v) for c, v in zip(change, face)
                ]
                hi = cells(p, 2)
                lo = [pltpu.roll(v, 1, axis=1) for v in hi]
                face = faces(2, lo, hi)
                for f in range(FIELDS):
                    end = ends[f, p]
                    top = jnp.where(lane == lanes - 1, end, pltpu.roll(face[f], lanes - 1, axis=1))
                    low_face = jnp.where(lane == 0, end, face[f])
                    sink = block_ref[FIELDS, p] if f == FIELDS - 1 else None
                    now[f, p] = advance(
                        now[f, p], change[f] + (top - low_face), block_ref[f, p], sink, a, b
                    )

    for f in range(FIELDS):
        for x in range(planes):
            out_ref[f, x] = now[f, x + HALO, 0:rows]


def metal_kernel(dims, rows, where, order, *refs):
    count_blk, count_sub, along, across = dims
    devices = count_blk * count_sub
    pieces = [(refs[k], start) for k, start in where]
    (
        out_ref, sol, res, dirn, image, diag, cx, cy, cz, cyu, czu, caps, heat, route, faced,
    ) = refs[-15:]
    lanes = out_ref.shape[-1]
    cells = along * across
    wide = count_sub * across
    deep = count_blk * along
    blk, sub = lax.axis_index("blk"), lax.axis_index("sub")
    mine = blk * along
    side = pl.multiple_of(sub * across, TILE)

    zero = jnp.zeros((wide, lanes), jnp.float32)
    for ref in (dirn, cx):
        ref[0] = zero
        ref[deep + 1] = zero

    for n, ((ref, first), (flip_blk, flip_sub)) in enumerate(zip(pieces, order)):
        b = jnp.bitwise_xor(blk, flip_blk) * along
        y = pl.multiple_of(jnp.bitwise_xor(sub, flip_sub) * across, TILE)
        for field, (dest, shift) in enumerate(((dirn, 1), (caps, 0), (cx, 1), (cy, 0), (cz, 0))):
            start = first + field * cells
            dest[pl.ds(b + shift, along), pl.ds(y, across)] = ref[
                start:start + cells
            ].reshape(along, across, lanes)
        start = first + 5 * cells
        faced[n * rows:(n + 1) * rows] = ref[start:start + rows]
        route[:, n * rows:(n + 1) * rows] = ref[start + rows:start + rows + TILE][:, 0:rows]

    walls = jnp.concatenate([dirn[1 + b * along] for b in range(count_blk)], axis=0)
    strips = devices * across
    chosen = (
        iota((strips, devices * rows), 0) == route[0:1].astype(jnp.int32)
    ).astype(jnp.float32)
    flux = film_coeff * (faced[...] - dot(chosen, walls, 0, 0))
    heat[...] = dot(chosen, flux, 1, 0)

    chunk = 4 if deep % 4 == 0 else 1
    none = jnp.zeros((TILE, lanes), jnp.float32)

    def sweep(body, init):
        return lax.fori_loop(0, deep // chunk, lambda i, c: body(i * chunk, c), init)

    def fold(value):
        return jnp.sum(value.reshape(-1, TILE, lanes), axis=0)

    def turned(v, step, axis):
        return pltpu.roll(v, step % v.shape[axis], axis=axis)

    def prepare(x, carry):
        here, own = pl.ds(x, chunk), pl.ds(x + 1, chunk)
        ups = cx[pl.ds(x + 2, chunk)], turned(cy[here], -1, 1), turned(cz[here], -1, 2)
        cyu[here] = ups[1]
        czu[here] = ups[2]
        diag[here] = caps[here] + ((cx[own] + ups[0]) + (cy[here] + ups[1]) + (cz[here] + ups[2]))
        v = dirn[own]
        res[here] = (
            cx[own] * (dirn[pl.ds(x, chunk)] - v)
            + ups[0] * (dirn[pl.ds(x + 2, chunk)] - v)
            + (cy[here] * (turned(v, 1, 1) - v) + ups[1] * (turned(v, -1, 1) - v))
            + (cz[here] * (turned(v, 1, 2) - v) + ups[2] * (turned(v, -1, 2) - v))
        )
        return carry

    sweep(prepare, 0)
    sol[...] = dirn[pl.ds(mine + 1, along), pl.ds(side, across)]
    for b in range(count_blk):
        res[b * along] = res[b * along] + heat[b * wide:(b + 1) * wide]

    def start(x, acc):
        here = pl.ds(x, chunk)
        dirn[pl.ds(x + 1, chunk)] = res[here]
        return acc + fold(res[here] * res[here])

    def apply(x, acc):
        here, own = pl.ds(x, chunk), pl.ds(x + 1, chunk)
        v = dirn[own]
        value = (
            diag[here] * v
            - (cx[own] * dirn[pl.ds(x, chunk)] + cx[pl.ds(x + 2, chunk)] * dirn[pl.ds(x + 2, chunk)])
            - (cy[here] * turned(v, 1, 1) + cyu[here] * turned(v, -1, 1))
            - (cz[here] * turned(v, 1, 2) + czu[here] * turned(v, -1, 2))
        )
        image[here] = value
        return acc + fold(v * value)

    norm = jnp.sum(sweep(start, none))
    for step in range(ITERS):
        alpha = norm / jnp.sum(sweep(apply, none))
        sol[...] = sol[...] + alpha * dirn[pl.ds(mine + 1, along), pl.ds(side, across)]
        if step + 1 == ITERS:
            break

        def reduce(x, acc, alpha=alpha):
            here = pl.ds(x, chunk)
            value = res[here] - alpha * image[here]
            res[here] = value
            return acc + fold(value * value)

        fresh = jnp.sum(sweep(reduce, none))
        beta = fresh / norm

        def turn(x, carry, beta=beta):
            own = pl.ds(x + 1, chunk)
            dirn[own] = res[pl.ds(x, chunk)] + beta * dirn[own]
            return carry

        sweep(turn, 0)
        norm = fresh
    out_ref[...] = sol[...]


def swap(value, axis, flip):
    count = lax.axis_size(axis)
    return lax.ppermute(value, axis, [(i, i ^ flip) for i in range(count)])


def outer(value):
    count = lax.axis_size("blk")
    pairs = [(i, (i + 1 if i % 2 else i - 1) % count) for i in range(count)]
    return lax.ppermute(value, "blk", pairs)


def ring(value, axis, step):
    count = lax.axis_size(axis)
    return lax.ppermute(value, axis, [(i, (i + step) % count) for i in range(count)])


def flips(count):
    return [1 << k for k in reversed(range((count - 1).bit_length()))]


def shards(
    mass_per_volume,
    flow_speed_vector,
    normal_stress,
    facing_strip_index,
    solid_kelvin,
    face_coupling,
    substance_index,
    substance_storage,
):
    planes, rows, lanes = mass_per_volume.shape
    along, across, _ = solid_kelvin.shape
    count_blk, count_sub = lax.axis_size("blk"), lax.axis_size("sub")
    devices = count_blk * count_sub
    cells = along * across
    edge = up_to_tile(FIELDS * planes * HALO)
    each = across + TILE
    record = 5 * cells + rows + TILE

    face = FIELDS * HALO * rows
    state, yedge, apay, bpay, metal, wall = call(
        pack_kernel,
        [
            f32(FIELDS, planes, rows, lanes), f32(2, edge, lanes),
            f32(face + record, lanes), f32(face + record, lanes),
            f32(record, lanes), f32(each, lanes),
        ],
        [
            mass_per_volume, flow_speed_vector, normal_stress,
            facing_strip_index.reshape(1, rows), solid_kelvin.reshape(cells, lanes),
            face_coupling.reshape(6 * cells, lanes), substance_index.reshape(cells, lanes),
            substance_storage,
        ],
        hbm=tuple(range(8)),
        scratch=[
            (planes, rows, lanes), (3, planes, rows, lanes), (planes, rows, lanes),
            pltpu.VMEM((1, rows), jnp.int32), pltpu.VMEM((cells, lanes), jnp.int32),
            pltpu.SMEM(substance_storage.shape, jnp.float32), pltpu.SemaphoreType.DMA((8,)),
        ],
    )
    paired = count_blk == 4 and count_sub == 2
    span = up_to_tile(FIELDS * HALO * HALO)
    bpay = outer(bpay)
    if paired:
        wall_a = swap(wall, "blk", 1)
        ypay = jnp.concatenate([yedge.reshape(2 * edge, lanes), wall, wall_a], axis=0)
        yrecv = swap(ypay, "sub", 1)
        ylo, yhi, lo_at, hi_at = yrecv, yrecv, edge, 0
        parts = [wall, wall_a, yrecv]
        starts = [(0, each), (0, each), (2 * edge, 2 * each)]
    else:
        ylo, yhi, lo_at, hi_at = ring(yedge[1], "sub", 1), ring(yedge[0], "sub", -1), 0, 0
        parts, starts = [], []
    apay = swap(apay, "blk", 1)
    aedge, bedge = call(
        functools.partial(edge_kernel, planes, lo_at, hi_at, starts),
        [f32(2 * span, lanes), f32(2 * span + sum(c for _, c in starts), lanes)],
        [ylo, yhi, *parts],
    )
    bedge = outer(bedge)
    aedge = swap(aedge, "blk", 1)
    if paired:
        walls = [wall, wall_a, yrecv, yrecv] + 4 * [bedge]
        wall_at = [(0, 0, 0), (0, 1, 0), (2 * edge, 0, 1), (2 * edge + each, 1, 1)]
        wall_at += [(2 * span + k * each, 3 ^ (k & 1), k >> 1) for k in range(4)]
    else:
        walls = [lax.all_gather(wall, ("blk", "sub"), axis=0, tiled=True)]
        wall_at = None
    deep, stride = planes + 2 * HALO, rows + TILE
    ends_rows = up_to_tile((FIELDS + 1) * HALO)
    wide_lanes = -(-deep * stride // lanes) * lanes
    block, zlo, zhi = call(
        functools.partial(
            assemble_kernel, ((count_blk, count_sub), across), lo_at, hi_at, wall_at
        ),
        [
            f32(FIELDS + 1, deep, stride, lanes),
            f32(ends_rows, wide_lanes),
            f32(ends_rows, wide_lanes),
        ],
        [state, apay, bpay, ylo, yhi, aedge, bedge, *walls],
        scratch=[(devices * each, lanes), (stride, lanes)],
    )
    zbelow = ring(zhi, "grp", 1)
    zabove = ring(zlo, "grp", -1)

    if paired:
        far = bpay[face:]
        near_y = swap(metal, "sub", 1)
        far_y = swap(far, "sub", 1)
        mates = swap(jnp.concatenate([far, near_y], axis=0), "blk", 1)
        mate_far_y = swap(far_y, "blk", 1)
        pieces = [metal, apay, bpay, near_y, far_y, mates, mate_far_y]
        where = [(0, 0), (1, face), (2, face), (3, 0), (4, 0), (5, 0), (5, record), (6, 0)]
        order = [(0, 0), (1, 0), (3, 0), (0, 1), (3, 1), (2, 0), (1, 1), (2, 1)]
    else:
        held, order = metal, [(0, 0)]
        steps = [("blk", flip) for flip in flips(count_blk)]
        steps += [("sub", flip) for flip in flips(count_sub)]
        for axis, flip in steps:
            held = jnp.concatenate([held, swap(held, axis, flip)], axis=0)
            order = order + [
                (b ^ flip, s) if axis == "blk" else (b, s ^ flip) for b, s in order
            ]
        pieces, where = [held], [(0, k * record) for k in range(devices)]
    wide = count_sub * across
    deep_metal = count_blk * along
    field = (deep_metal, wide, lanes)
    padded = (deep_metal + 2, wide, lanes)
    metal_next = call(
        functools.partial(
            metal_kernel, (count_blk, count_sub, along, across), rows, where, order
        ),
        f32(along, across, lanes),
        pieces,
        scratch=[
            (along, across, lanes), field, padded, field, field, padded, field, field, field,
            field, field, (devices * across, lanes), (TILE, devices * rows), (devices * rows, lanes),
        ],
    )
    fluid_next = call(
        fluid_kernel,
        f32(FIELDS, planes, rows, lanes),
        [block, zabove, zbelow, zlo, zhi],
        scratch=[
            (FIELDS, deep, stride, lanes), (8, deep, stride, lanes), (2, FIELDS, stride, lanes),
            (FIELDS, deep, stride, lanes), (FIELDS + 1, 2 * TILE, wide_lanes),
            (FIELDS, 2 * TILE, wide_lanes), (lanes, wide_lanes),
        ],
    )
    return (fluid_next, metal_next)


def solution(mesh):
    in_specs = (
        P("blk", "sub", "grp"),
        P(None, "blk", "sub", "grp"),
        P("blk", "sub", "grp"),
        P("grp", "blk", "sub"),
        P("blk", "sub", "grp"),
        P(None, "blk", "sub", "grp"),
        P("blk", "sub", "grp"),
        P(),
    )
    out_specs = (P(None, "blk", "sub", "grp"), P("blk", "sub", "grp"))
    return jax.shard_map(shards, mesh=mesh, in_specs=in_specs, out_specs=out_specs, check_vma=False)
```

```python
import functools
import math

import jax
import jax.numpy as jnp
from jax import lax
from jax.experimental import pallas as pl
from jax.experimental.pallas import tpu as pltpu
from jax.sharding import PartitionSpec as P


ITERS = 4
HALO = 3
TILE = 8
FIELDS = 5
ROWS = 512

gamma_gas = 1.4
time_step = 0.1
viscosity = 0.05
film_coeff = 1.0
third_part = 1.0 / 3.0
two_thirds = 2.0 / 3.0

HIGHEST = lax.Precision.HIGHEST
SPARE_BYTES = 6 * 1024 * 1024


def bytes_of(shapes):
    total = 0
    for shape in shapes:
        *lead, rows, lanes = (1, 1, *shape)
        total += 4 * math.prod(lead) * up_to_tile(rows) * (-(-lanes // 128) * 128)
    return total


def call(body, out, inputs, hbm=(), cost=100_000, scratch=()):
    inputs = [
        pltpu.with_memory_space_constraint(x, pltpu.HBM) if i in hbm else x
        for i, x in enumerate(inputs)
    ]
    limit = SPARE_BYTES + bytes_of(
        [x.shape for i, x in enumerate(inputs) if i not in hbm]
        + [x.shape for x in jax.tree.leaves(out)]
        + [x for x in scratch if isinstance(x, tuple)]
    )
    return pl.pallas_call(
        body,
        out_shape=out,
        in_specs=[
            pl.BlockSpec(memory_space=pltpu.HBM if i in hbm else pltpu.VMEM)
            for i in range(len(inputs))
        ],
        out_specs=jax.tree.map(lambda _: pl.BlockSpec(memory_space=pltpu.VMEM), out),
        scratch_shapes=[
            pltpu.VMEM(x, jnp.float32) if isinstance(x, tuple) else x for x in scratch
        ],
        cost_estimate=pl.CostEstimate(flops=cost, bytes_accessed=cost, transcendentals=0),
        compiler_params=pltpu.CompilerParams(vmem_limit_bytes=limit),
    )(*inputs)


def f32(*shape):
    return jax.ShapeDtypeStruct(shape, jnp.float32)


def up_to_tile(count):
    return -(-count // TILE) * TILE


def iota(shape, dim):
    return lax.broadcasted_iota(jnp.int32, shape, dim)


def dot(a, b, a_dim, b_dim):
    return lax.dot_general(
        a, b, (((a_dim,), (b_dim,)), ((), ())), precision=HIGHEST,
        preferred_element_type=jnp.float32,
    )


def pieces_of(value):
    out = []
    for _ in range(2):
        piece = value.astype(jnp.bfloat16)
        out.append(piece)
        value = value - piece.astype(jnp.float32)
    return out + [value.astype(jnp.bfloat16)]


def select_sum(chosen, value, dim):
    flags = chosen.astype(jnp.float32).astype(jnp.bfloat16)
    return sum(
        lax.dot_general(
            flags, piece, (((dim,), (0,)), ((), ())), preferred_element_type=jnp.float32
        )
        for piece in reversed(pieces_of(value))
    )


def parity():
    return lax.rem(lax.axis_index("blk"), 2)


def pack_kernel(
    rho_hbm, vel_hbm, pre_hbm, route_hbm, kelvin_hbm, couple_hbm, kind_hbm, store_hbm,
    state_ref, yedge_ref, apay_ref, bpay_ref, metal_ref, wall_ref,
    rho_ref, vel_ref, pre_ref, route_ref, kind_ref, store_ref, arrived,
):
    planes, rows, lanes = rho_ref.shape
    cells = kind_ref.shape[0]
    across = wall_ref.shape[0] - TILE
    face = FIELDS * HALO * rows
    copies = [
        pltpu.make_async_copy(src, dst, arrived.at[k])
        for k, (src, dst) in enumerate((
            (rho_hbm, rho_ref), (vel_hbm, vel_ref), (pre_hbm, pre_ref),
            (kelvin_hbm, metal_ref.at[0:cells]),
            (couple_hbm.at[0:3 * cells], metal_ref.at[2 * cells:5 * cells]),
            (kind_hbm, kind_ref), (store_hbm, store_ref), (route_hbm, route_ref),
        ))
    ]
    for copy in copies:
        copy.start()
    for copy in copies[:3]:
        copy.wait()
    for x in range(planes):
        rho = rho_ref[x]
        vel = [vel_ref[d, x] for d in range(3)]
        mom = [rho * v for v in vel]
        kinetic = mom[0] * vel[0] + mom[1] * vel[1] + mom[2] * vel[2]
        energy = pre_ref[x] / (gamma_gas - 1.0) + 0.5 * kinetic
        for f, value in enumerate([rho, *mom, energy]):
            state_ref[f, x] = value
    used = FIELDS * planes * HALO
    for f in range(FIELDS):
        for x in range(planes):
            at = (f * planes + x) * HALO
            yedge_ref[0, at:at + HALO] = state_ref[f, x, 0:HALO]
            yedge_ref[1, at:at + HALO] = state_ref[f, x, rows - HALO:rows]
    if yedge_ref.shape[1] > used:
        for side in range(2):
            yedge_ref[side, used:] = jnp.zeros(
                (yedge_ref.shape[1] - used, lanes), jnp.float32
            )
    for odd in range(2):

        @pl.when(parity() == odd)
        def _():
            for f in range(FIELDS):
                for j in range(HALO):
                    at = (f * HALO + j) * rows
                    apay_ref[at:at + rows] = state_ref[f, j + (planes - HALO) * (1 - odd)]
                    bpay_ref[at:at + rows] = state_ref[f, j + (planes - HALO) * odd]

    for copy in copies[3:]:
        copy.wait()
    wall_ref[0:across] = metal_ref[0:across]
    wall_ref[across:across + TILE] = jnp.zeros((TILE, lanes), jnp.float32)
    wall_ref[across:across + 1, 0:rows] = route_ref[...].astype(jnp.float32)
    kind = kind_ref[...]
    capacity = jnp.zeros((cells, lanes), jnp.float32)
    for m in range(store_ref.shape[0]):
        capacity = jnp.where(kind == m, store_ref[m], capacity)
    metal_ref[cells:2 * cells] = capacity
    metal_ref[5 * cells:5 * cells + rows] = pre_ref[0] / rho_ref[0]
    metal_ref[5 * cells + rows:5 * cells + rows + TILE] = wall_ref[across:across + TILE]
    record = 5 * cells + rows + TILE
    apay_ref[face:face + record] = metal_ref[...]
    bpay_ref[face:face + record] = metal_ref[...]


def edge_kernel(planes, lo_at, hi_at, starts, *refs):
    ylo_ref, yhi_ref = refs[0], refs[1]
    parts, (aedge_ref, bedge_ref) = refs[2:-2], refs[-2:]
    used = FIELDS * HALO * HALO
    span = up_to_tile(used)
    for odd in range(2):

        @pl.when(parity() == odd)
        def _():
            for out, first in (
                (aedge_ref, (planes - HALO) * (1 - odd)),
                (bedge_ref, (planes - HALO) * odd),
            ):
                for f in range(FIELDS):
                    for side, (ref, base) in enumerate(((ylo_ref, lo_at), (yhi_ref, hi_at))):
                        at = side * span + f * HALO * HALO
                        src = base + (f * planes + first) * HALO
                        out[at:at + HALO * HALO] = ref[src:src + HALO * HALO]

    for out in (aedge_ref, bedge_ref):
        for side in range(2):
            if span > used:
                out[side * span + used:(side + 1) * span] = jnp.zeros(
                    (span - used, ylo_ref.shape[1]), jnp.float32
                )
    at = 2 * span
    for ref, (start, count) in zip(parts, starts):
        bedge_ref[at:at + count] = ref[start:start + count]
        at += count


def assemble_kernel(dims, lo_at, hi_at, wall_at, *refs):
    axes, across = dims
    count_blk, count_sub = axes
    state_ref, aface_ref, bface_ref, ylo_ref, yhi_ref, aedge_ref, bedge_ref = refs[:7]
    wall_refs = refs[7:-5]
    block_ref, zlo_ref, zhi_ref, table, seen = refs[-5:]
    _, planes, rows, lanes = state_ref.shape
    deep, stride = block_ref.shape[1:3]
    span = up_to_tile(FIELDS * HALO * HALO)
    each = across + TILE
    blk, sub = lax.axis_index("blk"), lax.axis_index("sub")

    def place(f, x, own, lo, hi):
        block_ref[f, x + HALO, 0:rows] = own
        block_ref[f, x + HALO, rows:rows + HALO] = hi
        block_ref[f, x + HALO, stride - HALO:stride] = lo

    for f in range(FIELDS):
        for x in range(planes):
            at = (f * planes + x) * HALO
            place(
                f, x, state_ref[f, x],
                ylo_ref[lo_at + at:lo_at + at + HALO], yhi_ref[hi_at + at:hi_at + at + HALO],
            )
    for odd in range(2):

        @pl.when(parity() == odd)
        def _():
            for face_ref, edge_ref, above in (
                (aface_ref, aedge_ref, odd == 0), (bface_ref, bedge_ref, odd == 1),
            ):
                for f in range(FIELDS):
                    for j in range(HALO):
                        at = (f * HALO + j) * HALO
                        place(
                            f, planes + j if above else j - HALO,
                            face_ref[(f * HALO + j) * rows:(f * HALO + j + 1) * rows],
                            edge_ref[at:at + HALO], edge_ref[span + at:span + at + HALO],
                        )

    if wall_at is None:
        table = wall_refs[0]
    else:
        for ref, (start, flip_blk, flip_sub) in zip(wall_refs, wall_at):
            device = jnp.bitwise_xor(blk, flip_blk) * count_sub + jnp.bitwise_xor(sub, flip_sub)
            table[pl.ds(pl.multiple_of(device * each, TILE), each)] = ref[start:start + each]
    devices = count_blk * count_sub
    walls = jnp.concatenate(
        [table[d * each:d * each + across] for d in range(devices)], axis=0
    )

    def facing(blk_at, sub_at):
        device = lax.rem(blk_at, count_blk) * count_sub + lax.rem(sub_at, count_sub)
        at = pl.multiple_of(device * each + across, TILE)
        routes = table[pl.ds(at, TILE)][0:1, 0:rows].astype(jnp.int32)
        return select_sum(iota((devices * across, rows), 0) == routes, walls, 0)

    block_ref[FIELDS] = jnp.zeros(block_ref.shape[1:], jnp.float32)
    for x, blk_at in ((0, blk), (planes, blk + 1)):
        below = facing(blk_at, sub + count_sub - 1)
        above = below if count_sub == 2 else facing(blk_at, sub + 1)
        seen[0:rows] = facing(blk_at, sub)
        seen[rows:] = jnp.zeros((stride - rows, lanes), jnp.float32)
        seen[rows:rows + HALO] = above[0:HALO]
        seen[stride - HALO:stride] = below[rows - HALO:rows]
        rho, mx, my, mz, energy = [block_ref[f, x + HALO] for f in range(FIELDS)]
        pressure = (gamma_gas - 1.0) * (energy - 0.5 * (mx * mx + my * my + mz * mz) / rho)
        block_ref[FIELDS, x + HALO] = film_coeff * (pressure / rho - seen[...])
    pick = iota((TILE, lanes), 0)
    cell = iota((TILE, lanes), 1)
    chosen = (
        ((pick == cell) & (pick < HALO))
        | ((pick - HALO + lanes - HALO == cell) & (pick >= HALO) & (pick < 2 * HALO))
    ).astype(jnp.float32)
    size = deep * stride
    for f in range(FIELDS + 1):
        ends = dot(chosen, block_ref[f].reshape(size, lanes), 1, 1)
        zlo_ref[f * HALO:(f + 1) * HALO, 0:size] = ends[0:HALO]
        zhi_ref[f * HALO:(f + 1) * HALO, 0:size] = ends[HALO:2 * HALO]
    used = (FIELDS + 1) * HALO
    for ref in (zlo_ref, zhi_ref):
        if ref.shape[1] > size:
            ref[:, size:] = jnp.zeros((ref.shape[0], ref.shape[1] - size), jnp.float32)
        if ref.shape[0] > used:
            ref[used:] = jnp.zeros((ref.shape[0] - used, ref.shape[1]), jnp.float32)


def primitives(u):
    rho, mx, my, mz, energy = u
    inverse = 1.0 / rho
    ux, uy, uz = mx * inverse, my * inverse, mz * inverse
    pressure = (gamma_gas - 1.0) * (energy - 0.5 * (mx * ux + my * uy + mz * uz))
    sound = jnp.sqrt(gamma_gas * pressure * inverse)
    return [
        ux, uy, uz, jnp.abs(ux) + sound, jnp.abs(uy) + sound, jnp.abs(uz) + sound,
        pressure, energy + pressure,
    ]


def faces(d, lo, hi):
    def flux(v):
        speed, pressure, enthalpy = v[5], v[7], v[8]
        f = [v[1 + d]] + [v[1 + i] * speed for i in range(3)] + [enthalpy * speed]
        f[1 + d] = f[1 + d] + pressure
        return f

    below, here = flux(lo), flux(hi)
    fast = jnp.maximum(lo[6], hi[6])
    slow = fast + 2.0 * viscosity
    return [
        (below[i] + here[i]) - (fast if i == 0 else slow) * (hi[i] - lo[i]) for i in range(5)
    ]


def fluid_kernel(
    block_ref, above_ref, below_ref, low_ref, high_ref, out_ref,
    now, prim, xface, ends, slab_base, slab, comb,
):
    _, _, rows, lanes = out_ref.shape
    deep, stride = block_ref.shape[1:3]
    size = deep * stride
    wide = slab.shape[2]
    group = TILE
    part = FIELDS * TILE
    source = iota((lanes, FIELDS * lanes), 0)
    target = iota((lanes, FIELDS * lanes), 1)
    field = lax.rem(source, part) // TILE
    end = lax.rem(source, TILE)
    spread = (
        ((end == 0) & (target == field * lanes))
        | ((end == 1) & (target == field * lanes + lanes - 1))
    ) & (source < 3 * part)
    spread = spread.astype(jnp.float32).astype(jnp.bfloat16)
    comb[...] = jnp.zeros(comb.shape, jnp.float32)
    slab_base[...] = jnp.zeros(slab_base.shape, jnp.float32)
    for f in range(FIELDS + 1):
        at = slice(f * HALO, (f + 1) * HALO)
        slab_base[f, 0:HALO] = below_ref[at]
        slab_base[f, HALO:2 * HALO] = low_ref[at]
        slab_base[f, group:group + HALO] = high_ref[at]
        slab_base[f, group + HALO:group + 2 * HALO] = above_ref[at]
    for f in range(FIELDS):
        slab[f] = slab_base[f]

    first_row = lax.rem(iota((2 * TILE, wide), 1), stride) == 0
    last_row = lax.rem(iota((2 * TILE, wide), 1), stride) == stride - 1

    def lane_roll(v, shift):
        return pltpu.roll(v, shift % wide, axis=1)

    def advance(stage, old, change, start, sink):
        fresh = old - (0.5 * time_step) * change
        if sink is not None:
            fresh = fresh - time_step * sink
        if stage == 0:
            return fresh
        if stage == 1:
            return 0.75 * start + 0.25 * fresh
        return third_part * start + two_thirds * fresh

    lane = iota((stride, lanes), 1)
    for stage in range(3):
        src = block_ref if stage == 0 else now

        u = [slab[f] for f in range(FIELDS)]
        q = primitives(u)
        hi = u + [q[2], q[5], q[6], q[7]]
        lo = [pltpu.roll(v, 1, axis=0) for v in hi]
        zface = faces(2, lo, hi)
        for f in range(FIELDS):
            comb[f * TILE:f * TILE + 1] = zface[f][HALO:HALO + 1]
            comb[f * TILE + 1:f * TILE + 2] = zface[f][group + HALO:group + HALO + 1]
        change = [pltpu.roll(v, 2 * TILE - 1, axis=0) - v for v in zface]
        hi = u + [q[0], q[3], q[6], q[7]]
        face = faces(0, [lane_roll(v, stride) for v in hi], hi)
        change = [c + (lane_roll(v, -stride) - v) for c, v in zip(change, face)]
        hi = u + [q[1], q[4], q[6], q[7]]
        lo = [
            jnp.where(first_row, lane_roll(v, 1 - stride), lane_roll(v, 1)) for v in hi
        ]
        face = faces(1, lo, hi)
        change = [
            c + (jnp.where(last_row, lane_roll(v, stride - 1), lane_roll(v, -1)) - v)
            for c, v in zip(change, face)
        ]
        for f in range(FIELDS):
            sink = slab_base[FIELDS] if f == FIELDS - 1 else None
            slab[f] = advance(stage, u[f], change[f], slab_base[f], sink)
        whole = comb[0:part]
        for k in range(2):
            piece = whole.astype(jnp.bfloat16).astype(jnp.float32)
            comb[k * part:(k + 1) * part] = piece
            whole = whole - piece
        comb[2 * part:3 * part] = whole
        turned = jnp.transpose(comb[...]).astype(jnp.bfloat16)
        moved = lax.dot_general(
            turned, spread, (((1,), (0,)), ((), ())), preferred_element_type=jnp.float32
        )
        for f in range(FIELDS):
            ends[f] = moved[0:size, f * lanes:(f + 1) * lanes].reshape(deep, stride, lanes)

        low = stage + 1
        high = deep - 1 - stage
        for x in range(low - 1, high + 1):
            for k, value in enumerate(primitives([src[f, x] for f in range(FIELDS)])):
                prim[k, x] = value

        def cells(x, d, src=src):
            return [src[f, x] for f in range(FIELDS)] + [
                prim[d, x], prim[3 + d, x], prim[6, x], prim[7, x]
            ]

        for x in range(low, high + 1):
            new = faces(0, cells(x - 1, 0), cells(x, 0))
            for f in range(FIELDS):
                xface[x % 2, f] = new[f]
            if x == low:
                continue
            p = x - 1
            change = [new[f] - xface[p % 2, f] for f in range(FIELDS)]
            hi = cells(p, 1)
            lo = [pltpu.roll(v, 1, axis=0) for v in hi]
            face = faces(1, lo, hi)
            change = [c + (pltpu.roll(v, stride - 1, axis=0) - v) for c, v in zip(change, face)]
            hi = cells(p, 2)
            lo = [pltpu.roll(v, 1, axis=1) for v in hi]
            face = faces(2, lo, hi)
            for f in range(FIELDS):
                end = ends[f, p]
                top = jnp.where(lane == lanes - 1, end, pltpu.roll(face[f], lanes - 1, axis=1))
                bottom = jnp.where(lane == 0, end, face[f])
                sink = block_ref[FIELDS, p] if f == FIELDS - 1 else None
                value = advance(
                    stage, src[f, p], change[f] + (top - bottom), block_ref[f, p], sink
                )
                if stage == 2:
                    out_ref[f, p - HALO] = value[0:rows]
                else:
                    now[f, p] = value


def metal_kernel(dims, rows, where, order, *refs):
    count_blk, count_sub, along, across = dims
    devices = count_blk * count_sub
    pieces = [(refs[k], start) for k, start in where]
    (
        out_ref, sol, kelvin, res, dirn, drift, image, diag, cx, cy, cz, cyu, czu, caps, heat,
        route, faced,
    ) = refs[-17:]
    lanes = out_ref.shape[-1]
    cells = along * across
    wide = count_sub * across
    deep = count_blk * along
    blk, sub = lax.axis_index("blk"), lax.axis_index("sub")
    mine = blk * along
    side = pl.multiple_of(sub * across, TILE)

    zero = jnp.zeros((wide, lanes), jnp.float32)
    for ref in (kelvin, res, cx):
        ref[0] = zero
        ref[deep + 1] = zero

    for n, ((ref, first), (flip_blk, flip_sub)) in enumerate(zip(pieces, order)):
        b = jnp.bitwise_xor(blk, flip_blk) * along
        y = pl.multiple_of(jnp.bitwise_xor(sub, flip_sub) * across, TILE)
        for field, (dest, shift) in enumerate(((kelvin, 1), (caps, 0), (cx, 1), (cy, 0), (cz, 0))):
            start = first + field * cells
            dest[pl.ds(b + shift, along), pl.ds(y, across)] = ref[
                start:start + cells
            ].reshape(along, across, lanes)
        start = first + 5 * cells
        faced[n * rows:(n + 1) * rows] = ref[start:start + rows]
        route[:, n * rows:(n + 1) * rows] = ref[start + rows:start + rows + TILE][:, 0:rows]

    walls = jnp.concatenate([kelvin[1 + b * along] for b in range(count_blk)], axis=0)
    strips = devices * across
    chosen = iota((strips, devices * rows), 0) == route[0:1].astype(jnp.int32)
    flux = film_coeff * (faced[...] - select_sum(chosen, walls, 0))
    heat[...] = select_sum(chosen, flux, 1)

    chunk = math.gcd(deep, max(1, ROWS // wide))
    none = jnp.zeros((TILE, lanes), jnp.float32)

    def sweep(body, init):
        return lax.fori_loop(0, deep // chunk, lambda i, c: body(i * chunk, c), init)

    def fold(value):
        return jnp.sum(value.reshape(-1, TILE, lanes), axis=0)

    def total(value):
        one = jnp.sum(jnp.sum(value, axis=0, keepdims=True), axis=1, keepdims=True)
        return jnp.broadcast_to(one, (TILE, lanes))

    def times(factor, value):
        return (factor * value.reshape(-1, TILE, lanes)).reshape(value.shape)

    def turned(v, step, axis):
        return pltpu.roll(v, step % v.shape[axis], axis=axis)

    def prepare(x, carry):
        here, own = pl.ds(x, chunk), pl.ds(x + 1, chunk)
        ups = cx[pl.ds(x + 2, chunk)], turned(cy[here], -1, 1), turned(cz[here], -1, 2)
        cyu[here] = ups[1]
        czu[here] = ups[2]
        diag[here] = caps[here] + ((cx[own] + ups[0]) + (cy[here] + ups[1]) + (cz[here] + ups[2]))
        v = kelvin[own]
        res[own] = (
            cx[own] * (kelvin[pl.ds(x, chunk)] - v)
            + ups[0] * (kelvin[pl.ds(x + 2, chunk)] - v)
            + (cy[here] * (turned(v, 1, 1) - v) + ups[1] * (turned(v, -1, 1) - v))
            + (cz[here] * (turned(v, 1, 2) - v) + ups[2] * (turned(v, -1, 2) - v))
        )
        return carry

    sweep(prepare, 0)
    for b in range(count_blk):
        at = b * along + 1
        res[at] = res[at] + heat[b * wide:(b + 1) * wide]

    def apply(x, sums):
        here, own = pl.ds(x, chunk), pl.ds(x + 1, chunk)
        v = res[own]
        value = (
            diag[here] * v
            - (cx[own] * res[pl.ds(x, chunk)] + cx[pl.ds(x + 2, chunk)] * res[pl.ds(x + 2, chunk)])
            - (cy[here] * turned(v, 1, 1) + cyu[here] * turned(v, -1, 1))
            - (cz[here] * turned(v, 1, 2) + czu[here] * turned(v, -1, 2))
        )
        image[here] = value
        return sums[0] + fold(v * v), sums[1] + fold(v * value)

    mine_at = pl.ds(mine, along), pl.ds(side, across)
    sol[...] = kelvin[pl.ds(mine + 1, along), pl.ds(side, across)]
    norm = alpha = beta = None
    for step in range(ITERS):
        fresh, product = (total(v) for v in sweep(apply, (none, none)))
        if step == 0:
            alpha = fresh / product
        else:
            beta = fresh / norm
            alpha = fresh / (product - beta * fresh / alpha)
        norm = fresh
        if step + 1 == ITERS:
            towards = res[pl.ds(mine + 1, along), pl.ds(side, across)] + times(beta, dirn[mine_at])
            out_ref[...] = sol[...] + times(alpha, towards)
            break

        def update(x, carry, step=step, alpha=alpha, beta=beta):
            here, own = pl.ds(x, chunk), pl.ds(x + 1, chunk)
            towards, moved = res[own], image[here]
            if step:
                towards = towards + times(beta, dirn[here])
                moved = moved + times(beta, drift[here])
            dirn[here] = towards
            drift[here] = moved
            res[own] = res[own] - times(alpha, moved)
            return carry

        sweep(update, 0)
        sol[...] = sol[...] + times(alpha, dirn[mine_at])


def swap(value, axis, flip):
    count = lax.axis_size(axis)
    return lax.ppermute(value, axis, [(i, i ^ flip) for i in range(count)])


def outer(value):
    count = lax.axis_size("blk")
    pairs = [(i, (i + 1 if i % 2 else i - 1) % count) for i in range(count)]
    return lax.ppermute(value, "blk", pairs)


def ring(value, axis, step):
    count = lax.axis_size(axis)
    return lax.ppermute(value, axis, [(i, (i + step) % count) for i in range(count)])


def flips(count):
    return [1 << k for k in reversed(range((count - 1).bit_length()))]


def shards(
    mass_per_volume,
    flow_speed_vector,
    normal_stress,
    facing_strip_index,
    solid_kelvin,
    face_coupling,
    substance_index,
    substance_storage,
):
    planes, rows, lanes = mass_per_volume.shape
    along, across, _ = solid_kelvin.shape
    count_blk, count_sub = lax.axis_size("blk"), lax.axis_size("sub")
    devices = count_blk * count_sub
    cells = along * across
    edge = up_to_tile(FIELDS * planes * HALO)
    each = across + TILE
    record = 5 * cells + rows + TILE

    face = FIELDS * HALO * rows
    state, yedge, apay, bpay, metal, wall = call(
        pack_kernel,
        [
            f32(FIELDS, planes, rows, lanes), f32(2, edge, lanes),
            f32(face + record, lanes), f32(face + record, lanes),
            f32(record, lanes), f32(each, lanes),
        ],
        [
            mass_per_volume, flow_speed_vector, normal_stress,
            facing_strip_index.reshape(1, rows), solid_kelvin.reshape(cells, lanes),
            face_coupling.reshape(6 * cells, lanes), substance_index.reshape(cells, lanes),
            substance_storage,
        ],
        hbm=tuple(range(8)),
        scratch=[
            (planes, rows, lanes), (3, planes, rows, lanes), (planes, rows, lanes),
            pltpu.VMEM((1, rows), jnp.int32), pltpu.VMEM((cells, lanes), jnp.int32),
            pltpu.SMEM(substance_storage.shape, jnp.float32), pltpu.SemaphoreType.DMA((8,)),
        ],
    )
    paired = count_blk == 4 and count_sub == 2
    span = up_to_tile(FIELDS * HALO * HALO)
    bpay = outer(bpay)
    if paired:
        wall_a = swap(wall, "blk", 1)
        ypay = jnp.concatenate([yedge.reshape(2 * edge, lanes), wall, wall_a], axis=0)
        yrecv = swap(ypay, "sub", 1)
        ylo, yhi, lo_at, hi_at = yrecv, yrecv, edge, 0
        parts = [wall, wall_a, yrecv]
        starts = [(0, each), (0, each), (2 * edge, 2 * each)]
    else:
        ylo, yhi, lo_at, hi_at = ring(yedge[1], "sub", 1), ring(yedge[0], "sub", -1), 0, 0
        parts, starts = [], []
    apay = swap(apay, "blk", 1)
    aedge, bedge = call(
        functools.partial(edge_kernel, planes, lo_at, hi_at, starts),
        [f32(2 * span, lanes), f32(2 * span + sum(c for _, c in starts), lanes)],
        [ylo, yhi, *parts],
    )
    bedge = outer(bedge)
    aedge = swap(aedge, "blk", 1)
    if paired:
        walls = [wall, wall_a, yrecv, yrecv] + 4 * [bedge]
        wall_at = [(0, 0, 0), (0, 1, 0), (2 * edge, 0, 1), (2 * edge + each, 1, 1)]
        wall_at += [(2 * span + k * each, 3 ^ (k & 1), k >> 1) for k in range(4)]
    else:
        walls = [lax.all_gather(wall, ("blk", "sub"), axis=0, tiled=True)]
        wall_at = None
    deep, stride = planes + 2 * HALO, rows + TILE
    ends_rows = up_to_tile((FIELDS + 1) * HALO)
    wide_lanes = -(-deep * stride // lanes) * lanes
    block, zlo, zhi = call(
        functools.partial(
            assemble_kernel, ((count_blk, count_sub), across), lo_at, hi_at, wall_at
        ),
        [
            f32(FIELDS + 1, deep, stride, lanes),
            f32(ends_rows, wide_lanes),
            f32(ends_rows, wide_lanes),
        ],
        [state, apay, bpay, ylo, yhi, aedge, bedge, *walls],
        scratch=[(devices * each, lanes), (stride, lanes)],
    )
    zbelow = ring(zhi, "grp", 1)
    zabove = ring(zlo, "grp", -1)

    if paired:
        far = bpay[face:]
        near_y = swap(metal, "sub", 1)
        far_y = swap(far, "sub", 1)
        mates = swap(jnp.concatenate([far, near_y], axis=0), "blk", 1)
        mate_far_y = swap(far_y, "blk", 1)
        pieces = [metal, apay, bpay, near_y, far_y, mates, mate_far_y]
        where = [(0, 0), (1, face), (2, face), (3, 0), (4, 0), (5, 0), (5, record), (6, 0)]
        order = [(0, 0), (1, 0), (3, 0), (0, 1), (3, 1), (2, 0), (1, 1), (2, 1)]
    else:
        held, order = metal, [(0, 0)]
        steps = [("blk", flip) for flip in flips(count_blk)]
        steps += [("sub", flip) for flip in flips(count_sub)]
        for axis, flip in steps:
            held = jnp.concatenate([held, swap(held, axis, flip)], axis=0)
            order = order + [
                (b ^ flip, s) if axis == "blk" else (b, s ^ flip) for b, s in order
            ]
        pieces, where = [held], [(0, k * record) for k in range(devices)]
    wide = count_sub * across
    deep_metal = count_blk * along
    field = (deep_metal, wide, lanes)
    padded = (deep_metal + 2, wide, lanes)
    metal_next = call(
        functools.partial(
            metal_kernel, (count_blk, count_sub, along, across), rows, where, order
        ),
        f32(along, across, lanes),
        pieces,
        scratch=[
            (along, across, lanes), padded, padded, field, field, field, field, padded, field,
            field, field, field, field, (devices * across, lanes), (TILE, devices * rows), (devices * rows, lanes),
        ],
    )
    fluid_next = call(
        fluid_kernel,
        f32(FIELDS, planes, rows, lanes),
        [block, zabove, zbelow, zlo, zhi],
        scratch=[
            (FIELDS, deep, stride, lanes), (8, deep, stride, lanes), (2, FIELDS, stride, lanes),
            (FIELDS, deep, stride, lanes), (FIELDS + 1, 2 * TILE, wide_lanes),
            (FIELDS, 2 * TILE, wide_lanes), (lanes, wide_lanes),
        ],
    )
    return (fluid_next, metal_next)


def solution(mesh):
    in_specs = (
        P("blk", "sub", "grp"),
        P(None, "blk", "sub", "grp"),
        P("blk", "sub", "grp"),
        P("grp", "blk", "sub"),
        P("blk", "sub", "grp"),
        P(None, "blk", "sub", "grp"),
        P("blk", "sub", "grp"),
        P(),
    )
    out_specs = (P(None, "blk", "sub", "grp"), P("blk", "sub", "grp"))
    return jax.shard_map(shards, mesh=mesh, in_specs=in_specs, out_specs=out_specs, check_vma=False)
```

```python
import functools
import math

import jax
import jax.numpy as jnp
from jax import lax
from jax.experimental import pallas as pl
from jax.experimental.pallas import tpu as pltpu
from jax.sharding import PartitionSpec as P


ITERS = 4
HALO = 3
TILE = 8
FIELDS = 5
ROWS = 512

gamma_gas = 1.4
time_step = 0.1
viscosity = 0.05
film_coeff = 1.0
third_part = 1.0 / 3.0
two_thirds = 2.0 / 3.0

HIGHEST = lax.Precision.HIGHEST
SPARE_BYTES = 6 * 1024 * 1024


def bytes_of(shapes):
    total = 0
    for shape in shapes:
        *lead, rows, lanes = (1, 1, *shape)
        total += 4 * math.prod(lead) * up_to_tile(rows) * (-(-lanes // 128) * 128)
    return total


def call(body, out, inputs, hbm=(), cost=100_000, scratch=()):
    inputs = [
        pltpu.with_memory_space_constraint(x, pltpu.HBM) if i in hbm else x
        for i, x in enumerate(inputs)
    ]
    limit = SPARE_BYTES + bytes_of(
        [x.shape for i, x in enumerate(inputs) if i not in hbm]
        + [x.shape for x in jax.tree.leaves(out)]
        + [x for x in scratch if isinstance(x, tuple)]
    )
    return pl.pallas_call(
        body,
        out_shape=out,
        in_specs=[
            pl.BlockSpec(memory_space=pltpu.HBM if i in hbm else pltpu.VMEM)
            for i in range(len(inputs))
        ],
        out_specs=jax.tree.map(lambda _: pl.BlockSpec(memory_space=pltpu.VMEM), out),
        scratch_shapes=[
            pltpu.VMEM(x, jnp.float32) if isinstance(x, tuple) else x for x in scratch
        ],
        cost_estimate=pl.CostEstimate(flops=cost, bytes_accessed=cost, transcendentals=0),
        compiler_params=pltpu.CompilerParams(vmem_limit_bytes=limit),
    )(*inputs)


def f32(*shape):
    return jax.ShapeDtypeStruct(shape, jnp.float32)


def up_to_tile(count):
    return -(-count // TILE) * TILE


def iota(shape, dim):
    return lax.broadcasted_iota(jnp.int32, shape, dim)


def dot(a, b, a_dim, b_dim):
    return lax.dot_general(
        a, b, (((a_dim,), (b_dim,)), ((), ())), precision=HIGHEST,
        preferred_element_type=jnp.float32,
    )


def pieces_of(value):
    out = []
    for _ in range(2):
        piece = value.astype(jnp.bfloat16)
        out.append(piece)
        value = value - piece.astype(jnp.float32)
    return out + [value.astype(jnp.bfloat16)]


def select_sum(chosen, value, dim):
    flags = chosen.astype(jnp.float32).astype(jnp.bfloat16)
    return sum(
        lax.dot_general(
            flags, piece, (((dim,), (0,)), ((), ())), preferred_element_type=jnp.float32
        )
        for piece in reversed(pieces_of(value))
    )


def parity(axis="blk"):
    return lax.rem(lax.axis_index(axis), 2)


def pack_kernel(
    rho_hbm, vel_hbm, pre_hbm, route_hbm, kelvin_hbm, couple_hbm, kind_hbm, store_hbm,
    state_ref, yedge_ref, apay_ref, bpay_ref, metal_ref, wall_ref,
    rho_ref, vel_ref, pre_ref, route_ref, kind_ref, store_ref, arrived,
):
    planes, rows, lanes = rho_ref.shape
    cells = kind_ref.shape[0]
    across = wall_ref.shape[0] - TILE
    face = FIELDS * HALO * rows
    copies = [
        pltpu.make_async_copy(src, dst, arrived.at[k])
        for k, (src, dst) in enumerate((
            (rho_hbm, rho_ref), (vel_hbm, vel_ref), (pre_hbm, pre_ref),
            (kelvin_hbm, metal_ref.at[0:cells]),
            (couple_hbm.at[0:3 * cells], metal_ref.at[2 * cells:5 * cells]),
            (kind_hbm, kind_ref), (store_hbm, store_ref), (route_hbm, route_ref),
        ))
    ]
    for copy in copies:
        copy.start()
    for copy in copies[:3]:
        copy.wait()
    for x in range(planes):
        rho = rho_ref[x]
        vel = [vel_ref[d, x] for d in range(3)]
        mom = [rho * v for v in vel]
        kinetic = mom[0] * vel[0] + mom[1] * vel[1] + mom[2] * vel[2]
        energy = pre_ref[x] / (gamma_gas - 1.0) + 0.5 * kinetic
        for f, value in enumerate([rho, *mom, energy]):
            state_ref[f, x] = value
    used = FIELDS * planes * HALO
    for f in range(FIELDS):
        for x in range(planes):
            at = (f * planes + x) * HALO
            yedge_ref[0, at:at + HALO] = state_ref[f, x, 0:HALO]
            yedge_ref[1, at:at + HALO] = state_ref[f, x, rows - HALO:rows]
    if yedge_ref.shape[1] > used:
        for side in range(2):
            yedge_ref[side, used:] = jnp.zeros(
                (yedge_ref.shape[1] - used, lanes), jnp.float32
            )
    for odd in range(2):

        @pl.when(parity() == odd)
        def _():
            for f in range(FIELDS):
                for j in range(HALO):
                    at = (f * HALO + j) * rows
                    apay_ref[at:at + rows] = state_ref[f, j + (planes - HALO) * (1 - odd)]
                    bpay_ref[at:at + rows] = state_ref[f, j + (planes - HALO) * odd]

    for copy in copies[3:]:
        copy.wait()
    wall_ref[0:across] = metal_ref[0:across]
    wall_ref[across:across + TILE] = jnp.zeros((TILE, lanes), jnp.float32)
    wall_ref[across:across + 1, 0:rows] = route_ref[...].astype(jnp.float32)
    kind = kind_ref[...]
    capacity = jnp.zeros((cells, lanes), jnp.float32)
    for m in range(store_ref.shape[0]):
        capacity = jnp.where(kind == m, store_ref[m], capacity)
    metal_ref[cells:2 * cells] = capacity
    metal_ref[5 * cells:5 * cells + rows] = pre_ref[0] / rho_ref[0]
    metal_ref[5 * cells + rows:5 * cells + rows + TILE] = wall_ref[across:across + TILE]
    record = 5 * cells + rows + TILE
    apay_ref[face:face + record] = metal_ref[...]


def edge_kernel(planes, lo_at, hi_at, starts, *refs):
    ylo_ref, yhi_ref = refs[0], refs[1]
    parts, (aedge_ref, bedge_ref) = refs[2:-2], refs[-2:]
    used = FIELDS * HALO * HALO
    span = up_to_tile(used)
    for odd in range(2):

        @pl.when(parity() == odd)
        def _():
            for out, first in (
                (aedge_ref, (planes - HALO) * (1 - odd)),
                (bedge_ref, (planes - HALO) * odd),
            ):
                for f in range(FIELDS):
                    for side, (ref, base) in enumerate(((ylo_ref, lo_at), (yhi_ref, hi_at))):
                        at = side * span + f * HALO * HALO
                        src = base + (f * planes + first) * HALO
                        out[at:at + HALO * HALO] = ref[src:src + HALO * HALO]

    for out in (aedge_ref, bedge_ref):
        for side in range(2):
            if span > used:
                out[side * span + used:(side + 1) * span] = jnp.zeros(
                    (span - used, ylo_ref.shape[1]), jnp.float32
                )
    at = 2 * span
    for ref, (start, count) in zip(parts, starts):
        bedge_ref[at:at + count] = ref[start:start + count]
        at += count


def assemble_kernel(dims, lo_at, hi_at, wall_at, *refs):
    axes, across = dims
    count_blk, count_sub = axes
    state_ref, aface_ref, bface_ref, ylo_ref, yhi_ref, aedge_ref, bedge_ref = refs[:7]
    wall_refs = refs[7:-5]
    block_ref, inner_ref, outer_ref, table, seen = refs[-5:]
    _, planes, rows, lanes = state_ref.shape
    deep, stride = block_ref.shape[1:3]
    span = up_to_tile(FIELDS * HALO * HALO)
    each = across + TILE
    blk, sub = lax.axis_index("blk"), lax.axis_index("sub")

    def place(f, x, own, lo, hi):
        block_ref[f, x + HALO, 0:rows] = own
        block_ref[f, x + HALO, rows:rows + HALO] = hi
        block_ref[f, x + HALO, stride - HALO:stride] = lo

    for f in range(FIELDS):
        for x in range(planes):
            at = (f * planes + x) * HALO
            place(
                f, x, state_ref[f, x],
                ylo_ref[lo_at + at:lo_at + at + HALO], yhi_ref[hi_at + at:hi_at + at + HALO],
            )
    for odd in range(2):

        @pl.when(parity() == odd)
        def _():
            for face_ref, edge_ref, above in (
                (aface_ref, aedge_ref, odd == 0), (bface_ref, bedge_ref, odd == 1),
            ):
                for f in range(FIELDS):
                    for j in range(HALO):
                        at = (f * HALO + j) * HALO
                        place(
                            f, planes + j if above else j - HALO,
                            face_ref[(f * HALO + j) * rows:(f * HALO + j + 1) * rows],
                            edge_ref[at:at + HALO], edge_ref[span + at:span + at + HALO],
                        )

    if wall_at is None:
        table = wall_refs[0]
    else:
        for ref, (start, flip_blk, flip_sub) in zip(wall_refs, wall_at):
            device = jnp.bitwise_xor(blk, flip_blk) * count_sub + jnp.bitwise_xor(sub, flip_sub)
            table[pl.ds(pl.multiple_of(device * each, TILE), each)] = ref[start:start + each]
    devices = count_blk * count_sub
    walls = jnp.concatenate(
        [table[d * each:d * each + across] for d in range(devices)], axis=0
    )

    def facing(blk_at, sub_at):
        device = lax.rem(blk_at, count_blk) * count_sub + lax.rem(sub_at, count_sub)
        at = pl.multiple_of(device * each + across, TILE)
        routes = table[pl.ds(at, TILE)][0:1, 0:rows].astype(jnp.int32)
        return select_sum(iota((devices * across, rows), 0) == routes, walls, 0)

    block_ref[FIELDS] = jnp.zeros(block_ref.shape[1:], jnp.float32)
    for x, blk_at in ((0, blk), (planes, blk + 1)):
        below = facing(blk_at, sub + count_sub - 1)
        above = below if count_sub == 2 else facing(blk_at, sub + 1)
        seen[0:rows] = facing(blk_at, sub)
        seen[rows:] = jnp.zeros((stride - rows, lanes), jnp.float32)
        seen[rows:rows + HALO] = above[0:HALO]
        seen[stride - HALO:stride] = below[rows - HALO:rows]
        rho, mx, my, mz, energy = [block_ref[f, x + HALO] for f in range(FIELDS)]
        pressure = (gamma_gas - 1.0) * (energy - 0.5 * (mx * mx + my * my + mz * mz) / rho)
        block_ref[FIELDS, x + HALO] = film_coeff * (pressure / rho - seen[...])
    pick = iota((TILE, lanes), 0)
    cell = iota((TILE, lanes), 1)
    chosen = (
        ((pick == cell) & (pick < HALO))
        | ((pick - HALO + lanes - HALO == cell) & (pick >= HALO) & (pick < 2 * HALO))
    ).astype(jnp.float32)
    size = deep * stride
    upper = parity("grp") == 1
    for f in range(FIELDS + 1):
        ends = dot(chosen, block_ref[f].reshape(size, lanes), 1, 1)
        low, high = ends[0:HALO], ends[HALO:2 * HALO]
        inner_ref[f * HALO:(f + 1) * HALO, 0:size] = jnp.where(upper, low, high)
        outer_ref[f * HALO:(f + 1) * HALO, 0:size] = jnp.where(upper, high, low)
    used = (FIELDS + 1) * HALO
    for ref in (inner_ref, outer_ref):
        if ref.shape[1] > size:
            ref[:, size:] = jnp.zeros((ref.shape[0], ref.shape[1] - size), jnp.float32)
        if ref.shape[0] > used:
            ref[used:] = jnp.zeros((ref.shape[0] - used, ref.shape[1]), jnp.float32)


def primitives(u):
    rho, mx, my, mz, energy = u
    inverse = 1.0 / rho
    ux, uy, uz = mx * inverse, my * inverse, mz * inverse
    pressure = (gamma_gas - 1.0) * (energy - 0.5 * (mx * ux + my * uy + mz * uz))
    sound = jnp.sqrt(gamma_gas * pressure * inverse)
    return [
        ux, uy, uz, jnp.abs(ux) + sound, jnp.abs(uy) + sound, jnp.abs(uz) + sound,
        pressure, energy + pressure,
    ]


def faces(d, lo, hi):
    def flux(v):
        speed, pressure, enthalpy = v[5], v[7], v[8]
        f = [v[1 + d]] + [v[1 + i] * speed for i in range(3)] + [enthalpy * speed]
        f[1 + d] = f[1 + d] + pressure
        return f

    below, here = flux(lo), flux(hi)
    fast = jnp.maximum(lo[6], hi[6])
    slow = fast + 2.0 * viscosity
    return [
        (below[i] + here[i]) - (fast if i == 0 else slow) * (hi[i] - lo[i]) for i in range(5)
    ]


def advance(stage, old, change, start, sink):
    fresh = old - (0.5 * time_step) * change
    if sink is not None:
        fresh = fresh - time_step * sink
    if stage == 0:
        return fresh
    if stage == 1:
        return 0.75 * start + 0.25 * fresh
    return third_part * start + two_thirds * fresh


def plane_stage(stage, src, block_ref, ends, put, prim, xface):
    deep, stride, lanes = src.shape[1:]
    lane = iota((stride, lanes), 1)
    low, high = stage + 1, deep - 1 - stage
    for x in range(low - 1, high + 1):
        for k, value in enumerate(primitives([src[f, x] for f in range(FIELDS)])):
            prim[k, x] = value

    def cells(x, d):
        return [src[f, x] for f in range(FIELDS)] + [
            prim[d, x], prim[3 + d, x], prim[6, x], prim[7, x]
        ]

    for x in range(low, high + 1):
        new = faces(0, cells(x - 1, 0), cells(x, 0))
        for f in range(FIELDS):
            xface[x % 2, f] = new[f]
        if x == low:
            continue
        p = x - 1
        change = [new[f] - xface[p % 2, f] for f in range(FIELDS)]
        hi = cells(p, 1)
        lo = [pltpu.roll(v, 1, axis=0) for v in hi]
        face = faces(1, lo, hi)
        change = [c + (pltpu.roll(v, stride - 1, axis=0) - v) for c, v in zip(change, face)]
        hi = cells(p, 2)
        lo = [pltpu.roll(v, 1, axis=1) for v in hi]
        face = [jnp.where(lane == 0, 0.0, v) for v in faces(2, lo, hi)]
        for f in range(FIELDS):
            total = change[f] + (pltpu.roll(face[f], lanes - 1, axis=1) - face[f])
            if ends is not None:
                total = total + ends[f, p]
            sink = block_ref[FIELDS, p] if f == FIELDS - 1 else None
            put(f, p, advance(stage, src[f, p], total, block_ref[f, p], sink))


def begin_kernel(block_ref, now_ref, prim, xface):
    def put(f, p, value):
        now_ref[f, p] = value

    plane_stage(0, block_ref, block_ref, None, put, prim, xface)


def fluid_kernel(
    block_ref, now, inner_own, outer_own, inner_ref, outer_ref, out_ref,
    prim, xface, ends, slab_base, slab, comb,
):
    _, _, rows, lanes = out_ref.shape
    deep, stride = block_ref.shape[1:3]
    size = deep * stride
    wide = slab.shape[2]
    group = TILE
    part = FIELDS * TILE
    source = iota((lanes, FIELDS * lanes), 0)
    target = iota((lanes, FIELDS * lanes), 1)
    field = lax.rem(source, part) // TILE
    end = lax.rem(source, TILE)
    at_low = (end == 0) & (target == field * lanes) & (source < 3 * part)
    at_high = (end == 1) & (target == field * lanes + lanes - 1) & (source < 3 * part)
    spread = (at_high.astype(jnp.float32) - at_low.astype(jnp.float32)).astype(jnp.bfloat16)
    comb[...] = jnp.zeros(comb.shape, jnp.float32)
    slab_base[...] = jnp.zeros(slab_base.shape, jnp.float32)
    upper = parity("grp") == 1
    for f in range(FIELDS + 1):
        at = slice(f * HALO, (f + 1) * HALO)
        inner_z, outer_z, inner, outer = (
            ref[at] for ref in (inner_own, outer_own, inner_ref, outer_ref)
        )
        slab_base[f, 0:HALO] = jnp.where(upper, inner, outer)
        slab_base[f, HALO:2 * HALO] = jnp.where(upper, inner_z, outer_z)
        slab_base[f, group:group + HALO] = jnp.where(upper, outer_z, inner_z)
        slab_base[f, group + HALO:group + 2 * HALO] = jnp.where(upper, outer, inner)
    for f in range(FIELDS):
        slab[f] = slab_base[f]

    first_row = lax.rem(iota((2 * TILE, wide), 1), stride) == 0
    last_row = lax.rem(iota((2 * TILE, wide), 1), stride) == stride - 1

    def lane_roll(v, shift):
        return pltpu.roll(v, shift % wide, axis=1)

    def put(f, p, value):
        if stage == 2:
            out_ref[f, p - HALO] = value[0:rows]
        else:
            now[f, p] = value

    for stage in range(3):
        u = [slab[f] for f in range(FIELDS)]
        q = primitives(u)
        hi = u + [q[2], q[5], q[6], q[7]]
        lo = [pltpu.roll(v, 1, axis=0) for v in hi]
        zface = faces(2, lo, hi)
        for f in range(FIELDS):
            comb[f * TILE:f * TILE + 1] = zface[f][HALO:HALO + 1]
            comb[f * TILE + 1:f * TILE + 2] = zface[f][group + HALO:group + HALO + 1]
        change = [pltpu.roll(v, 2 * TILE - 1, axis=0) - v for v in zface]
        hi = u + [q[0], q[3], q[6], q[7]]
        face = faces(0, [lane_roll(v, stride) for v in hi], hi)
        change = [c + (lane_roll(v, -stride) - v) for c, v in zip(change, face)]
        hi = u + [q[1], q[4], q[6], q[7]]
        lo = [
            jnp.where(first_row, lane_roll(v, 1 - stride), lane_roll(v, 1)) for v in hi
        ]
        face = faces(1, lo, hi)
        change = [
            c + (jnp.where(last_row, lane_roll(v, stride - 1), lane_roll(v, -1)) - v)
            for c, v in zip(change, face)
        ]
        for f in range(FIELDS):
            sink = slab_base[FIELDS] if f == FIELDS - 1 else None
            slab[f] = advance(stage, u[f], change[f], slab_base[f], sink)
        whole = comb[0:part]
        for k in range(2):
            piece = whole.astype(jnp.bfloat16).astype(jnp.float32)
            comb[k * part:(k + 1) * part] = piece
            whole = whole - piece
        comb[2 * part:3 * part] = whole
        turned = jnp.transpose(comb[...]).astype(jnp.bfloat16)
        moved = lax.dot_general(
            turned, spread, (((1,), (0,)), ((), ())), preferred_element_type=jnp.float32
        )
        for f in range(FIELDS):
            ends[f] = moved[0:size, f * lanes:(f + 1) * lanes].reshape(deep, stride, lanes)

        if stage == 0:
            for p in range(1, deep - 1):
                for f in range(FIELDS):
                    now[f, p] = now[f, p] - (0.5 * time_step) * ends[f, p]
        else:
            plane_stage(stage, now, block_ref, ends, put, prim, xface)


def metal_kernel(dims, rows, where, order, *refs):
    count_blk, count_sub, along, across = dims
    devices = count_blk * count_sub
    pieces = [(refs[k], start) for k, start in where]
    (
        out_ref, sol, kelvin, res, dirn, drift, image, diag, cx, cy, cz, cyu, czu, caps, heat,
        route, faced,
    ) = refs[-17:]
    lanes = out_ref.shape[-1]
    cells = along * across
    wide = count_sub * across
    deep = count_blk * along
    blk, sub = lax.axis_index("blk"), lax.axis_index("sub")
    mine = blk * along
    side = pl.multiple_of(sub * across, TILE)

    zero = jnp.zeros((wide, lanes), jnp.float32)
    for ref in (kelvin, res, cx):
        ref[0] = zero
        ref[deep + 1] = zero

    for n, ((ref, first), (flip_blk, flip_sub)) in enumerate(zip(pieces, order)):
        b = jnp.bitwise_xor(blk, flip_blk) * along
        y = pl.multiple_of(jnp.bitwise_xor(sub, flip_sub) * across, TILE)
        for field, (dest, shift) in enumerate(((kelvin, 1), (caps, 0), (cx, 1), (cy, 0), (cz, 0))):
            start = first + field * cells
            dest[pl.ds(b + shift, along), pl.ds(y, across)] = ref[
                start:start + cells
            ].reshape(along, across, lanes)
        start = first + 5 * cells
        faced[n * rows:(n + 1) * rows] = ref[start:start + rows]
        route[:, n * rows:(n + 1) * rows] = ref[start + rows:start + rows + TILE][:, 0:rows]

    walls = jnp.concatenate([kelvin[1 + b * along] for b in range(count_blk)], axis=0)
    strips = devices * across
    chosen = iota((strips, devices * rows), 0) == route[0:1].astype(jnp.int32)
    flux = film_coeff * (faced[...] - select_sum(chosen, walls, 0))
    heat[...] = select_sum(chosen, flux, 1)

    chunk = math.gcd(deep, max(1, ROWS // wide))
    none = jnp.zeros((TILE, lanes), jnp.float32)

    def sweep(body, init):
        return lax.fori_loop(0, deep // chunk, lambda i, c: body(i * chunk, c), init)

    def fold(value):
        return jnp.sum(value.reshape(-1, TILE, lanes), axis=0)

    def total(value):
        one = jnp.sum(jnp.sum(value, axis=0, keepdims=True), axis=1, keepdims=True)
        return jnp.broadcast_to(one, (TILE, lanes))

    def times(factor, value):
        return (factor * value.reshape(-1, TILE, lanes)).reshape(value.shape)

    def turned(v, step, axis):
        return pltpu.roll(v, step % v.shape[axis], axis=axis)

    def prepare(x, carry):
        here, own = pl.ds(x, chunk), pl.ds(x + 1, chunk)
        ups = cx[pl.ds(x + 2, chunk)], turned(cy[here], -1, 1), turned(cz[here], -1, 2)
        cyu[here] = ups[1]
        czu[here] = ups[2]
        diag[here] = caps[here] + ((cx[own] + ups[0]) + (cy[here] + ups[1]) + (cz[here] + ups[2]))
        v = kelvin[own]
        res[own] = (
            cx[own] * (kelvin[pl.ds(x, chunk)] - v)
            + ups[0] * (kelvin[pl.ds(x + 2, chunk)] - v)
            + (cy[here] * (turned(v, 1, 1) - v) + ups[1] * (turned(v, -1, 1) - v))
            + (cz[here] * (turned(v, 1, 2) - v) + ups[2] * (turned(v, -1, 2) - v))
        )
        return carry

    sweep(prepare, 0)
    for b in range(count_blk):
        at = b * along + 1
        res[at] = res[at] + heat[b * wide:(b + 1) * wide]

    def apply(x, sums):
        here, own = pl.ds(x, chunk), pl.ds(x + 1, chunk)
        v = res[own]
        value = (
            diag[here] * v
            - (cx[own] * res[pl.ds(x, chunk)] + cx[pl.ds(x + 2, chunk)] * res[pl.ds(x + 2, chunk)])
            - (cy[here] * turned(v, 1, 1) + cyu[here] * turned(v, -1, 1))
            - (cz[here] * turned(v, 1, 2) + czu[here] * turned(v, -1, 2))
        )
        image[here] = value
        return sums[0] + fold(v * v), sums[1] + fold(v * value)

    mine_at = pl.ds(mine, along), pl.ds(side, across)
    sol[...] = kelvin[pl.ds(mine + 1, along), pl.ds(side, across)]
    norm = alpha = beta = None
    for step in range(ITERS):
        fresh, product = (total(v) for v in sweep(apply, (none, none)))
        if step == 0:
            alpha = fresh / product
        else:
            beta = fresh / norm
            alpha = fresh / (product - beta * fresh / alpha)
        norm = fresh
        if step + 1 == ITERS:
            towards = res[pl.ds(mine + 1, along), pl.ds(side, across)] + times(beta, dirn[mine_at])
            out_ref[...] = sol[...] + times(alpha, towards)
            break

        def update(x, carry, step=step, alpha=alpha, beta=beta):
            here, own = pl.ds(x, chunk), pl.ds(x + 1, chunk)
            towards, moved = res[own], image[here]
            if step:
                towards = towards + times(beta, dirn[here])
                moved = moved + times(beta, drift[here])
            dirn[here] = towards
            drift[here] = moved
            res[own] = res[own] - times(alpha, moved)
            return carry

        sweep(update, 0)
        sol[...] = sol[...] + times(alpha, dirn[mine_at])


def swap(value, axis, flip):
    count = lax.axis_size(axis)
    return lax.ppermute(value, axis, [(i, i ^ flip) for i in range(count)])


def outer(value, axis="blk"):
    count = lax.axis_size(axis)
    pairs = [(i, (i + 1 if i % 2 else i - 1) % count) for i in range(count)]
    return lax.ppermute(value, axis, pairs)


def ring(value, axis, step):
    count = lax.axis_size(axis)
    return lax.ppermute(value, axis, [(i, (i + step) % count) for i in range(count)])


def flips(count):
    return [1 << k for k in reversed(range((count - 1).bit_length()))]


def shards(
    mass_per_volume,
    flow_speed_vector,
    normal_stress,
    facing_strip_index,
    solid_kelvin,
    face_coupling,
    substance_index,
    substance_storage,
):
    planes, rows, lanes = mass_per_volume.shape
    along, across, _ = solid_kelvin.shape
    count_blk, count_sub = lax.axis_size("blk"), lax.axis_size("sub")
    devices = count_blk * count_sub
    cells = along * across
    edge = up_to_tile(FIELDS * planes * HALO)
    each = across + TILE
    record = 5 * cells + rows + TILE

    face = FIELDS * HALO * rows
    state, yedge, apay, bpay, metal, wall = call(
        pack_kernel,
        [
            f32(FIELDS, planes, rows, lanes), f32(2, edge, lanes),
            f32(face + record, lanes), f32(face, lanes),
            f32(record, lanes), f32(each, lanes),
        ],
        [
            mass_per_volume, flow_speed_vector, normal_stress,
            facing_strip_index.reshape(1, rows), solid_kelvin.reshape(cells, lanes),
            face_coupling.reshape(6 * cells, lanes), substance_index.reshape(cells, lanes),
            substance_storage,
        ],
        hbm=tuple(range(8)),
        scratch=[
            (planes, rows, lanes), (3, planes, rows, lanes), (planes, rows, lanes),
            pltpu.VMEM((1, rows), jnp.int32), pltpu.VMEM((cells, lanes), jnp.int32),
            pltpu.SMEM(substance_storage.shape, jnp.float32), pltpu.SemaphoreType.DMA((8,)),
        ],
    )
    paired = count_blk == 4 and count_sub == 2
    span = up_to_tile(FIELDS * HALO * HALO)
    bpay = outer(bpay)
    if paired:
        wall_a = swap(wall, "blk", 1)
        ypay = jnp.concatenate([yedge.reshape(2 * edge, lanes), wall, wall_a], axis=0)
        yrecv = swap(ypay, "sub", 1)
        ylo, yhi, lo_at, hi_at = yrecv, yrecv, edge, 0
        parts = [wall, wall_a, yrecv]
        starts = [(0, each), (0, each), (2 * edge, 2 * each)]
    else:
        ylo, yhi, lo_at, hi_at = ring(yedge[1], "sub", 1), ring(yedge[0], "sub", -1), 0, 0
        parts, starts = [], []
    apay = swap(apay, "blk", 1)
    aedge, bedge = call(
        functools.partial(edge_kernel, planes, lo_at, hi_at, starts),
        [f32(2 * span, lanes), f32(2 * span + sum(c for _, c in starts), lanes)],
        [ylo, yhi, *parts],
    )
    bedge = outer(bedge)
    aedge = swap(aedge, "blk", 1)
    if paired:
        walls = [wall, wall_a, yrecv, yrecv] + 4 * [bedge]
        wall_at = [(0, 0, 0), (0, 1, 0), (2 * edge, 0, 1), (2 * edge + each, 1, 1)]
        wall_at += [(2 * span + k * each, 3 ^ (k & 1), k >> 1) for k in range(4)]
    else:
        walls = [lax.all_gather(wall, ("blk", "sub"), axis=0, tiled=True)]
        wall_at = None
    deep, stride = planes + 2 * HALO, rows + TILE
    ends_rows = up_to_tile((FIELDS + 1) * HALO)
    wide_lanes = -(-deep * stride // lanes) * lanes
    block, inner_z, outer_z = call(
        functools.partial(
            assemble_kernel, ((count_blk, count_sub), across), lo_at, hi_at, wall_at
        ),
        [
            f32(FIELDS + 1, deep, stride, lanes),
            f32(ends_rows, wide_lanes),
            f32(ends_rows, wide_lanes),
        ],
        [state, apay, bpay, ylo, yhi, aedge, bedge, *walls],
        scratch=[(devices * each, lanes), (stride, lanes)],
    )
    inner_got = swap(inner_z, "grp", 1)
    outer_got = outer(outer_z, "grp")
    whole = (FIELDS, deep, stride, lanes)
    work = [(8, deep, stride, lanes), (2, FIELDS, stride, lanes)]
    first = call(begin_kernel, f32(*whole), [block], scratch=work)

    if paired:
        near_y = swap(metal, "sub", 1)
        far = swap(metal, "blk", 2)
        pairs = [
            (b * count_sub + s, (b ^ 2) * count_sub + (s ^ 1))
            for b in range(count_blk) for s in range(count_sub)
        ]
        far_y = lax.ppermute(metal, ("blk", "sub"), pairs)
        mates = swap(jnp.concatenate([near_y, far_y, far], axis=0), "blk", 1)
        pieces = [metal, apay, far, near_y, far_y, mates]
        where = [(0, 0), (1, face), (2, 0), (3, 0), (4, 0)] + [(5, k * record) for k in range(3)]
        order = [(0, 0), (1, 0), (2, 0), (0, 1), (2, 1), (1, 1), (3, 1), (3, 0)]
    else:
        held, order = metal, [(0, 0)]
        steps = [("blk", flip) for flip in flips(count_blk)]
        steps += [("sub", flip) for flip in flips(count_sub)]
        for axis, flip in steps:
            held = jnp.concatenate([held, swap(held, axis, flip)], axis=0)
            order = order + [
                (b ^ flip, s) if axis == "blk" else (b, s ^ flip) for b, s in order
            ]
        pieces, where = [held], [(0, k * record) for k in range(devices)]
    wide = count_sub * across
    deep_metal = count_blk * along
    field = (deep_metal, wide, lanes)
    padded = (deep_metal + 2, wide, lanes)
    metal_next = call(
        functools.partial(
            metal_kernel, (count_blk, count_sub, along, across), rows, where, order
        ),
        f32(along, across, lanes),
        pieces,
        scratch=[
            (along, across, lanes), padded, padded, field, field, field, field, padded, field,
            field, field, field, field, (devices * across, lanes), (TILE, devices * rows), (devices * rows, lanes),
        ],
    )
    fluid_next = call(
        fluid_kernel,
        f32(FIELDS, planes, rows, lanes),
        [block, first, inner_z, outer_z, inner_got, outer_got],
        scratch=[
            *work, whole, (FIELDS + 1, 2 * TILE, wide_lanes), (FIELDS, 2 * TILE, wide_lanes),
            (lanes, wide_lanes),
        ],
    )
    return (fluid_next, metal_next)


def solution(mesh):
    in_specs = (
        P("blk", "sub", "grp"),
        P(None, "blk", "sub", "grp"),
        P("blk", "sub", "grp"),
        P("grp", "blk", "sub"),
        P("blk", "sub", "grp"),
        P(None, "blk", "sub", "grp"),
        P("blk", "sub", "grp"),
        P(),
    )
    out_specs = (P(None, "blk", "sub", "grp"), P("blk", "sub", "grp"))
    return jax.shard_map(shards, mesh=mesh, in_specs=in_specs, out_specs=out_specs, check_vma=False)
```

```python
import functools
import math

import jax
import jax.numpy as jnp
from jax import lax
from jax.experimental import pallas as pl
from jax.experimental.pallas import tpu as pltpu
from jax.sharding import PartitionSpec as P


ITERS = 4
HALO = 3
TILE = 8
FIELDS = 5
NEAR = 2 * HALO
ROWS = 512

gamma_gas = 1.4
time_step = 0.1
viscosity = 0.05
film_coeff = 1.0
third_part = 1.0 / 3.0
two_thirds = 2.0 / 3.0

SPARE_BYTES = 6 * 1024 * 1024


def bytes_of(shapes):
    total = 0
    for shape in shapes:
        *lead, rows, lanes = (1, 1, *shape)
        total += 4 * math.prod(lead) * up_to_tile(rows) * (-(-lanes // 128) * 128)
    return total


def call(body, out, inputs, hbm=(), cost=100_000, scratch=()):
    inputs = [
        pltpu.with_memory_space_constraint(x, pltpu.HBM) if i in hbm else x
        for i, x in enumerate(inputs)
    ]
    limit = SPARE_BYTES + bytes_of(
        [x.shape for i, x in enumerate(inputs) if i not in hbm]
        + [x.shape for x in jax.tree.leaves(out)]
        + [x for x in scratch if isinstance(x, tuple)]
    )
    return pl.pallas_call(
        body,
        out_shape=out,
        in_specs=[
            pl.BlockSpec(memory_space=pltpu.HBM if i in hbm else pltpu.VMEM)
            for i in range(len(inputs))
        ],
        out_specs=jax.tree.map(lambda _: pl.BlockSpec(memory_space=pltpu.VMEM), out),
        scratch_shapes=[
            pltpu.VMEM(x, jnp.float32) if isinstance(x, tuple) else x for x in scratch
        ],
        cost_estimate=pl.CostEstimate(flops=cost, bytes_accessed=cost, transcendentals=0),
        compiler_params=pltpu.CompilerParams(vmem_limit_bytes=limit),
    )(*inputs)


def f32(*shape):
    return jax.ShapeDtypeStruct(shape, jnp.float32)


def up_to_tile(count):
    return -(-count // TILE) * TILE


def iota(shape, dim):
    return lax.broadcasted_iota(jnp.int32, shape, dim)


def pieces_of(value):
    out = []
    for _ in range(2):
        piece = value.astype(jnp.bfloat16)
        out.append(piece)
        value = value - piece.astype(jnp.float32)
    return out + [value.astype(jnp.bfloat16)]


def select_sum(chosen, value, dim):
    flags = chosen.astype(jnp.float32).astype(jnp.bfloat16)
    return sum(
        lax.dot_general(
            flags, piece, (((dim,), (0,)), ((), ())), preferred_element_type=jnp.float32
        )
        for piece in reversed(pieces_of(value))
    )


def parity(axis="blk"):
    return lax.rem(lax.axis_index(axis), 2)


def pack_kernel(
    rho_hbm, vel_hbm, pre_hbm, route_hbm, kelvin_hbm, couple_hbm, kind_hbm, store_hbm,
    state_ref, yedge_ref, apay_ref, bpay_ref, metal_ref, wall_ref,
    rho_ref, vel_ref, pre_ref, route_ref, kind_ref, store_ref, arrived,
):
    planes, rows, lanes = rho_ref.shape
    cells = kind_ref.shape[0]
    across = wall_ref.shape[0] - 1
    face = FIELDS * HALO * rows
    copies = [
        pltpu.make_async_copy(src, dst, arrived.at[k])
        for k, (src, dst) in enumerate((
            (rho_hbm, rho_ref), (vel_hbm, vel_ref), (pre_hbm, pre_ref),
            (kelvin_hbm, metal_ref.at[0:cells]),
            (couple_hbm.at[0:3 * cells], metal_ref.at[2 * cells:5 * cells]),
            (kind_hbm, kind_ref), (store_hbm, store_ref), (route_hbm, route_ref),
        ))
    ]
    for copy in copies:
        copy.start()
    for copy in copies[:3]:
        copy.wait()
    for x in range(planes):
        rho = rho_ref[x]
        vel = [vel_ref[d, x] for d in range(3)]
        mom = [rho * v for v in vel]
        kinetic = mom[0] * vel[0] + mom[1] * vel[1] + mom[2] * vel[2]
        energy = pre_ref[x] / (gamma_gas - 1.0) + 0.5 * kinetic
        for f, value in enumerate([rho, *mom, energy]):
            state_ref[f, x] = value
    used = FIELDS * planes * HALO
    for f in range(FIELDS):
        for x in range(planes):
            at = (f * planes + x) * HALO
            yedge_ref[at:at + HALO] = state_ref[f, x, 0:HALO]
            yedge_ref[used + at:used + at + HALO] = state_ref[f, x, rows - HALO:rows]
    for odd in range(2):

        @pl.when(parity() == odd)
        def _():
            for f in range(FIELDS):
                for j in range(HALO):
                    at = (f * HALO + j) * rows
                    apay_ref[at:at + rows] = state_ref[f, j + (planes - HALO) * (1 - odd)]
                    bpay_ref[at:at + rows] = state_ref[f, j + (planes - HALO) * odd]

    for copy in copies[3:]:
        copy.wait()
    wall_ref[0:across] = metal_ref[0:across]
    wall_ref[across:across + 1] = jnp.zeros((1, lanes), jnp.float32)
    wall_ref[across:across + 1, 0:rows] = route_ref[...].astype(jnp.float32)
    kind = kind_ref[...]
    capacity = jnp.zeros((cells, lanes), jnp.float32)
    for m in range(store_ref.shape[0]):
        capacity = jnp.where(kind == m, store_ref[m], capacity)
    metal_ref[cells:2 * cells] = capacity
    metal_ref[5 * cells:5 * cells + rows] = pre_ref[0] / rho_ref[0]
    metal_ref[5 * cells + rows:5 * cells + rows + TILE] = jnp.zeros((TILE, lanes), jnp.float32)
    metal_ref[5 * cells + rows:5 * cells + rows + 1] = wall_ref[across:across + 1]
    record = 5 * cells + rows + TILE
    apay_ref[face:face + record] = metal_ref[...]


def corner_rows():
    at, out = 0, []
    for j in range(1, HALO):
        out.append((j, at, HALO - j))
        at += HALO - j
    return out, at


def edge_kernel(planes, lo_at, hi_at, starts, *refs):
    ylo_ref, yhi_ref = refs[0], refs[1]
    parts, (aedge_ref, bedge_ref) = refs[2:-2], refs[-2:]
    corners, each = corner_rows()
    for odd in range(2):

        @pl.when(parity() == odd)
        def _():
            for out, last in ((aedge_ref, odd == 0), (bedge_ref, odd == 1)):
                for f in range(FIELDS):
                    for j, first, count in corners:
                        src = (f * planes + (planes - j if last else j - 1)) * HALO
                        lo, hi = lo_at + src + HALO - count, hi_at + src
                        at = f * each + first
                        out[at:at + count] = ylo_ref[lo:lo + count]
                        at += FIELDS * each
                        out[at:at + count] = yhi_ref[hi:hi + count]

    at = 2 * FIELDS * each
    for ref, (start, count) in zip(parts, starts):
        bedge_ref[at:at + count] = ref[start:start + count]
        at += count


def assemble_kernel(dims, lo_at, hi_at, wall_at, *refs):
    axes, across = dims
    count_blk, count_sub = axes
    state_ref, apay_ref, bpay_ref, ylo_ref, yhi_ref, aedge_ref, bedge_ref = refs[:7]
    wall_refs = refs[7:-6]
    block_ref, own_ref, inner_ref, outer_ref, table, seen = refs[-6:]
    _, planes, rows, lanes = state_ref.shape
    deep, stride = block_ref.shape[1:3]
    corners, each_corner = corner_rows()
    each = across + TILE
    blk, sub = lax.axis_index("blk"), lax.axis_index("sub")

    for f in range(FIELDS):
        for x in range(planes):
            at = (f * planes + x) * HALO
            block_ref[f, x + HALO, 0:rows] = state_ref[f, x]
            block_ref[f, x + HALO, rows:rows + HALO] = yhi_ref[hi_at + at:hi_at + at + HALO]
            block_ref[f, x + HALO, stride - HALO:stride] = ylo_ref[lo_at + at:lo_at + at + HALO]
    for odd in range(2):

        @pl.when(parity() == odd)
        def _():
            for face_ref, edge_ref, above in (
                (apay_ref, aedge_ref, odd == 0), (bpay_ref, bedge_ref, odd == 1),
            ):
                for f in range(FIELDS):
                    for j in range(HALO):
                        at = (f * HALO + j) * rows
                        x = planes + HALO + j if above else j
                        block_ref[f, x, 0:rows] = face_ref[at:at + rows]
                    for j, first, count in corners:
                        at = f * each_corner + first
                        x = planes + HALO + j - 1 if above else HALO - j
                        block_ref[f, x, stride - count:stride] = edge_ref[at:at + count]
                        at += FIELDS * each_corner
                        block_ref[f, x, rows:rows + count] = edge_ref[at:at + count]

    if wall_at is None:
        table = wall_refs[0]
    else:
        for ref, (start, flip_blk, flip_sub) in zip(wall_refs, wall_at):
            device = jnp.bitwise_xor(blk, flip_blk) * count_sub + jnp.bitwise_xor(sub, flip_sub)
            table[pl.ds(pl.multiple_of(device * each, TILE), across + 1)] = ref[
                start:start + across + 1
            ]
    devices = count_blk * count_sub
    walls = jnp.concatenate(
        [table[d * each:d * each + across] for d in range(devices)], axis=0
    )

    def facing(blk_at, sub_at):
        device = lax.rem(blk_at, count_blk) * count_sub + lax.rem(sub_at, count_sub)
        at = pl.multiple_of(device * each + across, TILE)
        routes = table[pl.ds(at, TILE)][0:1, 0:rows].astype(jnp.int32)
        return select_sum(iota((devices * across, rows), 0) == routes, walls, 0)

    block_ref[FIELDS] = jnp.zeros(block_ref.shape[1:], jnp.float32)
    for x, blk_at in ((0, blk), (planes, blk + 1)):
        below = facing(blk_at, sub + count_sub - 1)
        above = below if count_sub == 2 else facing(blk_at, sub + 1)
        seen[0:rows] = facing(blk_at, sub)
        seen[rows:] = jnp.zeros((stride - rows, lanes), jnp.float32)
        seen[rows:rows + HALO] = above[0:HALO]
        seen[stride - HALO:stride] = below[rows - HALO:rows]
        rho, mx, my, mz, energy = [block_ref[f, x + HALO] for f in range(FIELDS)]
        pressure = (gamma_gas - 1.0) * (energy - 0.5 * (mx * mx + my * my + mz * mz) / rho)
        block_ref[FIELDS, x + HALO] = film_coeff * (pressure / rho - seen[...])
    pick = iota((2 * TILE, lanes), 0)
    cell = iota((2 * TILE, lanes), 1)
    chosen = (
        ((pick == cell) & (pick < NEAR))
        | ((pick - TILE + lanes - NEAR == cell) & (pick >= TILE) & (pick < TILE + NEAR))
    ).astype(jnp.float32).astype(jnp.bfloat16)
    size = deep * stride
    upper = parity("grp") == 1
    for f in range(FIELDS + 1):
        ends = sum(
            lax.dot_general(
                chosen, piece, (((1,), (1,)), ((), ())), preferred_element_type=jnp.float32
            )
            for piece in reversed(pieces_of(block_ref[f].reshape(size, lanes)))
        )
        own_ref[f * 2 * TILE:(f + 1) * 2 * TILE, 0:size] = ends
        low, high = ends[0:HALO], ends[TILE + NEAR - HALO:TILE + NEAR]
        inner_ref[f * HALO:(f + 1) * HALO, 0:size] = jnp.where(upper, low, high)
        outer_ref[f * HALO:(f + 1) * HALO, 0:size] = jnp.where(upper, high, low)
    used = (FIELDS + 1) * HALO
    if own_ref.shape[1] > size:
        own_ref[:, size:] = jnp.zeros((own_ref.shape[0], own_ref.shape[1] - size), jnp.float32)
    for ref in (inner_ref, outer_ref):
        if ref.shape[1] > size:
            ref[:, size:] = jnp.zeros((ref.shape[0], ref.shape[1] - size), jnp.float32)
        if ref.shape[0] > used:
            ref[used:] = jnp.zeros((ref.shape[0] - used, ref.shape[1]), jnp.float32)


def primitives(u):
    rho, mx, my, mz, energy = u
    inverse = 1.0 / rho
    ux, uy, uz = mx * inverse, my * inverse, mz * inverse
    pressure = (gamma_gas - 1.0) * (energy - 0.5 * (mx * ux + my * uy + mz * uz))
    sound = jnp.sqrt(gamma_gas * pressure * inverse)
    return [
        ux, uy, uz, jnp.abs(ux) + sound, jnp.abs(uy) + sound, jnp.abs(uz) + sound,
        pressure, energy + pressure,
    ]


def faces(d, lo, hi):
    def flux(v):
        speed, pressure, enthalpy = v[5], v[7], v[8]
        f = [v[1 + d]] + [v[1 + i] * speed for i in range(3)] + [enthalpy * speed]
        f[1 + d] = f[1 + d] + pressure
        return f

    below, here = flux(lo), flux(hi)
    fast = jnp.maximum(lo[6], hi[6])
    slow = fast + 2.0 * viscosity
    return [
        (below[i] + here[i]) - (fast if i == 0 else slow) * (hi[i] - lo[i]) for i in range(5)
    ]


def advance(stage, old, change, start, sink):
    fresh = old - (0.5 * time_step) * change
    if sink is not None:
        fresh = fresh - time_step * sink
    if stage == 0:
        return fresh
    if stage == 1:
        return 0.75 * start + 0.25 * fresh
    return third_part * start + two_thirds * fresh


def planes_kernel(block_ref, out_ref, now, prim, xface):
    deep, _, _ = block_ref.shape[1:]
    rows = out_ref.shape[2]
    for stage in range(3):
        src = block_ref if stage == 0 else now
        low, high = stage + 1, deep - 1 - stage
        for x in range(low - 1, high + 1):
            for k, value in enumerate(primitives([src[f, x] for f in range(FIELDS)])):
                prim[k, x] = value

        def cells(x, d, src=src):
            return [src[f, x] for f in range(FIELDS)] + [
                prim[d, x], prim[3 + d, x], prim[6, x], prim[7, x]
            ]

        for x in range(low, high + 1):
            new = faces(0, cells(x - 1, 0), cells(x, 0))
            for f in range(FIELDS):
                xface[x % 2, f] = new[f]
            if x == low:
                continue
            p = x - 1
            change = [new[f] - xface[p % 2, f] for f in range(FIELDS)]
            for d, axis in ((1, 0), (2, 1)):
                hi = cells(p, d)
                lo = [pltpu.roll(v, 1, axis=axis) for v in hi]
                face = faces(d, lo, hi)
                last = hi[0].shape[axis] - 1
                change = [c + (pltpu.roll(v, last, axis=axis) - v) for c, v in zip(change, face)]
            for f in range(FIELDS):
                sink = block_ref[FIELDS, p] if f == FIELDS - 1 else None
                value = advance(stage, src[f, p], change[f], block_ref[f, p], sink)
                if stage == 2:
                    out_ref[f, p - HALO] = value[0:rows]
                else:
                    now[f, p] = value


def ends_kernel(
    stride, main_ref, own_ref, inner_ref, outer_ref, out_ref, slab_base, slab, comb
):
    _, planes, rows, lanes = out_ref.shape
    wide = slab.shape[2]
    half = slab.shape[1] // 2
    part = FIELDS * TILE
    source = iota((lanes, FIELDS * lanes), 0)
    target = iota((lanes, FIELDS * lanes), 1)
    field = lax.rem(source, part) // TILE
    end = lax.rem(source, TILE)
    spread = (
        ((end < HALO) & (target == field * lanes + end))
        | (
            (end >= HALO) & (end < 2 * HALO)
            & (target == field * lanes + lanes - 2 * HALO + end)
        )
    ) & (source < 3 * part)
    spread = spread.astype(jnp.float32).astype(jnp.bfloat16)
    comb[...] = jnp.zeros(comb.shape, jnp.float32)
    slab_base[...] = jnp.zeros(slab_base.shape, jnp.float32)
    upper = parity("grp") == 1
    for f in range(FIELDS + 1):
        inner, outer = (ref[f * HALO:(f + 1) * HALO] for ref in (inner_ref, outer_ref))
        at = f * 2 * TILE
        slab_base[f, 0:HALO] = jnp.where(upper, inner, outer)
        slab_base[f, HALO:HALO + NEAR] = own_ref[at:at + NEAR]
        slab_base[f, half:half + NEAR] = own_ref[at + TILE:at + TILE + NEAR]
        slab_base[f, half + NEAR:half + NEAR + HALO] = jnp.where(upper, outer, inner)

    first_row = lax.rem(iota((2 * half, wide), 1), stride) == 0
    last_row = lax.rem(iota((2 * half, wide), 1), stride) == stride - 1

    def lane_roll(v, shift):
        return pltpu.roll(v, shift % wide, axis=1)

    for stage in range(3):
        u = [(slab_base if stage == 0 else slab)[f] for f in range(FIELDS)]
        q = primitives(u)
        hi = u + [q[2], q[5], q[6], q[7]]
        face = faces(2, [pltpu.roll(v, 1, axis=0) for v in hi], hi)
        change = [pltpu.roll(v, 2 * half - 1, axis=0) - v for v in face]
        hi = u + [q[0], q[3], q[6], q[7]]
        face = faces(0, [lane_roll(v, stride) for v in hi], hi)
        change = [c + (lane_roll(v, -stride) - v) for c, v in zip(change, face)]
        hi = u + [q[1], q[4], q[6], q[7]]
        lo = [jnp.where(first_row, lane_roll(v, 1 - stride), lane_roll(v, 1)) for v in hi]
        face = faces(1, lo, hi)
        change = [
            c + (jnp.where(last_row, lane_roll(v, stride - 1), lane_roll(v, -1)) - v)
            for c, v in zip(change, face)
        ]
        for f in range(FIELDS):
            sink = slab_base[FIELDS] if f == FIELDS - 1 else None
            slab[f] = advance(stage, u[f], change[f], slab_base[f], sink)

    for f in range(FIELDS):
        comb[f * TILE:f * TILE + HALO] = slab[f, HALO:2 * HALO]
        first = half + NEAR - HALO
        comb[f * TILE + HALO:f * TILE + 2 * HALO] = slab[f, first:first + HALO]
    whole = comb[0:part]
    for k in range(2):
        piece = whole.astype(jnp.bfloat16).astype(jnp.float32)
        comb[k * part:(k + 1) * part] = piece
        whole = whole - piece
    comb[2 * part:3 * part] = whole
    turned = jnp.transpose(comb[...]).astype(jnp.bfloat16)
    moved = lax.dot_general(
        turned[HALO * stride:(HALO + planes) * stride], spread, (((1,), (0,)), ((), ())),
        preferred_element_type=jnp.float32,
    )
    lane = iota((rows, lanes), 1)
    near = (lane < HALO) | (lane >= lanes - HALO)
    for f in range(FIELDS):
        for x in range(planes):
            edge = moved[x * stride:x * stride + rows, f * lanes:(f + 1) * lanes]
            out_ref[f, x] = jnp.where(near, edge, main_ref[f, x])


def metal_kernel(dims, rows, where, order, *refs):
    count_blk, count_sub, along, across = dims
    devices = count_blk * count_sub
    pieces = [(refs[k], start) for k, start in where]
    (
        out_ref, sol, kelvin, res, dirn, drift, image, diag, cx, cy, cz, cyu, czu, caps, heat,
        route, faced,
    ) = refs[-17:]
    lanes = out_ref.shape[-1]
    cells = along * across
    wide = count_sub * across
    deep = count_blk * along
    blk, sub = lax.axis_index("blk"), lax.axis_index("sub")
    mine = blk * along
    side = pl.multiple_of(sub * across, TILE)

    zero = jnp.zeros((wide, lanes), jnp.float32)
    for ref in (kelvin, res, cx):
        ref[0] = zero
        ref[deep + 1] = zero

    for n, ((ref, first), (flip_blk, flip_sub)) in enumerate(zip(pieces, order)):
        b = jnp.bitwise_xor(blk, flip_blk) * along
        y = pl.multiple_of(jnp.bitwise_xor(sub, flip_sub) * across, TILE)
        for field, (dest, shift) in enumerate(((kelvin, 1), (caps, 0), (cx, 1), (cy, 0), (cz, 0))):
            start = first + field * cells
            dest[pl.ds(b + shift, along), pl.ds(y, across)] = ref[
                start:start + cells
            ].reshape(along, across, lanes)
        start = first + 5 * cells
        faced[n * rows:(n + 1) * rows] = ref[start:start + rows]
        route[:, n * rows:(n + 1) * rows] = ref[start + rows:start + rows + TILE][:, 0:rows]

    walls = jnp.concatenate([kelvin[1 + b * along] for b in range(count_blk)], axis=0)
    strips = devices * across
    chosen = iota((strips, devices * rows), 0) == route[0:1].astype(jnp.int32)
    flux = film_coeff * (faced[...] - select_sum(chosen, walls, 0))
    heat[...] = select_sum(chosen, flux, 1)

    chunk = math.gcd(deep, max(1, ROWS // wide))
    none = jnp.zeros((TILE, lanes), jnp.float32)

    def sweep(body, init):
        return lax.fori_loop(0, deep // chunk, lambda i, c: body(i * chunk, c), init)

    def fold(value):
        return jnp.sum(value.reshape(-1, TILE, lanes), axis=0)

    def total(value):
        one = jnp.sum(jnp.sum(value, axis=0, keepdims=True), axis=1, keepdims=True)
        return jnp.broadcast_to(one, (TILE, lanes))

    def times(factor, value):
        return (factor * value.reshape(-1, TILE, lanes)).reshape(value.shape)

    def turned(v, step, axis):
        return pltpu.roll(v, step % v.shape[axis], axis=axis)

    def prepare(x, carry):
        here, own = pl.ds(x, chunk), pl.ds(x + 1, chunk)
        ups = cx[pl.ds(x + 2, chunk)], turned(cy[here], -1, 1), turned(cz[here], -1, 2)
        cyu[here] = ups[1]
        czu[here] = ups[2]
        diag[here] = caps[here] + ((cx[own] + ups[0]) + (cy[here] + ups[1]) + (cz[here] + ups[2]))
        v = kelvin[own]
        res[own] = (
            cx[own] * (kelvin[pl.ds(x, chunk)] - v)
            + ups[0] * (kelvin[pl.ds(x + 2, chunk)] - v)
            + (cy[here] * (turned(v, 1, 1) - v) + ups[1] * (turned(v, -1, 1) - v))
            + (cz[here] * (turned(v, 1, 2) - v) + ups[2] * (turned(v, -1, 2) - v))
        )
        return carry

    sweep(prepare, 0)
    for b in range(count_blk):
        at = b * along + 1
        res[at] = res[at] + heat[b * wide:(b + 1) * wide]

    def apply(x, sums):
        here, own = pl.ds(x, chunk), pl.ds(x + 1, chunk)
        v = res[own]
        value = (
            diag[here] * v
            - (cx[own] * res[pl.ds(x, chunk)] + cx[pl.ds(x + 2, chunk)] * res[pl.ds(x + 2, chunk)])
            - (cy[here] * turned(v, 1, 1) + cyu[here] * turned(v, -1, 1))
            - (cz[here] * turned(v, 1, 2) + czu[here] * turned(v, -1, 2))
        )
        image[here] = value
        return sums[0] + fold(v * v), sums[1] + fold(v * value)

    mine_at = pl.ds(mine, along), pl.ds(side, across)
    sol[...] = kelvin[pl.ds(mine + 1, along), pl.ds(side, across)]
    norm = alpha = beta = None
    for step in range(ITERS):
        fresh, product = (total(v) for v in sweep(apply, (none, none)))
        if step == 0:
            alpha = fresh / product
        else:
            beta = fresh / norm
            alpha = fresh / (product - beta * fresh / alpha)
        norm = fresh
        if step + 1 == ITERS:
            towards = res[pl.ds(mine + 1, along), pl.ds(side, across)] + times(beta, dirn[mine_at])
            out_ref[...] = sol[...] + times(alpha, towards)
            break

        def update(x, carry, step=step, alpha=alpha, beta=beta):
            here, own = pl.ds(x, chunk), pl.ds(x + 1, chunk)
            towards, moved = res[own], image[here]
            if step:
                towards = towards + times(beta, dirn[here])
                moved = moved + times(beta, drift[here])
            dirn[here] = towards
            drift[here] = moved
            res[own] = res[own] - times(alpha, moved)
            return carry

        sweep(update, 0)
        sol[...] = sol[...] + times(alpha, dirn[mine_at])


def swap(value, axis, flip):
    count = lax.axis_size(axis)
    return lax.ppermute(value, axis, [(i, i ^ flip) for i in range(count)])


def outer(value, axis="blk"):
    count = lax.axis_size(axis)
    pairs = [(i, (i + 1 if i % 2 else i - 1) % count) for i in range(count)]
    return lax.ppermute(value, axis, pairs)


def ring(value, axis, step):
    count = lax.axis_size(axis)
    return lax.ppermute(value, axis, [(i, (i + step) % count) for i in range(count)])


def flips(count):
    return [1 << k for k in reversed(range((count - 1).bit_length()))]


def shards(
    mass_per_volume,
    flow_speed_vector,
    normal_stress,
    facing_strip_index,
    solid_kelvin,
    face_coupling,
    substance_index,
    substance_storage,
):
    planes, rows, lanes = mass_per_volume.shape
    along, across, _ = solid_kelvin.shape
    count_blk, count_sub = lax.axis_size("blk"), lax.axis_size("sub")
    devices = count_blk * count_sub
    cells = along * across
    edge = FIELDS * planes * HALO
    each = across + 1
    record = 5 * cells + rows + TILE

    face = FIELDS * HALO * rows
    state, yedge, apay, bpay, metal, wall = call(
        pack_kernel,
        [
            f32(FIELDS, planes, rows, lanes), f32(2 * edge, lanes),
            f32(face + record, lanes), f32(face, lanes),
            f32(record, lanes), f32(each, lanes),
        ],
        [
            mass_per_volume, flow_speed_vector, normal_stress,
            facing_strip_index.reshape(1, rows), solid_kelvin.reshape(cells, lanes),
            face_coupling.reshape(6 * cells, lanes), substance_index.reshape(cells, lanes),
            substance_storage,
        ],
        hbm=tuple(range(8)),
        scratch=[
            (planes, rows, lanes), (3, planes, rows, lanes), (planes, rows, lanes),
            pltpu.VMEM((1, rows), jnp.int32), pltpu.VMEM((cells, lanes), jnp.int32),
            pltpu.SMEM(substance_storage.shape, jnp.float32), pltpu.SemaphoreType.DMA((8,)),
        ],
    )
    paired = count_blk == 4 and count_sub == 2
    span = FIELDS * corner_rows()[1]
    bpay = outer(bpay)
    if paired:
        wall_a = swap(wall, "blk", 1)
        ypay = jnp.concatenate([yedge, wall, wall_a], axis=0)
        yrecv = swap(ypay, "sub", 1)
        ylo, yhi, lo_at, hi_at = yrecv, yrecv, edge, 0
        parts = [wall, wall_a, yrecv]
        starts = [(0, each), (0, each), (2 * edge, 2 * each)]
    else:
        ylo, yhi, lo_at, hi_at = ring(yedge[edge:], "sub", 1), ring(yedge[:edge], "sub", -1), 0, 0
        parts, starts = [], []
    apay = swap(apay, "blk", 1)
    aedge, bedge = call(
        functools.partial(edge_kernel, planes, lo_at, hi_at, starts),
        [f32(2 * span, lanes), f32(2 * span + sum(c for _, c in starts), lanes)],
        [ylo, yhi, *parts],
    )
    bedge = outer(bedge)
    aedge = swap(aedge, "blk", 1)
    if paired:
        walls = [wall, wall_a, yrecv, yrecv] + 4 * [bedge]
        wall_at = [(0, 0, 0), (0, 1, 0), (2 * edge, 0, 1), (2 * edge + each, 1, 1)]
        wall_at += [(2 * span + k * each, 3 ^ (k & 1), k >> 1) for k in range(4)]
    else:
        wall = jnp.pad(wall, ((0, across + TILE - each), (0, 0)))
        walls = [lax.all_gather(wall, ("blk", "sub"), axis=0, tiled=True)]
        wall_at = None
    deep, stride = planes + 2 * HALO, rows + TILE
    ends_rows = up_to_tile((FIELDS + 1) * HALO)
    wide_lanes = -(-deep * stride // lanes) * lanes
    block, own_z, inner_z, outer_z = call(
        functools.partial(
            assemble_kernel, ((count_blk, count_sub), across), lo_at, hi_at, wall_at
        ),
        [
            f32(FIELDS + 1, deep, stride, lanes),
            f32((FIELDS + 1) * 2 * TILE, wide_lanes),
            f32(ends_rows, wide_lanes),
            f32(ends_rows, wide_lanes),
        ],
        [state, apay, bpay, ylo, yhi, aedge, bedge, *walls],
        scratch=[(devices * (across + TILE), lanes), (stride, lanes)],
    )
    inner_got = swap(inner_z, "grp", 1)
    outer_got = outer(outer_z, "grp")
    planes_next = call(
        planes_kernel,
        f32(FIELDS, planes, rows, lanes),
        [block],
        scratch=[
            (FIELDS, deep, stride, lanes), (8, deep, stride, lanes), (2, FIELDS, stride, lanes)
        ],
    )

    if paired:
        near_y = swap(metal, "sub", 1)
        far = swap(metal, "blk", 2)
        far_y = swap(near_y, "blk", 2)
        mates = swap(jnp.concatenate([near_y, far, far_y], axis=0), "blk", 1)
        pieces = [metal, apay, near_y, far, far_y, mates]
        where = [(0, 0), (1, face), (2, 0), (3, 0), (4, 0)] + [(5, k * record) for k in range(3)]
        order = [(0, 0), (1, 0), (0, 1), (2, 0), (2, 1), (1, 1), (3, 0), (3, 1)]
    else:
        held, order = metal, [(0, 0)]
        steps = [("blk", flip) for flip in flips(count_blk)]
        steps += [("sub", flip) for flip in flips(count_sub)]
        for axis, flip in steps:
            held = jnp.concatenate([held, swap(held, axis, flip)], axis=0)
            order = order + [
                (b ^ flip, s) if axis == "blk" else (b, s ^ flip) for b, s in order
            ]
        pieces, where = [held], [(0, k * record) for k in range(devices)]
    wide = count_sub * across
    deep_metal = count_blk * along
    field = (deep_metal, wide, lanes)
    padded = (deep_metal + 2, wide, lanes)
    metal_next = call(
        functools.partial(
            metal_kernel, (count_blk, count_sub, along, across), rows, where, order
        ),
        f32(along, across, lanes),
        pieces,
        scratch=[
            (along, across, lanes), padded, padded, field, field, field, field, padded, field,
            field, field, field, field, (devices * across, lanes), (TILE, devices * rows), (devices * rows, lanes),
        ],
    )
    slab = 2 * -(-(NEAR + HALO) // (TILE // 2)) * (TILE // 2)
    fluid_next = call(
        functools.partial(ends_kernel, stride),
        f32(FIELDS, planes, rows, lanes),
        [planes_next, own_z, inner_got, outer_got],
        scratch=[
            (FIELDS + 1, slab, wide_lanes), (FIELDS, slab, wide_lanes), (lanes, wide_lanes)
        ],
    )
    return (fluid_next, metal_next)


def solution(mesh):
    in_specs = (
        P("blk", "sub", "grp"),
        P(None, "blk", "sub", "grp"),
        P("blk", "sub", "grp"),
        P("grp", "blk", "sub"),
        P("blk", "sub", "grp"),
        P(None, "blk", "sub", "grp"),
        P("blk", "sub", "grp"),
        P(),
    )
    out_specs = (P(None, "blk", "sub", "grp"), P("blk", "sub", "grp"))
    return jax.shard_map(shards, mesh=mesh, in_specs=in_specs, out_specs=out_specs, check_vma=False)
```

```python
import functools
import math

import jax
import jax.numpy as jnp
from jax import lax
from jax.experimental import pallas as pl
from jax.experimental.pallas import tpu as pltpu
from jax.sharding import PartitionSpec as P


ITERS = 4
HALO = 3
TILE = 8
FIELDS = 5
NEAR = 2 * HALO
ROWS = 512

gamma_gas = 1.4
time_step = 0.1
viscosity = 0.05
film_coeff = 1.0
third_part = 1.0 / 3.0
two_thirds = 2.0 / 3.0

SPARE_BYTES = 6 * 1024 * 1024


def bytes_of(shapes):
    total = 0
    for shape in shapes:
        *lead, rows, lanes = (1, 1, *shape)
        total += 4 * math.prod(lead) * up_to_tile(rows) * (-(-lanes // 128) * 128)
    return total


def call(body, out, inputs, hbm=(), hbm_out=(), cost=100_000, scratch=()):
    inputs = [
        pltpu.with_memory_space_constraint(x, pltpu.HBM) if i in hbm else x
        for i, x in enumerate(inputs)
    ]
    limit = SPARE_BYTES + bytes_of(
        [x.shape for i, x in enumerate(inputs) if i not in hbm]
        + [x.shape for x in jax.tree.leaves(out)]
        + [x for x in scratch if isinstance(x, tuple)]
    )
    return pl.pallas_call(
        body,
        out_shape=out,
        in_specs=[
            pl.BlockSpec(memory_space=pltpu.HBM if i in hbm else pltpu.VMEM)
            for i in range(len(inputs))
        ],
        out_specs=jax.tree.unflatten(
            jax.tree.structure(out),
            [
                pl.BlockSpec(memory_space=pltpu.HBM if i in hbm_out else pltpu.VMEM)
                for i in range(len(jax.tree.leaves(out)))
            ],
        ),
        scratch_shapes=[
            pltpu.VMEM(x, jnp.float32) if isinstance(x, tuple) else x for x in scratch
        ],
        cost_estimate=pl.CostEstimate(flops=cost, bytes_accessed=cost, transcendentals=0),
        compiler_params=pltpu.CompilerParams(vmem_limit_bytes=limit),
    )(*inputs)


def f32(*shape):
    return jax.ShapeDtypeStruct(shape, jnp.float32)


def up_to_tile(count):
    return -(-count // TILE) * TILE


def iota(shape, dim):
    return lax.broadcasted_iota(jnp.int32, shape, dim)


def pieces_of(value):
    out = []
    for _ in range(2):
        piece = value.astype(jnp.bfloat16)
        out.append(piece)
        value = value - piece.astype(jnp.float32)
    return out + [value.astype(jnp.bfloat16)]


def select_sum(chosen, value, dim):
    flags = chosen.astype(jnp.float32).astype(jnp.bfloat16)
    return sum(
        lax.dot_general(
            flags, piece, (((dim,), (0,)), ((), ())), preferred_element_type=jnp.float32
        )
        for piece in reversed(pieces_of(value))
    )


def parity(axis="blk"):
    return lax.rem(lax.axis_index(axis), 2)


def pack_kernel(
    rho_hbm, vel_hbm, pre_hbm, route_hbm, kelvin_hbm, couple_hbm, kind_hbm, store_hbm,
    state_ref, yedge_ref, apay_ref, bpay_ref, metal_ref, wall_ref,
    rho_ref, vel_ref, pre_ref, route_ref, kind_ref, store_ref, arrived,
):
    planes, rows, lanes = rho_ref.shape
    cells = kind_ref.shape[0]
    across = wall_ref.shape[0] - 1
    face = FIELDS * HALO * rows
    copies = [
        pltpu.make_async_copy(src, dst, arrived.at[k])
        for k, (src, dst) in enumerate((
            (rho_hbm, rho_ref), (vel_hbm, vel_ref), (pre_hbm, pre_ref),
            (kelvin_hbm, metal_ref.at[0:cells]),
            (couple_hbm.at[0:3 * cells], metal_ref.at[2 * cells:5 * cells]),
            (kind_hbm, kind_ref), (store_hbm, store_ref), (route_hbm, route_ref),
        ))
    ]
    for copy in copies:
        copy.start()
    for copy in copies[:3]:
        copy.wait()
    for x in range(planes):
        rho = rho_ref[x]
        vel = [vel_ref[d, x] for d in range(3)]
        mom = [rho * v for v in vel]
        kinetic = mom[0] * vel[0] + mom[1] * vel[1] + mom[2] * vel[2]
        energy = pre_ref[x] / (gamma_gas - 1.0) + 0.5 * kinetic
        for f, value in enumerate([rho, *mom, energy]):
            state_ref[f, x] = value
    used = FIELDS * planes * HALO
    for f in range(FIELDS):
        for x in range(planes):
            at = (f * planes + x) * HALO
            yedge_ref[at:at + HALO] = state_ref[f, x, 0:HALO]
            yedge_ref[used + at:used + at + HALO] = state_ref[f, x, rows - HALO:rows]
    for odd in range(2):

        @pl.when(parity() == odd)
        def _():
            for f in range(FIELDS):
                for j in range(HALO):
                    at = (f * HALO + j) * rows
                    apay_ref[at:at + rows] = state_ref[f, j + (planes - HALO) * (1 - odd)]
                    bpay_ref[at:at + rows] = state_ref[f, j + (planes - HALO) * odd]

    for copy in copies[3:]:
        copy.wait()
    wall_ref[0:across] = metal_ref[0:across]
    wall_ref[across:across + 1] = jnp.zeros((1, lanes), jnp.float32)
    wall_ref[across:across + 1, 0:rows] = route_ref[...].astype(jnp.float32)
    kind = kind_ref[...]
    capacity = jnp.zeros((cells, lanes), jnp.float32)
    for m in range(store_ref.shape[0]):
        capacity = jnp.where(kind == m, store_ref[m], capacity)
    metal_ref[cells:2 * cells] = capacity
    metal_ref[5 * cells:5 * cells + rows] = pre_ref[0] / rho_ref[0]
    metal_ref[5 * cells + rows:5 * cells + rows + TILE] = jnp.zeros((TILE, lanes), jnp.float32)
    metal_ref[5 * cells + rows:5 * cells + rows + 1] = wall_ref[across:across + 1]
    record = 5 * cells + rows + TILE
    apay_ref[face:face + record] = metal_ref[...]


def corner_rows():
    at, out = 0, []
    for j in range(1, HALO):
        out.append((j, at, HALO - j))
        at += HALO - j
    return out, at


def edge_kernel(planes, lo_at, hi_at, starts, *refs):
    ylo_ref, yhi_ref = refs[0], refs[1]
    parts, (aedge_ref, bedge_ref) = refs[2:-2], refs[-2:]
    corners, each = corner_rows()
    for odd in range(2):

        @pl.when(parity() == odd)
        def _():
            for out, last in ((aedge_ref, odd == 0), (bedge_ref, odd == 1)):
                for f in range(FIELDS):
                    for j, first, count in corners:
                        src = (f * planes + (planes - j if last else j - 1)) * HALO
                        lo, hi = lo_at + src + HALO - count, hi_at + src
                        at = f * each + first
                        out[at:at + count] = ylo_ref[lo:lo + count]
                        at += FIELDS * each
                        out[at:at + count] = yhi_ref[hi:hi + count]

    at = 2 * FIELDS * each
    for ref, (start, count) in zip(parts, starts):
        bedge_ref[at:at + count] = ref[start:start + count]
        at += count


def assemble_kernel(dims, lo_at, hi_at, wall_at, *refs):
    axes, across = dims
    count_blk, count_sub = axes
    state_ref, apay_ref, bpay_ref, ylo_ref, yhi_ref, aedge_ref, bedge_ref = refs[:7]
    wall_refs = refs[7:-6]
    block_ref, own_ref, inner_ref, outer_ref, table, seen = refs[-6:]
    _, planes, rows, lanes = state_ref.shape
    deep, stride = block_ref.shape[1:3]
    corners, each_corner = corner_rows()
    each = across + TILE
    blk, sub = lax.axis_index("blk"), lax.axis_index("sub")

    for f in range(FIELDS):
        for x in range(planes):
            at = (f * planes + x) * HALO
            block_ref[f, x + HALO, 0:rows] = state_ref[f, x]
            block_ref[f, x + HALO, rows:rows + HALO] = yhi_ref[hi_at + at:hi_at + at + HALO]
            block_ref[f, x + HALO, stride - HALO:stride] = ylo_ref[lo_at + at:lo_at + at + HALO]
    for odd in range(2):

        @pl.when(parity() == odd)
        def _():
            for face_ref, edge_ref, above in (
                (apay_ref, aedge_ref, odd == 0), (bpay_ref, bedge_ref, odd == 1),
            ):
                for f in range(FIELDS):
                    for j in range(HALO):
                        at = (f * HALO + j) * rows
                        x = planes + HALO + j if above else j
                        block_ref[f, x, 0:rows] = face_ref[at:at + rows]
                    for j, first, count in corners:
                        at = f * each_corner + first
                        x = planes + HALO + j - 1 if above else HALO - j
                        block_ref[f, x, stride - count:stride] = edge_ref[at:at + count]
                        at += FIELDS * each_corner
                        block_ref[f, x, rows:rows + count] = edge_ref[at:at + count]

    if wall_at is None:
        table = wall_refs[0]
    else:
        for ref, (start, flip_blk, flip_sub) in zip(wall_refs, wall_at):
            device = jnp.bitwise_xor(blk, flip_blk) * count_sub + jnp.bitwise_xor(sub, flip_sub)
            table[pl.ds(pl.multiple_of(device * each, TILE), across + 1)] = ref[
                start:start + across + 1
            ]
    devices = count_blk * count_sub
    walls = jnp.concatenate(
        [table[d * each:d * each + across] for d in range(devices)], axis=0
    )

    def facing(blk_at, sub_at):
        device = lax.rem(blk_at, count_blk) * count_sub + lax.rem(sub_at, count_sub)
        at = pl.multiple_of(device * each + across, TILE)
        routes = table[pl.ds(at, TILE)][0:1, 0:rows].astype(jnp.int32)
        return select_sum(iota((devices * across, rows), 0) == routes, walls, 0)

    block_ref[FIELDS] = jnp.zeros(block_ref.shape[1:], jnp.float32)
    for x, blk_at in ((0, blk), (planes, blk + 1)):
        below = facing(blk_at, sub + count_sub - 1)
        above = below if count_sub == 2 else facing(blk_at, sub + 1)
        seen[0:rows] = facing(blk_at, sub)
        seen[rows:] = jnp.zeros((stride - rows, lanes), jnp.float32)
        seen[rows:rows + HALO] = above[0:HALO]
        seen[stride - HALO:stride] = below[rows - HALO:rows]
        rho, mx, my, mz, energy = [block_ref[f, x + HALO] for f in range(FIELDS)]
        pressure = (gamma_gas - 1.0) * (energy - 0.5 * (mx * mx + my * my + mz * mz) / rho)
        block_ref[FIELDS, x + HALO] = film_coeff * (pressure / rho - seen[...])
    pick = iota((2 * TILE, lanes), 0)
    cell = iota((2 * TILE, lanes), 1)
    chosen = (
        ((pick == cell) & (pick < NEAR))
        | ((pick - TILE + lanes - NEAR == cell) & (pick >= TILE) & (pick < TILE + NEAR))
    ).astype(jnp.float32).astype(jnp.bfloat16)
    size = deep * stride
    upper = parity("grp") == 1
    for f in range(FIELDS + 1):
        ends = sum(
            lax.dot_general(
                chosen, piece, (((1,), (1,)), ((), ())), preferred_element_type=jnp.float32
            )
            for piece in reversed(pieces_of(block_ref[f].reshape(size, lanes)))
        )
        own_ref[f * 2 * TILE:(f + 1) * 2 * TILE, 0:size] = ends
        low, high = ends[0:HALO], ends[TILE + NEAR - HALO:TILE + NEAR]
        inner_ref[f * HALO:(f + 1) * HALO, 0:size] = jnp.where(upper, low, high)
        outer_ref[f * HALO:(f + 1) * HALO, 0:size] = jnp.where(upper, high, low)
    used = (FIELDS + 1) * HALO
    if own_ref.shape[1] > size:
        own_ref[:, size:] = jnp.zeros((own_ref.shape[0], own_ref.shape[1] - size), jnp.float32)
    for ref in (inner_ref, outer_ref):
        if ref.shape[1] > size:
            ref[:, size:] = jnp.zeros((ref.shape[0], ref.shape[1] - size), jnp.float32)
        if ref.shape[0] > used:
            ref[used:] = jnp.zeros((ref.shape[0] - used, ref.shape[1]), jnp.float32)


def primitives(u):
    rho, mx, my, mz, energy = u
    inverse = 1.0 / rho
    ux, uy, uz = mx * inverse, my * inverse, mz * inverse
    pressure = (gamma_gas - 1.0) * (energy - 0.5 * (mx * ux + my * uy + mz * uz))
    sound = jnp.sqrt(gamma_gas * pressure * inverse)
    return [
        ux, uy, uz, jnp.abs(ux) + sound, jnp.abs(uy) + sound, jnp.abs(uz) + sound,
        pressure, energy + pressure,
    ]


def faces(d, lo, hi):
    def flux(v):
        speed, pressure, enthalpy = v[5], v[7], v[8]
        f = [v[1 + d]] + [v[1 + i] * speed for i in range(3)] + [enthalpy * speed]
        f[1 + d] = f[1 + d] + pressure
        return f

    below, here = flux(lo), flux(hi)
    fast = jnp.maximum(lo[6], hi[6])
    slow = fast + 2.0 * viscosity
    return [
        (below[i] + here[i]) - (fast if i == 0 else slow) * (hi[i] - lo[i]) for i in range(5)
    ]


def advance(stage, old, change, start, sink):
    fresh = old - (0.5 * time_step) * change
    if sink is not None:
        fresh = fresh - time_step * sink
    if stage == 0:
        return fresh
    if stage == 1:
        return 0.75 * start + 0.25 * fresh
    return third_part * start + two_thirds * fresh


def planes_kernel(block_ref, out_ref, now, prim, xface):
    deep, _, _ = block_ref.shape[1:]
    rows = out_ref.shape[2]
    for stage in range(3):
        src = block_ref if stage == 0 else now
        low, high = stage + 1, deep - 1 - stage
        for x in range(low - 1, high + 1):
            for k, value in enumerate(primitives([src[f, x] for f in range(FIELDS)])):
                prim[k, x] = value

        def cells(x, d, src=src):
            return [src[f, x] for f in range(FIELDS)] + [
                prim[d, x], prim[3 + d, x], prim[6, x], prim[7, x]
            ]

        for x in range(low, high + 1):
            new = faces(0, cells(x - 1, 0), cells(x, 0))
            for f in range(FIELDS):
                xface[x % 2, f] = new[f]
            if x == low:
                continue
            p = x - 1
            change = [new[f] - xface[p % 2, f] for f in range(FIELDS)]
            for d, axis in ((1, 0), (2, 1)):
                hi = cells(p, d)
                lo = [pltpu.roll(v, 1, axis=axis) for v in hi]
                face = faces(d, lo, hi)
                last = hi[0].shape[axis] - 1
                change = [c + (pltpu.roll(v, last, axis=axis) - v) for c, v in zip(change, face)]
            for f in range(FIELDS):
                sink = block_ref[FIELDS, p] if f == FIELDS - 1 else None
                value = advance(stage, src[f, p], change[f], block_ref[f, p], sink)
                if stage == 2:
                    out_ref[f, p - HALO] = value[0:rows]
                else:
                    now[f, p] = value


def ends_kernel(
    stride, main_ref, own_ref, inner_ref, outer_ref, out_ref, slab_base, base, slab, comb
):
    _, planes, rows, lanes = out_ref.shape
    deep = planes + 2 * HALO
    wide = slab_base.shape[2]
    half = slab_base.shape[1] // 2
    part = FIELDS * TILE
    source = iota((lanes, FIELDS * lanes), 0)
    target = iota((lanes, FIELDS * lanes), 1)
    field = lax.rem(source, part) // TILE
    end = lax.rem(source, TILE)
    spread = (
        ((end < HALO) & (target == field * lanes + end))
        | (
            (end >= HALO) & (end < 2 * HALO)
            & (target == field * lanes + lanes - 2 * HALO + end)
        )
    ) & (source < 3 * part)
    spread = spread.astype(jnp.float32).astype(jnp.bfloat16)
    comb[...] = jnp.zeros(comb.shape, jnp.float32)
    slab_base[...] = jnp.zeros(slab_base.shape, jnp.float32)
    upper = parity("grp") == 1
    for f in range(FIELDS + 1):
        inner, outer = (ref[f * HALO:(f + 1) * HALO] for ref in (inner_ref, outer_ref))
        at = f * 2 * TILE
        slab_base[f, 0:HALO] = jnp.where(upper, inner, outer)
        slab_base[f, HALO:HALO + NEAR] = own_ref[at:at + NEAR]
        slab_base[f, half:half + NEAR] = own_ref[at + TILE:at + TILE + NEAR]
        slab_base[f, half + NEAR:half + NEAR + HALO] = jnp.where(upper, outer, inner)

    narrow = min(wide, -(-(deep - 1) * stride // lanes) * lanes)
    kept = NEAR + HALO - 2
    start = slab_base
    for stage in range(3):
        src = slab_base if stage == 0 else slab
        u = [src[f] for f in range(FIELDS)]
        tall, width = u[0].shape
        first_row = lax.rem(iota((tall, width), 1), stride) == 0
        last_row = lax.rem(iota((tall, width), 1), stride) == stride - 1

        def lane_roll(v, shift, width=width):
            return pltpu.roll(v, shift % width, axis=1)

        q = primitives(u)
        hi = u + [q[2], q[5], q[6], q[7]]
        face = faces(2, [pltpu.roll(v, 1, axis=0) for v in hi], hi)
        change = [pltpu.roll(v, tall - 1, axis=0) - v for v in face]
        hi = u + [q[0], q[3], q[6], q[7]]
        face = faces(0, [lane_roll(v, stride) for v in hi], hi)
        change = [c + (lane_roll(v, -stride) - v) for c, v in zip(change, face)]
        hi = u + [q[1], q[4], q[6], q[7]]
        lo = [jnp.where(first_row, lane_roll(v, 1 - stride), lane_roll(v, 1)) for v in hi]
        face = faces(1, lo, hi)
        change = [
            c + (jnp.where(last_row, lane_roll(v, stride - 1), lane_roll(v, -1)) - v)
            for c, v in zip(change, face)
        ]
        for f in range(FIELDS):
            sink = start[FIELDS] if f == FIELDS - 1 else None
            value = advance(stage, u[f], change[f], start[f], sink)
            if stage:
                slab[f] = value
                continue
            for group in range(2):
                slab[f, group * TILE:group * TILE + kept] = value[
                    group * half + 1:group * half + 1 + kept, 0:narrow
                ]
                slab[f, group * TILE + kept:(group + 1) * TILE] = jnp.zeros(
                    (TILE - kept, narrow), jnp.float32
                )
        if stage == 0:
            for f in range(FIELDS + 1):
                for group in range(2):
                    base[f, group * TILE:group * TILE + kept] = slab_base[
                        f, group * half + 1:group * half + 1 + kept, 0:narrow
                    ]
                    base[f, group * TILE + kept:(group + 1) * TILE] = jnp.zeros(
                        (TILE - kept, narrow), jnp.float32
                    )
            start = base

    for f in range(FIELDS):
        first = HALO - 1
        comb[f * TILE:f * TILE + HALO, 0:narrow] = slab[f, first:first + HALO]
        first = TILE + NEAR - HALO - 1
        comb[f * TILE + HALO:f * TILE + 2 * HALO, 0:narrow] = slab[f, first:first + HALO]
    whole = comb[0:part]
    for k in range(2):
        piece = whole.astype(jnp.bfloat16).astype(jnp.float32)
        comb[k * part:(k + 1) * part] = piece
        whole = whole - piece
    comb[2 * part:3 * part] = whole
    turned = jnp.transpose(comb[...]).astype(jnp.bfloat16)
    moved = lax.dot_general(
        turned[HALO * stride:(HALO + planes) * stride], spread, (((1,), (0,)), ((), ())),
        preferred_element_type=jnp.float32,
    )
    lane = iota((rows, lanes), 1)
    near = (lane < HALO) | (lane >= lanes - HALO)
    for f in range(FIELDS):
        for x in range(planes):
            edge = moved[x * stride:x * stride + rows, f * lanes:(f + 1) * lanes]
            out_ref[f, x] = jnp.where(near, edge, main_ref[f, x])


def metal_kernel(dims, rows, where, order, *refs):
    fluid_ref, fluid_hbm, written = refs[-20], refs[-18], refs[-1]
    refs = (*refs[:-20], refs[-19], *refs[-17:-1])
    leave = pltpu.make_async_copy(fluid_ref, fluid_hbm, written)
    leave.start()
    count_blk, count_sub, along, across = dims
    devices = count_blk * count_sub
    pieces = [(refs[k], start) for k, start in where]
    (
        out_ref, sol, kelvin, res, dirn, drift, image, diag, cx, cy, cz, cyu, czu, caps, heat,
        route, faced,
    ) = refs[-17:]
    lanes = out_ref.shape[-1]
    cells = along * across
    wide = count_sub * across
    deep = count_blk * along
    blk, sub = lax.axis_index("blk"), lax.axis_index("sub")
    mine = blk * along
    side = pl.multiple_of(sub * across, TILE)

    zero = jnp.zeros((wide, lanes), jnp.float32)
    for ref in (kelvin, res, cx):
        ref[0] = zero
        ref[deep + 1] = zero

    for n, ((ref, first), (flip_blk, flip_sub)) in enumerate(zip(pieces, order)):
        b = jnp.bitwise_xor(blk, flip_blk) * along
        y = pl.multiple_of(jnp.bitwise_xor(sub, flip_sub) * across, TILE)
        for field, (dest, shift) in enumerate(((kelvin, 1), (caps, 0), (cx, 1), (cy, 0), (cz, 0))):
            start = first + field * cells
            dest[pl.ds(b + shift, along), pl.ds(y, across)] = ref[
                start:start + cells
            ].reshape(along, across, lanes)
        start = first + 5 * cells
        faced[n * rows:(n + 1) * rows] = ref[start:start + rows]
        route[:, n * rows:(n + 1) * rows] = ref[start + rows:start + rows + TILE][:, 0:rows]

    walls = jnp.concatenate([kelvin[1 + b * along] for b in range(count_blk)], axis=0)
    strips = devices * across
    chosen = iota((strips, devices * rows), 0) == route[0:1].astype(jnp.int32)
    flux = film_coeff * (faced[...] - select_sum(chosen, walls, 0))
    heat[...] = select_sum(chosen, flux, 1)

    chunk = math.gcd(deep, max(1, ROWS // wide))
    none = jnp.zeros((TILE, lanes), jnp.float32)

    def sweep(body, init):
        return lax.fori_loop(0, deep // chunk, lambda i, c: body(i * chunk, c), init)

    def fold(value):
        return jnp.sum(value.reshape(-1, TILE, lanes), axis=0)

    def total(value):
        one = jnp.sum(jnp.sum(value, axis=0, keepdims=True), axis=1, keepdims=True)
        return jnp.broadcast_to(one, (TILE, lanes))

    def times(factor, value):
        return (factor * value.reshape(-1, TILE, lanes)).reshape(value.shape)

    def turned(v, step, axis):
        return pltpu.roll(v, step % v.shape[axis], axis=axis)

    def prepare(x, carry):
        here, own = pl.ds(x, chunk), pl.ds(x + 1, chunk)
        ups = cx[pl.ds(x + 2, chunk)], turned(cy[here], -1, 1), turned(cz[here], -1, 2)
        cyu[here] = ups[1]
        czu[here] = ups[2]
        diag[here] = caps[here] + ((cx[own] + ups[0]) + (cy[here] + ups[1]) + (cz[here] + ups[2]))
        v = kelvin[own]
        res[own] = (
            cx[own] * (kelvin[pl.ds(x, chunk)] - v)
            + ups[0] * (kelvin[pl.ds(x + 2, chunk)] - v)
            + (cy[here] * (turned(v, 1, 1) - v) + ups[1] * (turned(v, -1, 1) - v))
            + (cz[here] * (turned(v, 1, 2) - v) + ups[2] * (turned(v, -1, 2) - v))
        )
        return carry

    sweep(prepare, 0)
    for b in range(count_blk):
        at = b * along + 1
        res[at] = res[at] + heat[b * wide:(b + 1) * wide]

    def apply(x, sums):
        here, own = pl.ds(x, chunk), pl.ds(x + 1, chunk)
        v = res[own]
        value = (
            diag[here] * v
            - (cx[own] * res[pl.ds(x, chunk)] + cx[pl.ds(x + 2, chunk)] * res[pl.ds(x + 2, chunk)])
            - (cy[here] * turned(v, 1, 1) + cyu[here] * turned(v, -1, 1))
            - (cz[here] * turned(v, 1, 2) + czu[here] * turned(v, -1, 2))
        )
        image[here] = value
        return sums[0] + fold(v * v), sums[1] + fold(v * value)

    mine_at = pl.ds(mine, along), pl.ds(side, across)
    sol[...] = kelvin[pl.ds(mine + 1, along), pl.ds(side, across)]
    norm = alpha = beta = None
    for step in range(ITERS):
        fresh, product = (total(v) for v in sweep(apply, (none, none)))
        if step == 0:
            alpha = fresh / product
        else:
            beta = fresh / norm
            alpha = fresh / (product - beta * fresh / alpha)
        norm = fresh
        if step + 1 == ITERS:
            towards = res[pl.ds(mine + 1, along), pl.ds(side, across)] + times(beta, dirn[mine_at])
            out_ref[...] = sol[...] + times(alpha, towards)
            leave.wait()
            break

        def update(x, carry, step=step, alpha=alpha, beta=beta):
            here, own = pl.ds(x, chunk), pl.ds(x + 1, chunk)
            towards, moved = res[own], image[here]
            if step:
                towards = towards + times(beta, dirn[here])
                moved = moved + times(beta, drift[here])
            dirn[here] = towards
            drift[here] = moved
            res[own] = res[own] - times(alpha, moved)
            return carry

        sweep(update, 0)
        sol[...] = sol[...] + times(alpha, dirn[mine_at])


def swap(value, axis, flip):
    count = lax.axis_size(axis)
    return lax.ppermute(value, axis, [(i, i ^ flip) for i in range(count)])


def outer(value, axis="blk"):
    count = lax.axis_size(axis)
    pairs = [(i, (i + 1 if i % 2 else i - 1) % count) for i in range(count)]
    return lax.ppermute(value, axis, pairs)


def ring(value, axis, step):
    count = lax.axis_size(axis)
    return lax.ppermute(value, axis, [(i, (i + step) % count) for i in range(count)])


def flips(count):
    return [1 << k for k in reversed(range((count - 1).bit_length()))]


def shards(
    mass_per_volume,
    flow_speed_vector,
    normal_stress,
    facing_strip_index,
    solid_kelvin,
    face_coupling,
    substance_index,
    substance_storage,
):
    planes, rows, lanes = mass_per_volume.shape
    along, across, _ = solid_kelvin.shape
    count_blk, count_sub = lax.axis_size("blk"), lax.axis_size("sub")
    devices = count_blk * count_sub
    cells = along * across
    edge = FIELDS * planes * HALO
    each = across + 1
    record = 5 * cells + rows + TILE

    face = FIELDS * HALO * rows
    state, yedge, apay, bpay, metal, wall = call(
        pack_kernel,
        [
            f32(FIELDS, planes, rows, lanes), f32(2 * edge, lanes),
            f32(face + record, lanes), f32(face, lanes),
            f32(record, lanes), f32(each, lanes),
        ],
        [
            mass_per_volume, flow_speed_vector, normal_stress,
            facing_strip_index.reshape(1, rows), solid_kelvin.reshape(cells, lanes),
            face_coupling.reshape(6 * cells, lanes), substance_index.reshape(cells, lanes),
            substance_storage,
        ],
        hbm=tuple(range(8)),
        scratch=[
            (planes, rows, lanes), (3, planes, rows, lanes), (planes, rows, lanes),
            pltpu.VMEM((1, rows), jnp.int32), pltpu.VMEM((cells, lanes), jnp.int32),
            pltpu.SMEM(substance_storage.shape, jnp.float32), pltpu.SemaphoreType.DMA((8,)),
        ],
    )
    paired = count_blk == 4 and count_sub == 2
    span = FIELDS * corner_rows()[1]
    bpay = outer(bpay)
    if paired:
        wall_a = swap(wall, "blk", 1)
        ypay = jnp.concatenate([yedge, wall, wall_a], axis=0)
        yrecv = swap(ypay, "sub", 1)
        ylo, yhi, lo_at, hi_at = yrecv, yrecv, edge, 0
        parts = [wall, wall_a, yrecv]
        starts = [(0, each), (0, each), (2 * edge, 2 * each)]
    else:
        ylo, yhi, lo_at, hi_at = ring(yedge[edge:], "sub", 1), ring(yedge[:edge], "sub", -1), 0, 0
        parts, starts = [], []
    apay = swap(apay, "blk", 1)
    aedge, bedge = call(
        functools.partial(edge_kernel, planes, lo_at, hi_at, starts),
        [f32(2 * span, lanes), f32(2 * span + sum(c for _, c in starts), lanes)],
        [ylo, yhi, *parts],
    )
    bedge = outer(bedge)
    aedge = swap(aedge, "blk", 1)
    if paired:
        walls = [wall, wall_a, yrecv, yrecv] + 4 * [bedge]
        wall_at = [(0, 0, 0), (0, 1, 0), (2 * edge, 0, 1), (2 * edge + each, 1, 1)]
        wall_at += [(2 * span + k * each, 3 ^ (k & 1), k >> 1) for k in range(4)]
    else:
        wall = jnp.pad(wall, ((0, across + TILE - each), (0, 0)))
        walls = [lax.all_gather(wall, ("blk", "sub"), axis=0, tiled=True)]
        wall_at = None
    deep, stride = planes + 2 * HALO, rows + TILE
    ends_rows = up_to_tile((FIELDS + 1) * HALO)
    wide_lanes = -(-deep * stride // lanes) * lanes
    block, own_z, inner_z, outer_z = call(
        functools.partial(
            assemble_kernel, ((count_blk, count_sub), across), lo_at, hi_at, wall_at
        ),
        [
            f32(FIELDS + 1, deep, stride, lanes),
            f32((FIELDS + 1) * 2 * TILE, wide_lanes),
            f32(ends_rows, wide_lanes),
            f32(ends_rows, wide_lanes),
        ],
        [state, apay, bpay, ylo, yhi, aedge, bedge, *walls],
        scratch=[(devices * (across + TILE), lanes), (stride, lanes)],
    )
    inner_got = swap(inner_z, "grp", 1)
    outer_got = outer(outer_z, "grp")
    planes_next = call(
        planes_kernel,
        f32(FIELDS, planes, rows, lanes),
        [block],
        scratch=[
            (FIELDS, deep, stride, lanes), (8, deep, stride, lanes), (2, FIELDS, stride, lanes)
        ],
    )

    if paired:
        near_y = swap(metal, "sub", 1)
        far = swap(metal, "blk", 2)
        far_y = swap(near_y, "blk", 2)
        mates = swap(jnp.concatenate([near_y, far, far_y], axis=0), "blk", 1)
        pieces = [metal, apay, near_y, far, far_y, mates]
        where = [(0, 0), (1, face), (2, 0), (3, 0), (4, 0)] + [(5, k * record) for k in range(3)]
        order = [(0, 0), (1, 0), (0, 1), (2, 0), (2, 1), (1, 1), (3, 0), (3, 1)]
    else:
        held, order = metal, [(0, 0)]
        steps = [("blk", flip) for flip in flips(count_blk)]
        steps += [("sub", flip) for flip in flips(count_sub)]
        for axis, flip in steps:
            held = jnp.concatenate([held, swap(held, axis, flip)], axis=0)
            order = order + [
                (b ^ flip, s) if axis == "blk" else (b, s ^ flip) for b, s in order
            ]
        pieces, where = [held], [(0, k * record) for k in range(devices)]
    wide = count_sub * across
    deep_metal = count_blk * along
    field = (deep_metal, wide, lanes)
    padded = (deep_metal + 2, wide, lanes)
    slab = 2 * -(-(NEAR + HALO) // (TILE // 2)) * (TILE // 2)
    narrow = min(wide_lanes, -(-(deep - 1) * stride // lanes) * lanes)
    fluid = call(
        functools.partial(ends_kernel, stride),
        f32(FIELDS, planes, rows, lanes),
        [planes_next, own_z, inner_got, outer_got],
        scratch=[
            (FIELDS + 1, slab, wide_lanes), (FIELDS + 1, 2 * TILE, narrow),
            (FIELDS, 2 * TILE, narrow), (lanes, wide_lanes),
        ],
    )
    metal_next, fluid_next = call(
        functools.partial(
            metal_kernel, (count_blk, count_sub, along, across), rows, where, order
        ),
        [f32(along, across, lanes), f32(FIELDS, planes, rows, lanes)],
        [*pieces, fluid],
        hbm_out=(1,),
        scratch=[
            (along, across, lanes), padded, padded, field, field, field, field, padded, field,
            field, field, field, field, (devices * across, lanes), (TILE, devices * rows), (devices * rows, lanes),
            pltpu.SemaphoreType.DMA,
        ],
    )
    return (fluid_next, metal_next)


def solution(mesh):
    in_specs = (
        P("blk", "sub", "grp"),
        P(None, "blk", "sub", "grp"),
        P("blk", "sub", "grp"),
        P("grp", "blk", "sub"),
        P("blk", "sub", "grp"),
        P(None, "blk", "sub", "grp"),
        P("blk", "sub", "grp"),
        P(),
    )
    out_specs = (P(None, "blk", "sub", "grp"), P("blk", "sub", "grp"))
    return jax.shard_map(shards, mesh=mesh, in_specs=in_specs, out_specs=out_specs, check_vma=False)
```

```python
import functools
import math

import jax
import jax.numpy as jnp
from jax import lax
from jax.experimental import pallas as pl
from jax.experimental.pallas import tpu as pltpu
from jax.sharding import PartitionSpec as P


ITERS = 4
HALO = 3
TILE = 8
FIELDS = 5
NEAR = 2 * HALO
ROWS = 512

gamma_gas = 1.4
time_step = 0.1
viscosity = 0.05
film_coeff = 1.0
third_part = 1.0 / 3.0
two_thirds = 2.0 / 3.0

SPARE_BYTES = 6 * 1024 * 1024


def bytes_of(shapes):
    total = 0
    for shape in shapes:
        *lead, rows, lanes = (1, 1, *shape)
        total += 4 * math.prod(lead) * up_to_tile(rows) * (-(-lanes // 128) * 128)
    return total


def call(body, out, inputs, hbm=(), hbm_out=(), cost=100_000, scratch=()):
    inputs = [
        pltpu.with_memory_space_constraint(x, pltpu.HBM) if i in hbm else x
        for i, x in enumerate(inputs)
    ]
    limit = SPARE_BYTES + bytes_of(
        [x.shape for i, x in enumerate(inputs) if i not in hbm]
        + [x.shape for x in jax.tree.leaves(out)]
        + [x for x in scratch if isinstance(x, tuple)]
    )
    return pl.pallas_call(
        body,
        out_shape=out,
        in_specs=[
            pl.BlockSpec(memory_space=pltpu.HBM if i in hbm else pltpu.VMEM)
            for i in range(len(inputs))
        ],
        out_specs=jax.tree.unflatten(
            jax.tree.structure(out),
            [
                pl.BlockSpec(memory_space=pltpu.HBM if i in hbm_out else pltpu.VMEM)
                for i in range(len(jax.tree.leaves(out)))
            ],
        ),
        scratch_shapes=[
            pltpu.VMEM(x, jnp.float32) if isinstance(x, tuple) else x for x in scratch
        ],
        cost_estimate=pl.CostEstimate(flops=cost, bytes_accessed=cost, transcendentals=0),
        compiler_params=pltpu.CompilerParams(vmem_limit_bytes=limit),
    )(*inputs)


def f32(*shape):
    return jax.ShapeDtypeStruct(shape, jnp.float32)


def up_to_tile(count):
    return -(-count // TILE) * TILE


def iota(shape, dim):
    return lax.broadcasted_iota(jnp.int32, shape, dim)


def pieces_of(value):
    out = []
    for _ in range(2):
        piece = value.astype(jnp.bfloat16)
        out.append(piece)
        value = value - piece.astype(jnp.float32)
    return out + [value.astype(jnp.bfloat16)]


def select_sum(chosen, value, dim):
    flags = chosen.astype(jnp.float32).astype(jnp.bfloat16)
    return sum(
        lax.dot_general(
            flags, piece, (((dim,), (0,)), ((), ())), preferred_element_type=jnp.float32
        )
        for piece in reversed(pieces_of(value))
    )


def parity(axis="blk"):
    return lax.rem(lax.axis_index(axis), 2)


def pack_kernel(
    rho_hbm, vel_hbm, pre_hbm, route_hbm, kelvin_hbm, couple_hbm, kind_hbm, store_hbm,
    state_ref, yedge_ref, apay_ref, bpay_ref, metal_ref, wall_ref,
    rho_ref, vel_ref, pre_ref, route_ref, kind_ref, store_ref, arrived,
):
    planes, rows, lanes = rho_ref.shape
    cells = kind_ref.shape[0]
    across = wall_ref.shape[0] - 1
    face = FIELDS * HALO * rows
    copies = [
        pltpu.make_async_copy(src, dst, arrived.at[k])
        for k, (src, dst) in enumerate((
            (rho_hbm, rho_ref), (vel_hbm, vel_ref), (pre_hbm, pre_ref),
            (kelvin_hbm, metal_ref.at[0:cells]),
            (couple_hbm.at[0:3 * cells], metal_ref.at[2 * cells:5 * cells]),
            (kind_hbm, kind_ref), (store_hbm, store_ref), (route_hbm, route_ref),
        ))
    ]
    for copy in copies:
        copy.start()
    for copy in copies[:3]:
        copy.wait()
    for x in range(planes):
        rho = rho_ref[x]
        vel = [vel_ref[d, x] for d in range(3)]
        mom = [rho * v for v in vel]
        kinetic = mom[0] * vel[0] + mom[1] * vel[1] + mom[2] * vel[2]
        energy = pre_ref[x] / (gamma_gas - 1.0) + 0.5 * kinetic
        for f, value in enumerate([rho, *mom, energy]):
            state_ref[f, x] = value
    used = FIELDS * planes * HALO
    for f in range(FIELDS):
        for x in range(planes):
            at = (f * planes + x) * HALO
            yedge_ref[at:at + HALO] = state_ref[f, x, 0:HALO]
            yedge_ref[used + at:used + at + HALO] = state_ref[f, x, rows - HALO:rows]
    for odd in range(2):

        @pl.when(parity() == odd)
        def _():
            for f in range(FIELDS):
                for j in range(HALO):
                    at = (f * HALO + j) * rows
                    apay_ref[at:at + rows] = state_ref[f, j + (planes - HALO) * (1 - odd)]
                    bpay_ref[at:at + rows] = state_ref[f, j + (planes - HALO) * odd]

    for copy in copies[3:]:
        copy.wait()
    wall_ref[0:across] = metal_ref[0:across]
    wall_ref[across:across + 1] = jnp.zeros((1, lanes), jnp.float32)
    wall_ref[across:across + 1, 0:rows] = route_ref[...].astype(jnp.float32)
    kind = kind_ref[...]
    capacity = jnp.zeros((cells, lanes), jnp.float32)
    for m in range(store_ref.shape[0]):
        capacity = jnp.where(kind == m, store_ref[m], capacity)
    metal_ref[cells:2 * cells] = capacity
    metal_ref[5 * cells:5 * cells + rows] = pre_ref[0] / rho_ref[0]
    metal_ref[5 * cells + rows:5 * cells + rows + TILE] = jnp.zeros((TILE, lanes), jnp.float32)
    metal_ref[5 * cells + rows:5 * cells + rows + 1] = wall_ref[across:across + 1]
    record = 5 * cells + rows + TILE
    apay_ref[face:face + record] = metal_ref[...]


def corner_rows():
    at, out = 0, []
    for j in range(1, HALO):
        out.append((j, at, HALO - j))
        at += HALO - j
    return out, at


def edge_kernel(planes, lo_at, hi_at, starts, *refs):
    ylo_ref, yhi_ref = refs[0], refs[1]
    parts, (aedge_ref, bedge_ref) = refs[2:-2], refs[-2:]
    corners, each = corner_rows()
    for odd in range(2):

        @pl.when(parity() == odd)
        def _():
            for out, last in ((aedge_ref, odd == 0), (bedge_ref, odd == 1)):
                for f in range(FIELDS):
                    for j, first, count in corners:
                        src = (f * planes + (planes - j if last else j - 1)) * HALO
                        lo, hi = lo_at + src + HALO - count, hi_at + src
                        at = f * each + first
                        out[at:at + count] = ylo_ref[lo:lo + count]
                        at += FIELDS * each
                        out[at:at + count] = yhi_ref[hi:hi + count]

    at = 2 * FIELDS * each
    for ref, (start, count) in zip(parts, starts):
        bedge_ref[at:at + count] = ref[start:start + count]
        at += count


def far_row(f, planes, stride):
    first = HALO * stride
    row = (FIELDS + 1) * (HALO - 1) + min(f, FIELDS - 2)
    return row, first, first + planes * stride if f == FIELDS - 1 else first


def assemble_kernel(dims, lo_at, hi_at, wall_at, *refs):
    axes, across = dims
    count_blk, count_sub = axes
    state_ref, apay_ref, bpay_ref, ylo_ref, yhi_ref, aedge_ref, bedge_ref = refs[:7]
    wall_refs = refs[7:-6]
    block_ref, own_ref, inner_ref, outer_ref, table, seen = refs[-6:]
    _, planes, rows, lanes = state_ref.shape
    deep, stride = block_ref.shape[1:3]
    corners, each_corner = corner_rows()
    each = across + TILE
    blk, sub = lax.axis_index("blk"), lax.axis_index("sub")

    for f in range(FIELDS):
        for x in range(planes):
            at = (f * planes + x) * HALO
            block_ref[f, x + HALO, 0:rows] = state_ref[f, x]
            block_ref[f, x + HALO, rows:rows + HALO] = yhi_ref[hi_at + at:hi_at + at + HALO]
            block_ref[f, x + HALO, stride - HALO:stride] = ylo_ref[lo_at + at:lo_at + at + HALO]
    for odd in range(2):

        @pl.when(parity() == odd)
        def _():
            for face_ref, edge_ref, above in (
                (apay_ref, aedge_ref, odd == 0), (bpay_ref, bedge_ref, odd == 1),
            ):
                for f in range(FIELDS):
                    for j in range(HALO):
                        at = (f * HALO + j) * rows
                        x = planes + HALO + j if above else j
                        block_ref[f, x, 0:rows] = face_ref[at:at + rows]
                    for j, first, count in corners:
                        at = f * each_corner + first
                        x = planes + HALO + j - 1 if above else HALO - j
                        block_ref[f, x, stride - count:stride] = edge_ref[at:at + count]
                        at += FIELDS * each_corner
                        block_ref[f, x, rows:rows + count] = edge_ref[at:at + count]

    if wall_at is None:
        table = wall_refs[0]
    else:
        for ref, (start, flip_blk, flip_sub) in zip(wall_refs, wall_at):
            device = jnp.bitwise_xor(blk, flip_blk) * count_sub + jnp.bitwise_xor(sub, flip_sub)
            table[pl.ds(pl.multiple_of(device * each, TILE), across + 1)] = ref[
                start:start + across + 1
            ]
    devices = count_blk * count_sub
    walls = jnp.concatenate(
        [table[d * each:d * each + across] for d in range(devices)], axis=0
    )

    def facing(blk_at, sub_at):
        device = lax.rem(blk_at, count_blk) * count_sub + lax.rem(sub_at, count_sub)
        at = pl.multiple_of(device * each + across, TILE)
        routes = table[pl.ds(at, TILE)][0:1, 0:rows].astype(jnp.int32)
        return select_sum(iota((devices * across, rows), 0) == routes, walls, 0)

    block_ref[FIELDS] = jnp.zeros(block_ref.shape[1:], jnp.float32)
    for x, blk_at in ((0, blk), (planes, blk + 1)):
        below = facing(blk_at, sub + count_sub - 1)
        above = below if count_sub == 2 else facing(blk_at, sub + 1)
        seen[0:rows] = facing(blk_at, sub)
        seen[rows:] = jnp.zeros((stride - rows, lanes), jnp.float32)
        seen[rows:rows + HALO] = above[0:HALO]
        seen[stride - HALO:stride] = below[rows - HALO:rows]
        rho, mx, my, mz, energy = [block_ref[f, x + HALO] for f in range(FIELDS)]
        pressure = (gamma_gas - 1.0) * (energy - 0.5 * (mx * mx + my * my + mz * mz) / rho)
        block_ref[FIELDS, x + HALO] = film_coeff * (pressure / rho - seen[...])
    pick = iota((2 * TILE, lanes), 0)
    cell = iota((2 * TILE, lanes), 1)
    chosen = (
        ((pick == cell) & (pick < NEAR))
        | ((pick - TILE + lanes - NEAR == cell) & (pick >= TILE) & (pick < TILE + NEAR))
    ).astype(jnp.float32).astype(jnp.bfloat16)
    size = deep * stride
    upper = parity("grp") == 1
    for f in range(FIELDS + 1):
        ends = sum(
            lax.dot_general(
                chosen, piece, (((1,), (1,)), ((), ())), preferred_element_type=jnp.float32
            )
            for piece in reversed(pieces_of(block_ref[f].reshape(size, lanes)))
        )
        own_ref[f * 2 * TILE:(f + 1) * 2 * TILE, 0:size] = ends
        low, high = ends[0:HALO], ends[TILE + NEAR - HALO:TILE + NEAR]
        at = slice(f * (HALO - 1), (f + 1) * (HALO - 1))
        inner_ref[at, 0:size] = jnp.where(upper, low[:-1], high[1:])
        outer_ref[at, 0:size] = jnp.where(upper, high[1:], low[:-1])
        if f == FIELDS:
            continue
        inner, outer = jnp.where(upper, low[-1:], high[:1]), jnp.where(upper, high[:1], low[-1:])
        for ref, value in ((inner_ref, inner), (outer_ref, outer)):
            row, first, there = far_row(f, planes, stride)
            ref[row:row + 1, there:there + planes * stride] = value[
                :, first:first + planes * stride
            ]
    if own_ref.shape[1] > size:
        own_ref[:, size:] = jnp.zeros((own_ref.shape[0], own_ref.shape[1] - size), jnp.float32)


def primitives(u):
    rho, mx, my, mz, energy = u
    inverse = 1.0 / rho
    ux, uy, uz = mx * inverse, my * inverse, mz * inverse
    pressure = (gamma_gas - 1.0) * (energy - 0.5 * (mx * ux + my * uy + mz * uz))
    sound = jnp.sqrt(gamma_gas * pressure * inverse)
    return [
        ux, uy, uz, jnp.abs(ux) + sound, jnp.abs(uy) + sound, jnp.abs(uz) + sound,
        pressure, energy + pressure,
    ]


def faces(d, lo, hi):
    def flux(v):
        speed, pressure, enthalpy = v[5], v[7], v[8]
        f = [v[1 + d]] + [v[1 + i] * speed for i in range(3)] + [enthalpy * speed]
        f[1 + d] = f[1 + d] + pressure
        return f

    below, here = flux(lo), flux(hi)
    fast = jnp.maximum(lo[6], hi[6])
    slow = fast + 2.0 * viscosity
    return [
        (below[i] + here[i]) - (fast if i == 0 else slow) * (hi[i] - lo[i]) for i in range(5)
    ]


def advance(stage, old, change, start, sink):
    fresh = old - (0.5 * time_step) * change
    if sink is not None:
        fresh = fresh - time_step * sink
    if stage == 0:
        return fresh
    if stage == 1:
        return 0.75 * start + 0.25 * fresh
    return third_part * start + two_thirds * fresh


def planes_kernel(block_ref, out_ref, now, prim, xface):
    deep, _, _ = block_ref.shape[1:]
    rows = out_ref.shape[2]
    for stage in range(3):
        src = block_ref if stage == 0 else now
        low, high = stage + 1, deep - 1 - stage
        for x in range(low - 1, high + 1):
            for k, value in enumerate(primitives([src[f, x] for f in range(FIELDS)])):
                prim[k, x] = value

        def cells(x, d, src=src):
            return [src[f, x] for f in range(FIELDS)] + [
                prim[d, x], prim[3 + d, x], prim[6, x], prim[7, x]
            ]

        for x in range(low, high + 1):
            new = faces(0, cells(x - 1, 0), cells(x, 0))
            for f in range(FIELDS):
                xface[x % 2, f] = new[f]
            if x == low:
                continue
            p = x - 1
            change = [new[f] - xface[p % 2, f] for f in range(FIELDS)]
            for d, axis in ((1, 0), (2, 1)):
                hi = cells(p, d)
                lo = [pltpu.roll(v, 1, axis=axis) for v in hi]
                face = faces(d, lo, hi)
                last = hi[0].shape[axis] - 1
                change = [c + (pltpu.roll(v, last, axis=axis) - v) for c, v in zip(change, face)]
            for f in range(FIELDS):
                sink = block_ref[FIELDS, p] if f == FIELDS - 1 else None
                value = advance(stage, src[f, p], change[f], block_ref[f, p], sink)
                if stage == 2:
                    out_ref[f, p - HALO] = value[0:rows]
                else:
                    now[f, p] = value


def ends_kernel(
    stride, main_ref, own_ref, inner_ref, outer_ref, out_ref, slab_base, base, slab, comb
):
    _, planes, rows, lanes = out_ref.shape
    deep = planes + 2 * HALO
    wide = slab_base.shape[2]
    half = slab_base.shape[1] // 2
    part = FIELDS * TILE
    source = iota((lanes, FIELDS * lanes), 0)
    target = iota((lanes, FIELDS * lanes), 1)
    field = lax.rem(source, part) // TILE
    end = lax.rem(source, TILE)
    spread = (
        ((end < HALO) & (target == field * lanes + end))
        | (
            (end >= HALO) & (end < 2 * HALO)
            & (target == field * lanes + lanes - 2 * HALO + end)
        )
    ) & (source < 3 * part)
    spread = spread.astype(jnp.float32).astype(jnp.bfloat16)
    comb[...] = jnp.zeros(comb.shape, jnp.float32)
    slab_base[...] = jnp.zeros(slab_base.shape, jnp.float32)
    upper = parity("grp") == 1
    for f in range(FIELDS + 1):
        at = slice(f * (HALO - 1), (f + 1) * (HALO - 1))
        inner, outer = inner_ref[at], outer_ref[at]
        slab_base[f, 1:HALO] = jnp.where(upper, inner, outer)
        slab_base[f, half + NEAR:half + NEAR + HALO - 1] = jnp.where(upper, outer, inner)
        at = f * 2 * TILE
        slab_base[f, HALO:HALO + NEAR] = own_ref[at:at + NEAR]
        slab_base[f, half:half + NEAR] = own_ref[at + TILE:at + TILE + NEAR]
        if f == FIELDS:
            continue
        row, first, there = far_row(f, planes, stride)
        inner, outer = inner_ref[row:row + 1], outer_ref[row:row + 1]
        if there != first:
            inner, outer = (pltpu.roll(v, wide + first - there, axis=1) for v in (inner, outer))
        slab_base[f, 0:1] = jnp.where(upper, inner, outer)
        last = half + NEAR + HALO - 1
        slab_base[f, last:last + 1] = jnp.where(upper, outer, inner)

    narrow = min(wide, -(-(deep - 1) * stride // lanes) * lanes)
    kept = NEAR + HALO - 2
    start = slab_base
    for stage in range(3):
        src = slab_base if stage == 0 else slab
        u = [src[f] for f in range(FIELDS)]
        tall, width = u[0].shape
        first_row = lax.rem(iota((tall, width), 1), stride) == 0
        last_row = lax.rem(iota((tall, width), 1), stride) == stride - 1

        def lane_roll(v, shift, width=width):
            return pltpu.roll(v, shift % width, axis=1)

        q = primitives(u)
        hi = u + [q[2], q[5], q[6], q[7]]
        face = faces(2, [pltpu.roll(v, 1, axis=0) for v in hi], hi)
        change = [pltpu.roll(v, tall - 1, axis=0) - v for v in face]
        hi = u + [q[0], q[3], q[6], q[7]]
        face = faces(0, [lane_roll(v, stride) for v in hi], hi)
        change = [c + (lane_roll(v, -stride) - v) for c, v in zip(change, face)]
        hi = u + [q[1], q[4], q[6], q[7]]
        lo = [jnp.where(first_row, lane_roll(v, 1 - stride), lane_roll(v, 1)) for v in hi]
        face = faces(1, lo, hi)
        change = [
            c + (jnp.where(last_row, lane_roll(v, stride - 1), lane_roll(v, -1)) - v)
            for c, v in zip(change, face)
        ]
        for f in range(FIELDS):
            sink = start[FIELDS] if f == FIELDS - 1 else None
            value = advance(stage, u[f], change[f], start[f], sink)
            if stage:
                slab[f] = value
                continue
            for group in range(2):
                slab[f, group * TILE:group * TILE + kept] = value[
                    group * half + 1:group * half + 1 + kept, 0:narrow
                ]
                slab[f, group * TILE + kept:(group + 1) * TILE] = jnp.zeros(
                    (TILE - kept, narrow), jnp.float32
                )
        if stage == 0:
            for f in range(FIELDS + 1):
                for group in range(2):
                    base[f, group * TILE:group * TILE + kept] = slab_base[
                        f, group * half + 1:group * half + 1 + kept, 0:narrow
                    ]
                    base[f, group * TILE + kept:(group + 1) * TILE] = jnp.zeros(
                        (TILE - kept, narrow), jnp.float32
                    )
            start = base

    for f in range(FIELDS):
        first = HALO - 1
        comb[f * TILE:f * TILE + HALO, 0:narrow] = slab[f, first:first + HALO]
        first = TILE + NEAR - HALO - 1
        comb[f * TILE + HALO:f * TILE + 2 * HALO, 0:narrow] = slab[f, first:first + HALO]
    whole = comb[0:part]
    for k in range(2):
        piece = whole.astype(jnp.bfloat16).astype(jnp.float32)
        comb[k * part:(k + 1) * part] = piece
        whole = whole - piece
    comb[2 * part:3 * part] = whole
    turned = jnp.transpose(comb[...]).astype(jnp.bfloat16)
    moved = lax.dot_general(
        turned[HALO * stride:(HALO + planes) * stride], spread, (((1,), (0,)), ((), ())),
        preferred_element_type=jnp.float32,
    )
    lane = iota((rows, lanes), 1)
    near = (lane < HALO) | (lane >= lanes - HALO)
    for f in range(FIELDS):
        for x in range(planes):
            edge = moved[x * stride:x * stride + rows, f * lanes:(f + 1) * lanes]
            out_ref[f, x] = jnp.where(near, edge, main_ref[f, x])


def metal_kernel(dims, rows, where, order, *refs):
    fluid_ref, fluid_hbm, written = refs[-20], refs[-18], refs[-1]
    refs = (*refs[:-20], refs[-19], *refs[-17:-1])
    leave = pltpu.make_async_copy(fluid_ref, fluid_hbm, written)
    leave.start()
    count_blk, count_sub, along, across = dims
    devices = count_blk * count_sub
    pieces = [(refs[k], start) for k, start in where]
    (
        out_ref, sol, kelvin, res, dirn, drift, image, diag, cx, cy, cz, cyu, czu, caps, heat,
        route, faced,
    ) = refs[-17:]
    lanes = out_ref.shape[-1]
    cells = along * across
    wide = count_sub * across
    deep = count_blk * along
    blk, sub = lax.axis_index("blk"), lax.axis_index("sub")
    mine = blk * along
    side = pl.multiple_of(sub * across, TILE)

    zero = jnp.zeros((wide, lanes), jnp.float32)
    for ref in (kelvin, res, cx):
        ref[0] = zero
        ref[deep + 1] = zero

    for n, ((ref, first), (flip_blk, flip_sub)) in enumerate(zip(pieces, order)):
        b = jnp.bitwise_xor(blk, flip_blk) * along
        y = pl.multiple_of(jnp.bitwise_xor(sub, flip_sub) * across, TILE)
        for field, (dest, shift) in enumerate(((kelvin, 1), (caps, 0), (cx, 1), (cy, 0), (cz, 0))):
            start = first + field * cells
            dest[pl.ds(b + shift, along), pl.ds(y, across)] = ref[
                start:start + cells
            ].reshape(along, across, lanes)
        start = first + 5 * cells
        faced[n * rows:(n + 1) * rows] = ref[start:start + rows]
        route[:, n * rows:(n + 1) * rows] = ref[start + rows:start + rows + TILE][:, 0:rows]

    walls = jnp.concatenate([kelvin[1 + b * along] for b in range(count_blk)], axis=0)
    strips = devices * across
    chosen = iota((strips, devices * rows), 0) == route[0:1].astype(jnp.int32)
    flux = film_coeff * (faced[...] - select_sum(chosen, walls, 0))
    heat[...] = select_sum(chosen, flux, 1)

    chunk = math.gcd(deep, max(1, ROWS // wide))
    none = jnp.zeros((TILE, lanes), jnp.float32)

    def sweep(body, init):
        return lax.fori_loop(0, deep // chunk, lambda i, c: body(i * chunk, c), init)

    def fold(value):
        return jnp.sum(value.reshape(-1, TILE, lanes), axis=0)

    def total(value):
        one = jnp.sum(jnp.sum(value, axis=0, keepdims=True), axis=1, keepdims=True)
        return jnp.broadcast_to(one, (TILE, lanes))

    def times(factor, value):
        return (factor * value.reshape(-1, TILE, lanes)).reshape(value.shape)

    def turned(v, step, axis):
        return pltpu.roll(v, step % v.shape[axis], axis=axis)

    def prepare(x, carry):
        here, own = pl.ds(x, chunk), pl.ds(x + 1, chunk)
        ups = cx[pl.ds(x + 2, chunk)], turned(cy[here], -1, 1), turned(cz[here], -1, 2)
        cyu[here] = ups[1]
        czu[here] = ups[2]
        diag[here] = caps[here] + ((cx[own] + ups[0]) + (cy[here] + ups[1]) + (cz[here] + ups[2]))
        v = kelvin[own]
        res[own] = (
            cx[own] * (kelvin[pl.ds(x, chunk)] - v)
            + ups[0] * (kelvin[pl.ds(x + 2, chunk)] - v)
            + (cy[here] * (turned(v, 1, 1) - v) + ups[1] * (turned(v, -1, 1) - v))
            + (cz[here] * (turned(v, 1, 2) - v) + ups[2] * (turned(v, -1, 2) - v))
        )
        return carry

    sweep(prepare, 0)
    for b in range(count_blk):
        at = b * along + 1
        res[at] = res[at] + heat[b * wide:(b + 1) * wide]

    def apply(x, sums):
        here, own = pl.ds(x, chunk), pl.ds(x + 1, chunk)
        v = res[own]
        value = (
            diag[here] * v
            - (cx[own] * res[pl.ds(x, chunk)] + cx[pl.ds(x + 2, chunk)] * res[pl.ds(x + 2, chunk)])
            - (cy[here] * turned(v, 1, 1) + cyu[here] * turned(v, -1, 1))
            - (cz[here] * turned(v, 1, 2) + czu[here] * turned(v, -1, 2))
        )
        image[here] = value
        return sums[0] + fold(v * v), sums[1] + fold(v * value)

    mine_at = pl.ds(mine, along), pl.ds(side, across)
    sol[...] = kelvin[pl.ds(mine + 1, along), pl.ds(side, across)]
    norm = alpha = beta = None
    for step in range(ITERS):
        fresh, product = (total(v) for v in sweep(apply, (none, none)))
        if step == 0:
            alpha = fresh / product
        else:
            beta = fresh / norm
            alpha = fresh / (product - beta * fresh / alpha)
        norm = fresh
        if step + 1 == ITERS:
            towards = res[pl.ds(mine + 1, along), pl.ds(side, across)] + times(beta, dirn[mine_at])
            out_ref[...] = sol[...] + times(alpha, towards)
            leave.wait()
            break

        def update(x, carry, step=step, alpha=alpha, beta=beta):
            here, own = pl.ds(x, chunk), pl.ds(x + 1, chunk)
            towards, moved = res[own], image[here]
            if step:
                towards = towards + times(beta, dirn[here])
                moved = moved + times(beta, drift[here])
            dirn[here] = towards
            drift[here] = moved
            res[own] = res[own] - times(alpha, moved)
            return carry

        sweep(update, 0)
        sol[...] = sol[...] + times(alpha, dirn[mine_at])


def swap(value, axis, flip):
    count = lax.axis_size(axis)
    return lax.ppermute(value, axis, [(i, i ^ flip) for i in range(count)])


def outer(value, axis="blk"):
    count = lax.axis_size(axis)
    pairs = [(i, (i + 1 if i % 2 else i - 1) % count) for i in range(count)]
    return lax.ppermute(value, axis, pairs)


def ring(value, axis, step):
    count = lax.axis_size(axis)
    return lax.ppermute(value, axis, [(i, (i + step) % count) for i in range(count)])


def flips(count):
    return [1 << k for k in reversed(range((count - 1).bit_length()))]


def shards(
    mass_per_volume,
    flow_speed_vector,
    normal_stress,
    facing_strip_index,
    solid_kelvin,
    face_coupling,
    substance_index,
    substance_storage,
):
    planes, rows, lanes = mass_per_volume.shape
    along, across, _ = solid_kelvin.shape
    count_blk, count_sub = lax.axis_size("blk"), lax.axis_size("sub")
    devices = count_blk * count_sub
    cells = along * across
    edge = FIELDS * planes * HALO
    each = across + 1
    record = 5 * cells + rows + TILE

    face = FIELDS * HALO * rows
    state, yedge, apay, bpay, metal, wall = call(
        pack_kernel,
        [
            f32(FIELDS, planes, rows, lanes), f32(2 * edge, lanes),
            f32(face + record, lanes), f32(face, lanes),
            f32(record, lanes), f32(each, lanes),
        ],
        [
            mass_per_volume, flow_speed_vector, normal_stress,
            facing_strip_index.reshape(1, rows), solid_kelvin.reshape(cells, lanes),
            face_coupling.reshape(6 * cells, lanes), substance_index.reshape(cells, lanes),
            substance_storage,
        ],
        hbm=tuple(range(8)),
        scratch=[
            (planes, rows, lanes), (3, planes, rows, lanes), (planes, rows, lanes),
            pltpu.VMEM((1, rows), jnp.int32), pltpu.VMEM((cells, lanes), jnp.int32),
            pltpu.SMEM(substance_storage.shape, jnp.float32), pltpu.SemaphoreType.DMA((8,)),
        ],
    )
    paired = count_blk == 4 and count_sub == 2
    span = FIELDS * corner_rows()[1]
    bpay = outer(bpay)
    if paired:
        wall_a = swap(wall, "blk", 1)
        ypay = jnp.concatenate([yedge, wall, wall_a], axis=0)
        yrecv = swap(ypay, "sub", 1)
        ylo, yhi, lo_at, hi_at = yrecv, yrecv, edge, 0
        parts = [wall, wall_a, yrecv]
        starts = [(0, each), (0, each), (2 * edge, 2 * each)]
    else:
        ylo, yhi, lo_at, hi_at = ring(yedge[edge:], "sub", 1), ring(yedge[:edge], "sub", -1), 0, 0
        parts, starts = [], []
    apay = swap(apay, "blk", 1)
    aedge, bedge = call(
        functools.partial(edge_kernel, planes, lo_at, hi_at, starts),
        [f32(2 * span, lanes), f32(2 * span + sum(c for _, c in starts), lanes)],
        [ylo, yhi, *parts],
    )
    bedge = outer(bedge)
    aedge = swap(aedge, "blk", 1)
    if paired:
        walls = [wall, wall_a, yrecv, yrecv] + 4 * [bedge]
        wall_at = [(0, 0, 0), (0, 1, 0), (2 * edge, 0, 1), (2 * edge + each, 1, 1)]
        wall_at += [(2 * span + k * each, 3 ^ (k & 1), k >> 1) for k in range(4)]
    else:
        wall = jnp.pad(wall, ((0, across + TILE - each), (0, 0)))
        walls = [lax.all_gather(wall, ("blk", "sub"), axis=0, tiled=True)]
        wall_at = None
    deep, stride = planes + 2 * HALO, rows + TILE
    ends_rows = up_to_tile((FIELDS + 1) * (HALO - 1) + FIELDS - 1)
    wide_lanes = -(-deep * stride // lanes) * lanes
    block, own_z, inner_z, outer_z = call(
        functools.partial(
            assemble_kernel, ((count_blk, count_sub), across), lo_at, hi_at, wall_at
        ),
        [
            f32(FIELDS + 1, deep, stride, lanes),
            f32((FIELDS + 1) * 2 * TILE, wide_lanes),
            f32(ends_rows, wide_lanes),
            f32(ends_rows, wide_lanes),
        ],
        [state, apay, bpay, ylo, yhi, aedge, bedge, *walls],
        scratch=[(devices * (across + TILE), lanes), (stride, lanes)],
    )
    inner_got = swap(inner_z, "grp", 1)
    outer_got = outer(outer_z, "grp")
    planes_next = call(
        planes_kernel,
        f32(FIELDS, planes, rows, lanes),
        [block],
        scratch=[
            (FIELDS, deep, stride, lanes), (8, deep, stride, lanes), (2, FIELDS, stride, lanes)
        ],
    )

    if paired:
        near_y = swap(metal, "sub", 1)
        far = swap(metal, "blk", 2)
        far_y = swap(near_y, "blk", 2)
        mates = swap(jnp.concatenate([near_y, far, far_y], axis=0), "blk", 1)
        pieces = [metal, apay, near_y, far, far_y, mates]
        where = [(0, 0), (1, face), (2, 0), (3, 0), (4, 0)] + [(5, k * record) for k in range(3)]
        order = [(0, 0), (1, 0), (0, 1), (2, 0), (2, 1), (1, 1), (3, 0), (3, 1)]
    else:
        held, order = metal, [(0, 0)]
        steps = [("blk", flip) for flip in flips(count_blk)]
        steps += [("sub", flip) for flip in flips(count_sub)]
        for axis, flip in steps:
            held = jnp.concatenate([held, swap(held, axis, flip)], axis=0)
            order = order + [
                (b ^ flip, s) if axis == "blk" else (b, s ^ flip) for b, s in order
            ]
        pieces, where = [held], [(0, k * record) for k in range(devices)]
    wide = count_sub * across
    deep_metal = count_blk * along
    field = (deep_metal, wide, lanes)
    padded = (deep_metal + 2, wide, lanes)
    slab = 2 * -(-(NEAR + HALO) // (TILE // 2)) * (TILE // 2)
    narrow = min(wide_lanes, -(-(deep - 1) * stride // lanes) * lanes)
    fluid = call(
        functools.partial(ends_kernel, stride),
        f32(FIELDS, planes, rows, lanes),
        [planes_next, own_z, inner_got, outer_got],
        scratch=[
            (FIELDS + 1, slab, wide_lanes), (FIELDS + 1, 2 * TILE, narrow),
            (FIELDS, 2 * TILE, narrow), (lanes, wide_lanes),
        ],
    )
    metal_next, fluid_next = call(
        functools.partial(
            metal_kernel, (count_blk, count_sub, along, across), rows, where, order
        ),
        [f32(along, across, lanes), f32(FIELDS, planes, rows, lanes)],
        [*pieces, fluid],
        hbm_out=(1,),
        scratch=[
            (along, across, lanes), padded, padded, field, field, field, field, padded, field,
            field, field, field, field, (devices * across, lanes), (TILE, devices * rows), (devices * rows, lanes),
            pltpu.SemaphoreType.DMA,
        ],
    )
    return (fluid_next, metal_next)


def solution(mesh):
    in_specs = (
        P("blk", "sub", "grp"),
        P(None, "blk", "sub", "grp"),
        P("blk", "sub", "grp"),
        P("grp", "blk", "sub"),
        P("blk", "sub", "grp"),
        P(None, "blk", "sub", "grp"),
        P("blk", "sub", "grp"),
        P(),
    )
    out_specs = (P(None, "blk", "sub", "grp"), P("blk", "sub", "grp"))
    return jax.shard_map(shards, mesh=mesh, in_specs=in_specs, out_specs=out_specs, check_vma=False)
```

```python
import functools
import math

import jax
import jax.numpy as jnp
from jax import lax
from jax.experimental import pallas as pl
from jax.experimental.pallas import tpu as pltpu
from jax.sharding import PartitionSpec as P


ITERS = 4
HALO = 3
TILE = 8
FIELDS = 5
NEAR = 2 * HALO
ROWS = 512

gamma_gas = 1.4
time_step = 0.1
viscosity = 0.05
film_coeff = 1.0
third_part = 1.0 / 3.0
two_thirds = 2.0 / 3.0

SPARE_BYTES = 6 * 1024 * 1024


def bytes_of(shapes):
    total = 0
    for shape in shapes:
        *lead, rows, lanes = (1, 1, *shape)
        total += 4 * math.prod(lead) * up_to_tile(rows) * (-(-lanes // 128) * 128)
    return total


def call(body, out, inputs, hbm=(), hbm_out=(), cost=100_000, scratch=()):
    inputs = [
        pltpu.with_memory_space_constraint(x, pltpu.HBM) if i in hbm else x
        for i, x in enumerate(inputs)
    ]
    limit = SPARE_BYTES + bytes_of(
        [x.shape for i, x in enumerate(inputs) if i not in hbm]
        + [x.shape for x in jax.tree.leaves(out)]
        + [x for x in scratch if isinstance(x, tuple)]
    )
    return pl.pallas_call(
        body,
        out_shape=out,
        in_specs=[
            pl.BlockSpec(memory_space=pltpu.HBM if i in hbm else pltpu.VMEM)
            for i in range(len(inputs))
        ],
        out_specs=jax.tree.unflatten(
            jax.tree.structure(out),
            [
                pl.BlockSpec(memory_space=pltpu.HBM if i in hbm_out else pltpu.VMEM)
                for i in range(len(jax.tree.leaves(out)))
            ],
        ),
        scratch_shapes=[
            pltpu.VMEM(x, jnp.float32) if isinstance(x, tuple) else x for x in scratch
        ],
        cost_estimate=pl.CostEstimate(flops=cost, bytes_accessed=cost, transcendentals=0),
        compiler_params=pltpu.CompilerParams(vmem_limit_bytes=limit),
    )(*inputs)


def f32(*shape):
    return jax.ShapeDtypeStruct(shape, jnp.float32)


def up_to_tile(count):
    return -(-count // TILE) * TILE


def iota(shape, dim):
    return lax.broadcasted_iota(jnp.int32, shape, dim)


def pieces_of(value):
    out = []
    for _ in range(2):
        piece = value.astype(jnp.bfloat16)
        out.append(piece)
        value = value - piece.astype(jnp.float32)
    return out + [value.astype(jnp.bfloat16)]


def select_sum(chosen, value, dim):
    flags = chosen.astype(jnp.float32).astype(jnp.bfloat16)
    return sum(
        lax.dot_general(
            flags, piece, (((dim,), (0,)), ((), ())), preferred_element_type=jnp.float32
        )
        for piece in reversed(pieces_of(value))
    )


def parity(axis="blk"):
    return lax.rem(lax.axis_index(axis), 2)


def pack_kernel(
    rho_hbm, vel_hbm, pre_hbm, route_hbm, kelvin_hbm, couple_hbm, kind_hbm, store_hbm,
    state_ref, yedge_ref, apay_ref, bpay_ref, metal_ref, wall_ref,
    rho_ref, vel_ref, pre_ref, route_ref, kind_ref, store_ref, arrived,
):
    planes, rows, lanes = rho_ref.shape
    cells = kind_ref.shape[0]
    across = wall_ref.shape[0] - 1
    face = FIELDS * HALO * rows
    copies = [
        pltpu.make_async_copy(src, dst, arrived.at[k])
        for k, (src, dst) in enumerate((
            (rho_hbm, rho_ref), (vel_hbm, vel_ref), (pre_hbm, pre_ref),
            (kelvin_hbm, metal_ref.at[0:cells]),
            (couple_hbm.at[0:3 * cells], metal_ref.at[2 * cells:5 * cells]),
            (kind_hbm, kind_ref), (store_hbm, store_ref), (route_hbm, route_ref),
        ))
    ]
    for copy in copies:
        copy.start()
    for copy in copies[:3]:
        copy.wait()
    for x in range(planes):
        rho = rho_ref[x]
        vel = [vel_ref[d, x] for d in range(3)]
        mom = [rho * v for v in vel]
        kinetic = mom[0] * vel[0] + mom[1] * vel[1] + mom[2] * vel[2]
        energy = pre_ref[x] / (gamma_gas - 1.0) + 0.5 * kinetic
        for f, value in enumerate([rho, *mom, energy]):
            state_ref[f, x] = value
    used = FIELDS * planes * HALO
    for f in range(FIELDS):
        for x in range(planes):
            at = (f * planes + x) * HALO
            yedge_ref[at:at + HALO] = state_ref[f, x, 0:HALO]
            yedge_ref[used + at:used + at + HALO] = state_ref[f, x, rows - HALO:rows]
    for odd in range(2):

        @pl.when(parity() == odd)
        def _():
            for f in range(FIELDS):
                for j in range(HALO):
                    at = (f * HALO + j) * rows
                    apay_ref[at:at + rows] = state_ref[f, j + (planes - HALO) * (1 - odd)]
                    bpay_ref[at:at + rows] = state_ref[f, j + (planes - HALO) * odd]

    for copy in copies[3:]:
        copy.wait()
    wall_ref[0:across] = metal_ref[0:across]
    wall_ref[across:across + 1] = jnp.zeros((1, lanes), jnp.float32)
    wall_ref[across:across + 1, 0:rows] = route_ref[...].astype(jnp.float32)
    kind = kind_ref[...]
    capacity = jnp.zeros((cells, lanes), jnp.float32)
    for m in range(store_ref.shape[0]):
        capacity = jnp.where(kind == m, store_ref[m], capacity)
    metal_ref[cells:2 * cells] = capacity
    metal_ref[5 * cells:5 * cells + rows] = pre_ref[0] / rho_ref[0]
    metal_ref[5 * cells + rows:5 * cells + rows + TILE] = jnp.zeros((TILE, lanes), jnp.float32)
    metal_ref[5 * cells + rows:5 * cells + rows + 1] = wall_ref[across:across + 1]
    record = 5 * cells + rows + TILE
    apay_ref[face:face + record] = metal_ref[...]


def corner_rows():
    at, out = 0, []
    for j in range(1, HALO):
        out.append((j, at, HALO - j))
        at += HALO - j
    return out, at


def edge_kernel(planes, lo_at, hi_at, starts, *refs):
    ylo_ref, yhi_ref = refs[0], refs[1]
    parts, (aedge_ref, bedge_ref) = refs[2:-2], refs[-2:]
    corners, each = corner_rows()
    for odd in range(2):

        @pl.when(parity() == odd)
        def _():
            for out, last in ((aedge_ref, odd == 0), (bedge_ref, odd == 1)):
                for f in range(FIELDS):
                    for j, first, count in corners:
                        src = (f * planes + (planes - j if last else j - 1)) * HALO
                        lo, hi = lo_at + src + HALO - count, hi_at + src
                        at = f * each + first
                        out[at:at + count] = ylo_ref[lo:lo + count]
                        at += FIELDS * each
                        out[at:at + count] = yhi_ref[hi:hi + count]

    at = 2 * FIELDS * each
    for ref, (start, count) in zip(parts, starts):
        bedge_ref[at:at + count] = ref[start:start + count]
        at += count


def far_row(f, planes, stride):
    first = HALO * stride
    row = (FIELDS + 1) * (HALO - 1) + min(f, FIELDS - 2)
    return row, first, first + planes * stride if f == FIELDS - 1 else first


def assemble_kernel(dims, lo_at, hi_at, wall_at, *refs):
    axes, across = dims
    count_blk, count_sub = axes
    state_ref, apay_ref, bpay_ref, ylo_ref, yhi_ref, aedge_ref, bedge_ref = refs[:7]
    wall_refs = refs[7:-6]
    block_ref, own_ref, inner_ref, outer_ref, table, seen = refs[-6:]
    _, planes, rows, lanes = state_ref.shape
    deep, stride = block_ref.shape[1:3]
    corners, each_corner = corner_rows()
    each = across + TILE
    blk, sub = lax.axis_index("blk"), lax.axis_index("sub")

    for f in range(FIELDS):
        for x in range(planes):
            at = (f * planes + x) * HALO
            block_ref[f, x + HALO, 0:rows] = state_ref[f, x]
            block_ref[f, x + HALO, rows:rows + HALO] = yhi_ref[hi_at + at:hi_at + at + HALO]
            block_ref[f, x + HALO, stride - HALO:stride] = ylo_ref[lo_at + at:lo_at + at + HALO]
    for odd in range(2):

        @pl.when(parity() == odd)
        def _():
            for face_ref, edge_ref, above in (
                (apay_ref, aedge_ref, odd == 0), (bpay_ref, bedge_ref, odd == 1),
            ):
                for f in range(FIELDS):
                    for j in range(HALO):
                        at = (f * HALO + j) * rows
                        x = planes + HALO + j if above else j
                        block_ref[f, x, 0:rows] = face_ref[at:at + rows]
                    for j, first, count in corners:
                        at = f * each_corner + first
                        x = planes + HALO + j - 1 if above else HALO - j
                        block_ref[f, x, stride - count:stride] = edge_ref[at:at + count]
                        at += FIELDS * each_corner
                        block_ref[f, x, rows:rows + count] = edge_ref[at:at + count]

    if wall_at is None:
        table = wall_refs[0]
    else:
        for ref, (start, flip_blk, flip_sub) in zip(wall_refs, wall_at):
            device = jnp.bitwise_xor(blk, flip_blk) * count_sub + jnp.bitwise_xor(sub, flip_sub)
            table[pl.ds(pl.multiple_of(device * each, TILE), across + 1)] = ref[
                start:start + across + 1
            ]
    devices = count_blk * count_sub
    walls = jnp.concatenate(
        [table[d * each:d * each + across] for d in range(devices)], axis=0
    )

    def facing(blk_at, sub_at):
        device = lax.rem(blk_at, count_blk) * count_sub + lax.rem(sub_at, count_sub)
        at = pl.multiple_of(device * each + across, TILE)
        routes = table[pl.ds(at, TILE)][0:1, 0:rows].astype(jnp.int32)
        return select_sum(iota((devices * across, rows), 0) == routes, walls, 0)

    block_ref[FIELDS] = jnp.zeros(block_ref.shape[1:], jnp.float32)
    for x, blk_at in ((0, blk), (planes, blk + 1)):
        below = facing(blk_at, sub + count_sub - 1)
        above = below if count_sub == 2 else facing(blk_at, sub + 1)
        seen[0:rows] = facing(blk_at, sub)
        seen[rows:] = jnp.zeros((stride - rows, lanes), jnp.float32)
        seen[rows:rows + HALO] = above[0:HALO]
        seen[stride - HALO:stride] = below[rows - HALO:rows]
        rho, mx, my, mz, energy = [block_ref[f, x + HALO] for f in range(FIELDS)]
        pressure = (gamma_gas - 1.0) * (energy - 0.5 * (mx * mx + my * my + mz * mz) / rho)
        block_ref[FIELDS, x + HALO] = film_coeff * (pressure / rho - seen[...])
    pick = iota((2 * TILE, lanes), 0)
    cell = iota((2 * TILE, lanes), 1)
    chosen = (
        ((pick == cell) & (pick < NEAR))
        | ((pick - TILE + lanes - NEAR == cell) & (pick >= TILE) & (pick < TILE + NEAR))
    ).astype(jnp.float32).astype(jnp.bfloat16)
    size = deep * stride
    upper = parity("grp") == 1
    for f in range(FIELDS + 1):
        ends = sum(
            lax.dot_general(
                chosen, piece, (((1,), (1,)), ((), ())), preferred_element_type=jnp.float32
            )
            for piece in reversed(pieces_of(block_ref[f].reshape(size, lanes)))
        )
        own_ref[f * 2 * TILE:(f + 1) * 2 * TILE, 0:size] = ends
        low, high = ends[0:HALO], ends[TILE + NEAR - HALO:TILE + NEAR]
        at = slice(f * (HALO - 1), (f + 1) * (HALO - 1))
        inner_ref[at, 0:size] = jnp.where(upper, low[:-1], high[1:])
        outer_ref[at, 0:size] = jnp.where(upper, high[1:], low[:-1])
        if f == FIELDS:
            continue
        inner, outer = jnp.where(upper, low[-1:], high[:1]), jnp.where(upper, high[:1], low[-1:])
        for ref, value in ((inner_ref, inner), (outer_ref, outer)):
            row, first, there = far_row(f, planes, stride)
            ref[row:row + 1, there:there + planes * stride] = value[
                :, first:first + planes * stride
            ]
    if own_ref.shape[1] > size:
        own_ref[:, size:] = jnp.zeros((own_ref.shape[0], own_ref.shape[1] - size), jnp.float32)


def primitives(u):
    rho, mx, my, mz, energy = u
    inverse = 1.0 / rho
    ux, uy, uz = mx * inverse, my * inverse, mz * inverse
    pressure = (gamma_gas - 1.0) * (energy - 0.5 * (mx * ux + my * uy + mz * uz))
    sound = jnp.sqrt(gamma_gas * pressure * inverse)
    return [
        ux, uy, uz, jnp.abs(ux) + sound, jnp.abs(uy) + sound, jnp.abs(uz) + sound,
        pressure, energy + pressure,
    ]


def faces(d, lo, hi):
    def flux(v):
        speed, pressure, enthalpy = v[5], v[7], v[8]
        f = [v[1 + d]] + [v[1 + i] * speed for i in range(3)] + [enthalpy * speed]
        f[1 + d] = f[1 + d] + pressure
        return f

    below, here = flux(lo), flux(hi)
    fast = jnp.maximum(lo[6], hi[6])
    slow = fast + 2.0 * viscosity
    return [
        (below[i] + here[i]) - (fast if i == 0 else slow) * (hi[i] - lo[i]) for i in range(5)
    ]


def advance(stage, old, change, start, sink):
    fresh = old - (0.5 * time_step) * change
    if sink is not None:
        fresh = fresh - time_step * sink
    if stage == 0:
        return fresh
    if stage == 1:
        return 0.75 * start + 0.25 * fresh
    return third_part * start + two_thirds * fresh


def planes_kernel(block_ref, out_ref, now, prim, xface):
    deep, stride, lanes = block_ref.shape[1:]
    rows = out_ref.shape[2]
    for stage in range(3):
        src = block_ref if stage == 0 else now
        low, high = stage + 1, deep - 1 - stage
        for x in range(low - 1, high + 1):
            for k, value in enumerate(primitives([src[f, x] for f in range(FIELDS)])):
                prim[k, x] = value

        tall = rows if stage == 2 else stride

        def cells(x, d, tall=tall, src=src):
            return [src[f, x, 0:tall] for f in range(FIELDS)] + [
                prim[k, x, 0:tall] for k in (d, 3 + d, 6, 7)
            ]

        for x in range(low, high + 1):
            new = faces(0, cells(x - 1, 0), cells(x, 0))
            for f in range(FIELDS):
                xface[x % 2, f, 0:tall] = new[f]
            if x == low:
                continue
            p = x - 1
            change = [new[f] - xface[p % 2, f, 0:tall] for f in range(FIELDS)]
            hi = cells(p, 1, stride)
            face = faces(1, [pltpu.roll(v, 1, axis=0) for v in hi], hi)
            change = [
                c + (pltpu.roll(v, stride - 1, axis=0) - v)[0:tall] for c, v in zip(change, face)
            ]
            hi = cells(p, 2)
            face = faces(2, [pltpu.roll(v, 1, axis=1) for v in hi], hi)
            change = [
                c + (pltpu.roll(v, lanes - 1, axis=1) - v) for c, v in zip(change, face)
            ]
            for f in range(FIELDS):
                sink = block_ref[FIELDS, p, 0:tall] if f == FIELDS - 1 else None
                value = advance(
                    stage, src[f, p, 0:tall], change[f], block_ref[f, p, 0:tall], sink
                )
                if stage == 2:
                    out_ref[f, p - HALO] = value
                else:
                    now[f, p] = value


def ends_kernel(
    stride, main_ref, own_ref, inner_ref, outer_ref, out_ref, slab_base, base, slab, comb
):
    _, planes, rows, lanes = out_ref.shape
    deep = planes + 2 * HALO
    wide = slab_base.shape[2]
    half = slab_base.shape[1] // 2
    part = FIELDS * TILE
    source = iota((lanes, FIELDS * lanes), 0)
    target = iota((lanes, FIELDS * lanes), 1)
    field = lax.rem(source, part) // TILE
    end = lax.rem(source, TILE)
    spread = (
        ((end < HALO) & (target == field * lanes + end))
        | (
            (end >= HALO) & (end < 2 * HALO)
            & (target == field * lanes + lanes - 2 * HALO + end)
        )
    ) & (source < 3 * part)
    spread = spread.astype(jnp.float32).astype(jnp.bfloat16)
    comb[...] = jnp.zeros(comb.shape, jnp.float32)
    slab_base[...] = jnp.zeros(slab_base.shape, jnp.float32)
    upper = parity("grp") == 1
    for f in range(FIELDS + 1):
        at = slice(f * (HALO - 1), (f + 1) * (HALO - 1))
        inner, outer = inner_ref[at], outer_ref[at]
        slab_base[f, 1:HALO] = jnp.where(upper, inner, outer)
        slab_base[f, half + NEAR:half + NEAR + HALO - 1] = jnp.where(upper, outer, inner)
        at = f * 2 * TILE
        slab_base[f, HALO:HALO + NEAR] = own_ref[at:at + NEAR]
        slab_base[f, half:half + NEAR] = own_ref[at + TILE:at + TILE + NEAR]
        if f == FIELDS:
            continue
        row, first, there = far_row(f, planes, stride)
        inner, outer = inner_ref[row:row + 1], outer_ref[row:row + 1]
        if there != first:
            inner, outer = (pltpu.roll(v, wide + first - there, axis=1) for v in (inner, outer))
        slab_base[f, 0:1] = jnp.where(upper, inner, outer)
        last = half + NEAR + HALO - 1
        slab_base[f, last:last + 1] = jnp.where(upper, outer, inner)

    narrow = min(wide, -(-(deep - 1) * stride // lanes) * lanes)
    kept = NEAR + HALO - 2
    start = slab_base
    for stage in range(3):
        src = slab_base if stage == 0 else slab
        u = [src[f] for f in range(FIELDS)]
        tall, width = u[0].shape
        first_row = lax.rem(iota((tall, width), 1), stride) == 0
        last_row = lax.rem(iota((tall, width), 1), stride) == stride - 1

        def lane_roll(v, shift, width=width):
            return pltpu.roll(v, shift % width, axis=1)

        q = primitives(u)
        hi = u + [q[2], q[5], q[6], q[7]]
        face = faces(2, [pltpu.roll(v, 1, axis=0) for v in hi], hi)
        change = [pltpu.roll(v, tall - 1, axis=0) - v for v in face]
        hi = u + [q[0], q[3], q[6], q[7]]
        face = faces(0, [lane_roll(v, stride) for v in hi], hi)
        change = [c + (lane_roll(v, -stride) - v) for c, v in zip(change, face)]
        hi = u + [q[1], q[4], q[6], q[7]]
        lo = [jnp.where(first_row, lane_roll(v, 1 - stride), lane_roll(v, 1)) for v in hi]
        face = faces(1, lo, hi)
        change = [
            c + (jnp.where(last_row, lane_roll(v, stride - 1), lane_roll(v, -1)) - v)
            for c, v in zip(change, face)
        ]
        for f in range(FIELDS):
            sink = start[FIELDS] if f == FIELDS - 1 else None
            value = advance(stage, u[f], change[f], start[f], sink)
            if stage:
                slab[f] = value
                continue
            for group in range(2):
                slab[f, group * TILE:group * TILE + kept] = value[
                    group * half + 1:group * half + 1 + kept, 0:narrow
                ]
                slab[f, group * TILE + kept:(group + 1) * TILE] = jnp.zeros(
                    (TILE - kept, narrow), jnp.float32
                )
        if stage == 0:
            for f in range(FIELDS + 1):
                for group in range(2):
                    base[f, group * TILE:group * TILE + kept] = slab_base[
                        f, group * half + 1:group * half + 1 + kept, 0:narrow
                    ]
                    base[f, group * TILE + kept:(group + 1) * TILE] = jnp.zeros(
                        (TILE - kept, narrow), jnp.float32
                    )
            start = base

    for f in range(FIELDS):
        first = HALO - 1
        comb[f * TILE:f * TILE + HALO, 0:narrow] = slab[f, first:first + HALO]
        first = TILE + NEAR - HALO - 1
        comb[f * TILE + HALO:f * TILE + 2 * HALO, 0:narrow] = slab[f, first:first + HALO]
    whole = comb[0:part]
    for k in range(2):
        piece = whole.astype(jnp.bfloat16).astype(jnp.float32)
        comb[k * part:(k + 1) * part] = piece
        whole = whole - piece
    comb[2 * part:3 * part] = whole
    turned = jnp.transpose(comb[...]).astype(jnp.bfloat16)
    moved = lax.dot_general(
        turned[HALO * stride:(HALO + planes) * stride], spread, (((1,), (0,)), ((), ())),
        preferred_element_type=jnp.float32,
    )
    lane = iota((rows, lanes), 1)
    near = (lane < HALO) | (lane >= lanes - HALO)
    for f in range(FIELDS):
        for x in range(planes):
            edge = moved[x * stride:x * stride + rows, f * lanes:(f + 1) * lanes]
            out_ref[f, x] = jnp.where(near, edge, main_ref[f, x])


def metal_kernel(dims, rows, where, order, *refs):
    fluid_ref, fluid_hbm, written = refs[-20], refs[-18], refs[-1]
    refs = (*refs[:-20], refs[-19], *refs[-17:-1])
    leave = pltpu.make_async_copy(fluid_ref, fluid_hbm, written)
    leave.start()
    count_blk, count_sub, along, across = dims
    devices = count_blk * count_sub
    pieces = [(refs[k], start) for k, start in where]
    (
        out_ref, sol, kelvin, res, dirn, drift, image, diag, cx, cy, cz, cyu, czu, caps, heat,
        route, faced,
    ) = refs[-17:]
    lanes = out_ref.shape[-1]
    cells = along * across
    wide = count_sub * across
    deep = count_blk * along
    blk, sub = lax.axis_index("blk"), lax.axis_index("sub")
    mine = blk * along
    side = pl.multiple_of(sub * across, TILE)

    zero = jnp.zeros((wide, lanes), jnp.float32)
    for ref in (kelvin, res, cx):
        ref[0] = zero
        ref[deep + 1] = zero

    for n, ((ref, first), (flip_blk, flip_sub)) in enumerate(zip(pieces, order)):
        b = jnp.bitwise_xor(blk, flip_blk) * along
        y = pl.multiple_of(jnp.bitwise_xor(sub, flip_sub) * across, TILE)
        for field, (dest, shift) in enumerate(((kelvin, 1), (caps, 0), (cx, 1), (cy, 0), (cz, 0))):
            start = first + field * cells
            dest[pl.ds(b + shift, along), pl.ds(y, across)] = ref[
                start:start + cells
            ].reshape(along, across, lanes)
        start = first + 5 * cells
        faced[n * rows:(n + 1) * rows] = ref[start:start + rows]
        route[:, n * rows:(n + 1) * rows] = ref[start + rows:start + rows + TILE][:, 0:rows]

    walls = jnp.concatenate([kelvin[1 + b * along] for b in range(count_blk)], axis=0)
    strips = devices * across
    chosen = iota((strips, devices * rows), 0) == route[0:1].astype(jnp.int32)
    flux = film_coeff * (faced[...] - select_sum(chosen, walls, 0))
    heat[...] = select_sum(chosen, flux, 1)

    chunk = math.gcd(deep, max(1, ROWS // wide))
    none = jnp.zeros((TILE, lanes), jnp.float32)

    def sweep(body, init):
        return lax.fori_loop(0, deep // chunk, lambda i, c: body(i * chunk, c), init)

    def fold(value):
        return jnp.sum(value.reshape(-1, TILE, lanes), axis=0)

    def total(value):
        one = jnp.sum(jnp.sum(value, axis=0, keepdims=True), axis=1, keepdims=True)
        return jnp.broadcast_to(one, (TILE, lanes))

    def times(factor, value):
        return (factor * value.reshape(-1, TILE, lanes)).reshape(value.shape)

    def turned(v, step, axis):
        return pltpu.roll(v, step % v.shape[axis], axis=axis)

    def prepare(x, carry):
        here, own = pl.ds(x, chunk), pl.ds(x + 1, chunk)
        ups = cx[pl.ds(x + 2, chunk)], turned(cy[here], -1, 1), turned(cz[here], -1, 2)
        cyu[here] = ups[1]
        czu[here] = ups[2]
        diag[here] = caps[here] + ((cx[own] + ups[0]) + (cy[here] + ups[1]) + (cz[here] + ups[2]))
        v = kelvin[own]
        res[own] = (
            cx[own] * (kelvin[pl.ds(x, chunk)] - v)
            + ups[0] * (kelvin[pl.ds(x + 2, chunk)] - v)
            + (cy[here] * (turned(v, 1, 1) - v) + ups[1] * (turned(v, -1, 1) - v))
            + (cz[here] * (turned(v, 1, 2) - v) + ups[2] * (turned(v, -1, 2) - v))
        )
        return carry

    sweep(prepare, 0)
    for b in range(count_blk):
        at = b * along + 1
        res[at] = res[at] + heat[b * wide:(b + 1) * wide]

    def apply(x, sums):
        here, own = pl.ds(x, chunk), pl.ds(x + 1, chunk)
        v = res[own]
        value = (
            diag[here] * v
            - (cx[own] * res[pl.ds(x, chunk)] + cx[pl.ds(x + 2, chunk)] * res[pl.ds(x + 2, chunk)])
            - (cy[here] * turned(v, 1, 1) + cyu[here] * turned(v, -1, 1))
            - (cz[here] * turned(v, 1, 2) + czu[here] * turned(v, -1, 2))
        )
        image[here] = value
        return sums[0] + fold(v * v), sums[1] + fold(v * value)

    mine_at = pl.ds(mine, along), pl.ds(side, across)
    sol[...] = kelvin[pl.ds(mine + 1, along), pl.ds(side, across)]
    norm = alpha = beta = None
    for step in range(ITERS):
        fresh, product = (total(v) for v in sweep(apply, (none, none)))
        if step == 0:
            alpha = fresh / product
        else:
            beta = fresh / norm
            alpha = fresh / (product - beta * fresh / alpha)
        norm = fresh
        if step + 1 == ITERS:
            towards = res[pl.ds(mine + 1, along), pl.ds(side, across)] + times(beta, dirn[mine_at])
            out_ref[...] = sol[...] + times(alpha, towards)
            leave.wait()
            break

        def update(x, carry, step=step, alpha=alpha, beta=beta):
            here, own = pl.ds(x, chunk), pl.ds(x + 1, chunk)
            towards, moved = res[own], image[here]
            if step:
                towards = towards + times(beta, dirn[here])
                moved = moved + times(beta, drift[here])
            dirn[here] = towards
            drift[here] = moved
            res[own] = res[own] - times(alpha, moved)
            return carry

        sweep(update, 0)
        sol[...] = sol[...] + times(alpha, dirn[mine_at])


def swap(value, axis, flip):
    count = lax.axis_size(axis)
    return lax.ppermute(value, axis, [(i, i ^ flip) for i in range(count)])


def outer(value, axis="blk"):
    count = lax.axis_size(axis)
    pairs = [(i, (i + 1 if i % 2 else i - 1) % count) for i in range(count)]
    return lax.ppermute(value, axis, pairs)


def ring(value, axis, step):
    count = lax.axis_size(axis)
    return lax.ppermute(value, axis, [(i, (i + step) % count) for i in range(count)])


def flips(count):
    return [1 << k for k in reversed(range((count - 1).bit_length()))]


def shards(
    mass_per_volume,
    flow_speed_vector,
    normal_stress,
    facing_strip_index,
    solid_kelvin,
    face_coupling,
    substance_index,
    substance_storage,
):
    planes, rows, lanes = mass_per_volume.shape
    along, across, _ = solid_kelvin.shape
    count_blk, count_sub = lax.axis_size("blk"), lax.axis_size("sub")
    devices = count_blk * count_sub
    cells = along * across
    edge = FIELDS * planes * HALO
    each = across + 1
    record = 5 * cells + rows + TILE

    face = FIELDS * HALO * rows
    state, yedge, apay, bpay, metal, wall = call(
        pack_kernel,
        [
            f32(FIELDS, planes, rows, lanes), f32(2 * edge, lanes),
            f32(face + record, lanes), f32(face, lanes),
            f32(record, lanes), f32(each, lanes),
        ],
        [
            mass_per_volume, flow_speed_vector, normal_stress,
            facing_strip_index.reshape(1, rows), solid_kelvin.reshape(cells, lanes),
            face_coupling.reshape(6 * cells, lanes), substance_index.reshape(cells, lanes),
            substance_storage,
        ],
        hbm=tuple(range(8)),
        scratch=[
            (planes, rows, lanes), (3, planes, rows, lanes), (planes, rows, lanes),
            pltpu.VMEM((1, rows), jnp.int32), pltpu.VMEM((cells, lanes), jnp.int32),
            pltpu.SMEM(substance_storage.shape, jnp.float32), pltpu.SemaphoreType.DMA((8,)),
        ],
    )
    paired = count_blk == 4 and count_sub == 2
    span = FIELDS * corner_rows()[1]
    bpay = outer(bpay)
    if paired:
        wall_a = swap(wall, "blk", 1)
        ypay = jnp.concatenate([yedge, wall, wall_a], axis=0)
        yrecv = swap(ypay, "sub", 1)
        ylo, yhi, lo_at, hi_at = yrecv, yrecv, edge, 0
        parts = [wall, wall_a, yrecv]
        starts = [(0, each), (0, each), (2 * edge, 2 * each)]
    else:
        ylo, yhi, lo_at, hi_at = ring(yedge[edge:], "sub", 1), ring(yedge[:edge], "sub", -1), 0, 0
        parts, starts = [], []
    apay = swap(apay, "blk", 1)
    aedge, bedge = call(
        functools.partial(edge_kernel, planes, lo_at, hi_at, starts),
        [f32(2 * span, lanes), f32(2 * span + sum(c for _, c in starts), lanes)],
        [ylo, yhi, *parts],
    )
    bedge = outer(bedge)
    aedge = swap(aedge, "blk", 1)
    if paired:
        walls = [wall, wall_a, yrecv, yrecv] + 4 * [bedge]
        wall_at = [(0, 0, 0), (0, 1, 0), (2 * edge, 0, 1), (2 * edge + each, 1, 1)]
        wall_at += [(2 * span + k * each, 3 ^ (k & 1), k >> 1) for k in range(4)]
    else:
        wall = jnp.pad(wall, ((0, across + TILE - each), (0, 0)))
        walls = [lax.all_gather(wall, ("blk", "sub"), axis=0, tiled=True)]
        wall_at = None
    deep, stride = planes + 2 * HALO, rows + TILE
    ends_rows = up_to_tile((FIELDS + 1) * (HALO - 1) + FIELDS - 1)
    wide_lanes = -(-deep * stride // lanes) * lanes
    block, own_z, inner_z, outer_z = call(
        functools.partial(
            assemble_kernel, ((count_blk, count_sub), across), lo_at, hi_at, wall_at
        ),
        [
            f32(FIELDS + 1, deep, stride, lanes),
            f32((FIELDS + 1) * 2 * TILE, wide_lanes),
            f32(ends_rows, wide_lanes),
            f32(ends_rows, wide_lanes),
        ],
        [state, apay, bpay, ylo, yhi, aedge, bedge, *walls],
        scratch=[(devices * (across + TILE), lanes), (stride, lanes)],
    )
    inner_got = swap(inner_z, "grp", 1)
    outer_got = outer(outer_z, "grp")
    planes_next = call(
        planes_kernel,
        f32(FIELDS, planes, rows, lanes),
        [block],
        scratch=[
            (FIELDS, deep, stride, lanes), (8, deep, stride, lanes), (2, FIELDS, stride, lanes)
        ],
    )

    if paired:
        near_y = swap(metal, "sub", 1)
        far = swap(metal, "blk", 2)
        far_y = swap(near_y, "blk", 2)
        mates = swap(jnp.concatenate([near_y, far, far_y], axis=0), "blk", 1)
        pieces = [metal, apay, near_y, far, far_y, mates]
        where = [(0, 0), (1, face), (2, 0), (3, 0), (4, 0)] + [(5, k * record) for k in range(3)]
        order = [(0, 0), (1, 0), (0, 1), (2, 0), (2, 1), (1, 1), (3, 0), (3, 1)]
    else:
        held, order = metal, [(0, 0)]
        steps = [("blk", flip) for flip in flips(count_blk)]
        steps += [("sub", flip) for flip in flips(count_sub)]
        for axis, flip in steps:
            held = jnp.concatenate([held, swap(held, axis, flip)], axis=0)
            order = order + [
                (b ^ flip, s) if axis == "blk" else (b, s ^ flip) for b, s in order
            ]
        pieces, where = [held], [(0, k * record) for k in range(devices)]
    wide = count_sub * across
    deep_metal = count_blk * along
    field = (deep_metal, wide, lanes)
    padded = (deep_metal + 2, wide, lanes)
    slab = 2 * -(-(NEAR + HALO) // (TILE // 2)) * (TILE // 2)
    narrow = min(wide_lanes, -(-(deep - 1) * stride // lanes) * lanes)
    fluid = call(
        functools.partial(ends_kernel, stride),
        f32(FIELDS, planes, rows, lanes),
        [planes_next, own_z, inner_got, outer_got],
        scratch=[
            (FIELDS + 1, slab, wide_lanes), (FIELDS + 1, 2 * TILE, narrow),
            (FIELDS, 2 * TILE, narrow), (lanes, wide_lanes),
        ],
    )
    metal_next, fluid_next = call(
        functools.partial(
            metal_kernel, (count_blk, count_sub, along, across), rows, where, order
        ),
        [f32(along, across, lanes), f32(FIELDS, planes, rows, lanes)],
        [*pieces, fluid],
        hbm_out=(1,),
        scratch=[
            (along, across, lanes), padded, padded, field, field, field, field, padded, field,
            field, field, field, field, (devices * across, lanes), (TILE, devices * rows), (devices * rows, lanes),
            pltpu.SemaphoreType.DMA,
        ],
    )
    return (fluid_next, metal_next)


def solution(mesh):
    in_specs = (
        P("blk", "sub", "grp"),
        P(None, "blk", "sub", "grp"),
        P("blk", "sub", "grp"),
        P("grp", "blk", "sub"),
        P("blk", "sub", "grp"),
        P(None, "blk", "sub", "grp"),
        P("blk", "sub", "grp"),
        P(),
    )
    out_specs = (P(None, "blk", "sub", "grp"), P("blk", "sub", "grp"))
    return jax.shard_map(shards, mesh=mesh, in_specs=in_specs, out_specs=out_specs, check_vma=False)
```
